32 devices in a mesh: dp: 8 (over z, x), tensor: 4 (over y, core).
Axes of the slice: x: 2, y: 2, z: 4, core: 2. Of those that a mesh axis runs over, the one named last changes fastest.
Arguments:
- stream_in: bfloat16 [8, 1024, 2048], P('dp', 'tensor'), may hold values from -6 to 6
- segments: int32 [8, 1024], P('dp'), may hold values from 0 to 2, never falling along the last dimension, each value on 1 to 800 neighbouring positions
- first_gain: float32 [2048], replicated, may hold values from 0.5 to 1.5
- gelu_gate_weight: bfloat16 [2048, 2560], P(None, 'tensor'), may hold values from -0.125 to 0.125
- recurrent_branch_weight: bfloat16 [2048, 2560], P(None, 'tensor'), may hold values from -0.125 to 0.125
- conv_kernel: float32 [4, 2560], P(None, 'tensor'), may hold values from -3 to 3
- conv_bias: float32 [2560], P('tensor'), may hold values from -3 to 3
- recur_weight: bfloat16 [16, 160, 160], P('tensor'), may hold values from -0.5 to 0.5
- recur_bias: float32 [2560], P('tensor'), may hold values from -4 to 4
- inlet_weight: bfloat16 [16, 160, 160], P('tensor'), may hold values from -0.5 to 0.5
- inlet_bias: float32 [2560], P('tensor'), may hold values from -3 to 3
- decay_param: float32 [2560], P('tensor'), may hold values from 5 to 9
- recurrent_output_weight: bfloat16 [2560, 2048], P('tensor'), may hold values from -0.25 to 0.25
- second_gain: float32 [2048], replicated, may hold values from 0.5 to 1.5
- gate_projection_weight: bfloat16 [2048, 6144], P(None, 'tensor'), may hold values from -0.125 to 0.125
- up_projection_weight: bfloat16 [2048, 6144], P(None, 'tensor'), may hold values from -0.125 to 0.125
- down_projection_weight: bfloat16 [6144, 2048], P('tensor'), may hold values from -0.15625 to 0.15625
- cotangent: bfloat16 [8, 1024, 2048], P('dp', 'tensor'), may hold values from -6 to 6
Outputs:
- stream_out: float32 [8, 1024, 2048], P('dp', 'tensor')
- stream_grad: float32 [8, 1024, 2048], P('dp', 'tensor')
- first_gain_grad: float32 [2048], replicated
- gated_weight_grad: float32 [2048, 2560], P('dp', 'tensor')
- branch_weight_grad: float32 [2048, 2560], P('dp', 'tensor')
- conv_kernel_grad: float32 [4, 2560], P(None, 'tensor')
- conv_bias_grad: float32 [2560], P('tensor')
- recur_weight_grad: float32 [16, 160, 160], P('tensor')
- recur_bias_grad: float32 [2560], P('tensor')
- inlet_weight_grad: float32 [16, 160, 160], P('tensor')
- inlet_bias_grad: float32 [2560], P('tensor')
- decay_param_grad: float32 [2560], P('tensor')
- output_weight_grad: float32 [2560, 2048], P('tensor', 'dp')
- second_gain_grad: float32 [2048], replicated
- hidden_gate_grad: float32 [2048, 6144], P('dp', 'tensor')
- hidden_up_grad: float32 [2048, 6144], P('dp', 'tensor')
- hidden_down_grad: float32 [6144, 2048], P('tensor', 'dp')
The draws below stay inside these ranges and needn't reach their ends.
Inputs may be any that keep to these rules, and one draw needn't show every extreme that they name: `segments`: segment numbers never fall along a sequence; a document starts at position 0 and wherever the number changes, and no document is longer than 800 tokens.
All inputs are finite; a program needn't handle non-finite values.
Results may differ from the reference program's by a relative error of at most 0.0085.
Values may be sent and summed in bfloat16 or wider, within the bound.
A program may use at most 256 MiB of HBM per device.

```python
import math
import jax
import jax.numpy as jnp
import numpy as np
from jax import lax

D = 2048
R = 2560
FF = 6144
HEADS = 16
CONV = 4
LEN = 1024
BW = 160
SEQS = 8


def level_of(rng, shape, split, low, high):
    gain, own = 1.0, jax.random.fold_in(rng, 6)
    for position, blocks in split:
        steps = jnp.exp(jax.random.uniform(jax.random.fold_in(own, position), (blocks,), jnp.float32, low / len(split), high / len(split)))
        gain = gain * jnp.repeat(steps, shape[position] // blocks).reshape([-1 if axis == position else 1 for axis in range(len(shape))])
    return gain


def length_profile(number_of, total, bound, skew):
    portions = [(1 << 20) // math.isqrt(rank ** skew) + 1 for rank in range(2, number_of + 1)]
    rest, holding = total - bound - (number_of - 1), [1] * (number_of - 1)
    while rest > 0:
        free = [i for i in range(number_of - 1) if holding[i] < bound]
        pool, left = sum([portions[i] for i in free]), rest
        for i in free:
            extra = min(bound - holding[i], max(1, left * portions[i] // pool), rest)
            holding[i] = holding[i] + extra
            rest = rest - extra
    return np.array([bound] + holding)


def ragged_sizes(rng, amount, total, most, lean):
    if amount == 2:
        one = jax.random.randint(rng, (), max(1, total - most), min(most, total - 1) + 1)
        return jnp.stack([one, total - one])
    lengths = jnp.asarray(length_profile(amount, total, most, lean), jnp.int32)
    pairs = (amount - 1) // 2
    donor, taker = lengths[1:1 + 2 * pairs:2], lengths[2:2 + 2 * pairs:2]
    slack = jnp.minimum(donor - 1, most - taker)
    passed = jax.random.randint(jax.random.fold_in(rng, 1), (pairs,), 0, 1 << 20) % (slack + 1)
    lengths = lengths.at[1:1 + 2 * pairs:2].set(donor - passed).at[2:2 + 2 * pairs:2].set(taker + passed)
    return lengths[jax.random.permutation(jax.random.fold_in(rng, 2), amount)]


def noise(stream_key, extent, width, most, pieces=(), held_as=jnp.bfloat16):
    array = width * jax.random.normal(stream_key, extent, jnp.float32)
    if pieces:
        array = array * level_of(stream_key, extent, pieces, -0.22, 0.18)
    return jnp.clip(array, -most, most).astype(held_as)


def setup_inputs(seed: int = 0) -> dict:
    streams_of = jax.random.split(jax.random.key(seed), 19)
    return {
        "stream_in": noise(streams_of[0], (SEQS, LEN, D), 1.0, 6.0, ((0, 8), (1, 4))),
        "segments": jax.vmap(lambda own: jnp.searchsorted(jnp.cumsum(ragged_sizes(own, 3, LEN, LEN * 25 // 32, 0)), jnp.arange(LEN), side="right"))(jax.random.split(streams_of[1], SEQS)).reshape((SEQS, LEN)).astype(jnp.int32),
        "first_gain": jnp.clip(1.0 + 0.1 * jax.random.normal(streams_of[2], (D,), jnp.float32), 0.5, 1.5),
        "gelu_gate_weight": noise(streams_of[3], (D, R), D ** -0.5, 0.125, ((1, 4),)),
        "recurrent_branch_weight": noise(streams_of[4], (D, R), D ** -0.5, 0.125, ((1, 4),)),
        "conv_kernel": noise(streams_of[5], (CONV, R), CONV ** -0.5, 3.0, ((1, 4),), jnp.float32),
        "conv_bias": noise(streams_of[6], (R,), 0.5, 3.0, ((0, 4),), jnp.float32),
        "recur_weight": noise(streams_of[7], (HEADS, BW, BW), BW ** -0.5, 0.5, ((0, 4),)),
        "recur_bias": noise(streams_of[8], (R,), 1.0, 4.0, ((0, 4),), jnp.float32),
        "inlet_weight": noise(streams_of[9], (HEADS, BW, BW), BW ** -0.5, 0.5, ((0, 4),)),
        "inlet_bias": noise(streams_of[10], (R,), 0.5, 3.0, ((0, 4),), jnp.float32),
        "decay_param": jnp.clip(5.0 + 4.0 * jax.random.uniform(streams_of[11], (R,), jnp.float32) ** level_of(streams_of[11], (R,), ((0, 4),), -0.2, 0.2), 5.0, 9.0),
        "recurrent_output_weight": noise(streams_of[12], (R, D), (R // 4) ** -0.5, 0.25, ((0, 4),)),
        "second_gain": jnp.clip(1.0 + 0.1 * jax.random.normal(streams_of[13], (D,), jnp.float32), 0.5, 1.5),
        "gate_projection_weight": noise(streams_of[14], (D, FF), D ** -0.5, 0.125, ((1, 4),)),
        "up_projection_weight": noise(streams_of[15], (D, FF), D ** -0.5, 0.125, ((1, 4),)),
        "down_projection_weight": noise(streams_of[16], (FF, D), (FF // 4) ** -0.5, 0.15625, ((0, 4),)),
        "cotangent": noise(streams_of[17], (SEQS, LEN, D), 1.0, 6.0, ((0, 8), (1, 4))),
    }


epsilon = 1e-06
decay_scale = 8.0

@jax.custom_vjp
def low(v):
    return lax.optimization_barrier(v.astype(jnp.bfloat16)).astype(jnp.float32)

@jax.custom_vjp
def low_back(v):
    return v

def low_keep(v):
    return (low(v), None)

def low_pass(kept, grad):
    return (grad,)

def back_keep(v):
    return (v, None)

def back_low(kept, grad):
    return (low(grad),)
low.defvjp(low_keep, low_pass)
low_back.defvjp(back_keep, back_low)

def matmul(left_operand, right_operand):
    return jnp.einsum('atc,cv->atv', left_operand, right_operand, precision=lax.Precision.HIGHEST)

def rms_apply(values, gain_vec):
    inverse_rms = lax.rsqrt(lax.optimization_barrier(jnp.mean(values * values, axis=-1, keepdims=True)) + epsilon)
    return values * inverse_rms * gain_vec

def gelu_tanh(values):
    return jax.nn.gelu(values, approximate=True)

def segment_masks(segments, taps):
    seq_len = segments.shape[1]
    padded = jnp.pad(segments, ((0, 0), (taps - 1, 0)), constant_values=-1)
    same_list = []
    for offset in range(1, taps):
        earlier = padded[:, taps - 1 - offset:taps - 1 - offset + seq_len]
        same_list.append((earlier == segments).astype(jnp.float32)[..., None])
    starts = 1.0 - same_list[0]
    return (starts, same_list)

def causal_conv(inputs, kernel, bias_vec, same_list):
    summed = bias_vec + kernel[0] * inputs
    for offset in range(1, kernel.shape[0]):
        shifted = jnp.pad(inputs, ((0, 0), (offset, 0), (0, 0)))[:, :-offset]
        summed = summed + kernel[offset] * shifted * same_list[offset - 1]
    return summed

def combine_pairs(earlier, latter):
    return (earlier[0] * latter[0], latter[0] * earlier[1] + latter[1])

def recurrence(recur_pre, inlet_pre, inputs, decay_param, starts):
    forget_rate = jax.nn.sigmoid(recur_pre)
    log_a = -decay_scale * forget_rate * jax.nn.softplus(-decay_param)
    decay_step = jnp.exp(log_a)
    norm_factor = jnp.sqrt(-jnp.expm1(2.0 * log_a))
    multiplier = starts + (1.0 - starts) * norm_factor
    carried = decay_step * (1.0 - starts)
    driven = multiplier * jax.nn.sigmoid(inlet_pre) * inputs
    _, states = lax.associative_scan(combine_pairs, (carried, driven), axis=1)
    return states

def forward(values, params, starts, same_list):
    first_gain, gelu_gate_weight, recurrent_branch_weight, conv_kernel, conv_bias, recur_weight, recur_bias, inlet_weight, inlet_bias, decay_param, recurrent_output_weight, second_gain, gate_projection_weight, up_projection_weight, down_projection_weight = params
    seq_count, seq_len = (values.shape[0], values.shape[1])
    normalized_input = low(rms_apply(values, first_gain))
    gated_preactivation = low_back(matmul(normalized_input, gelu_gate_weight))
    branch_pre = low_back(matmul(normalized_input, recurrent_branch_weight))
    conv_out = low(causal_conv(branch_pre, conv_kernel, conv_bias, same_list))
    head_split = conv_out.reshape(seq_count, seq_len, HEADS, R // HEADS)
    recur_pre = low_back(jnp.einsum('slhi,hij->slhj', head_split, recur_weight, precision=lax.Precision.HIGHEST).reshape(seq_count, seq_len, R) + recur_bias)
    inlet_pre = low_back(jnp.einsum('slhi,hij->slhj', head_split, inlet_weight, precision=lax.Precision.HIGHEST).reshape(seq_count, seq_len, R) + inlet_bias)
    states = recurrence(recur_pre, inlet_pre, conv_out, decay_param, starts)
    gated_product = low(states * gelu_tanh(gated_preactivation))
    attended = low_back(matmul(gated_product, recurrent_output_weight))
    middle = values + attended
    normalized_second = low(rms_apply(middle, second_gain))
    gate_pre = low_back(matmul(normalized_second, gate_projection_weight))
    up_preactivation = low_back(matmul(normalized_second, up_projection_weight))
    hidden_activation = low(gelu_tanh(gate_pre) * up_preactivation)
    return middle + matmul(hidden_activation, down_projection_weight)

def reference(stream_in, segments, first_gain, gelu_gate_weight, recurrent_branch_weight, conv_kernel, conv_bias, recur_weight, recur_bias, inlet_weight, inlet_bias, decay_param, recurrent_output_weight, second_gain, gate_projection_weight, up_projection_weight, down_projection_weight, cotangent):
    params = tuple((param.astype(jnp.float32) for param in (first_gain, gelu_gate_weight, recurrent_branch_weight, conv_kernel, conv_bias, recur_weight, recur_bias, inlet_weight, inlet_bias, decay_param, recurrent_output_weight, second_gain, gate_projection_weight, up_projection_weight, down_projection_weight)))
    group_size = math.gcd(SEQS, 4)
    group_count = SEQS // group_size
    value_blocks = stream_in.astype(jnp.float32).reshape(group_count, group_size, LEN, D)
    seg_blocks = segments.reshape(group_count, group_size, LEN)
    cot_blocks = cotangent.astype(jnp.float32).reshape(group_count, group_size, LEN, D)

    def group_step(grad_sums, batch_item):
        block_values, block_segments, block_cot = batch_item
        starts, same_list = segment_masks(block_segments, CONV)
        result, pullback = jax.vjp(lambda v, p: forward(v, p, starts, same_list), block_values, params)
        value_grad, param_grads = pullback(block_cot)
        return (jax.tree.map(jnp.add, grad_sums, param_grads), (result, value_grad))
    initial = jax.tree.map(jnp.zeros_like, params)
    grad_sums, (results, value_grads) = lax.scan(group_step, initial, (value_blocks, seg_blocks, cot_blocks))
    return (results.reshape(SEQS, LEN, D), value_grads.reshape(SEQS, LEN, D), grad_sums[0], grad_sums[1], grad_sums[2], grad_sums[3], grad_sums[4], grad_sums[5], grad_sums[6], grad_sums[7], grad_sums[8], grad_sums[9], grad_sums[10], grad_sums[11], grad_sums[12], grad_sums[13], grad_sums[14])
```

```python
import functools

import jax
import jax.numpy as jnp
from jax import lax
from jax.experimental import pallas as pl
from jax.experimental.pallas import tpu as pltpu
from jax.sharding import PartitionSpec as P

epsilon = 1e-06
decay_scale = 8.0
LANES = 128
GELU_C = 0.7978845608028654
GELU_K = 0.044715
F32 = jnp.float32
BF16 = jnp.bfloat16
VMEM_BYTES = 60 * 1024 * 1024


def minus_expm1(y, exp_y):
    s = 1.0 + y * (1.0 / 9.0)
    for d in range(8, 1, -1):
        s = 1.0 + (y * (1.0 / d)) * s
    return jnp.where(y > -0.5, -y * s, 1.0 - exp_y)


def gelu_parts(v):
    v2 = v * v
    t = jnp.tanh(GELU_C * v * (1.0 + GELU_K * v2))
    half = 0.5 * (1.0 + t)
    slope = half + 0.5 * v * (1.0 - t * t) * (GELU_C * (1.0 + 3.0 * GELU_K * v2))
    return v * half, slope


def lane_tiles(width):
    return [slice(j * LANES, (j + 1) * LANES) for j in range(width // LANES)]


def fold_rows(v):
    return jnp.sum(v.reshape(v.shape[0] // 8, 8, v.shape[1]), axis=0)


def gates_pre(rows, step, conv_ref, w_ref, pre_s):
    @pl.loop(0, rows // step)
    def _(i):
        r = pl.ds(pl.multiple_of(i * step, step), step)
        pre_s[r, :] = jnp.dot(conv_ref[r, :], w_ref[...], preferred_element_type=F32)


def mixer_forward_kernel(branch_ref, gated_ref, mask_ref, vec_ref, w_ref, conv_ref, states_ref, product_ref, pre_s, a_s, b_s):
    rows, width = branch_ref.shape
    seg = rows // 8
    tiles = lane_tiles(width)

    @pl.loop(0, 8)
    def _(s):
        t0 = pl.multiple_of(s * seg, seg)
        before = pl.multiple_of(jnp.maximum(t0 - 8, 0), 8)
        same = [mask_ref[pl.ds(t0, seg), k : k + 1] for k in range(3)]
        for cols in tiles:
            b = branch_ref[pl.ds(t0, seg), cols]
            ext = jnp.concatenate([branch_ref[pl.ds(before, 8), cols], b], axis=0)
            out = vec_ref[4:5, cols] + vec_ref[0:1, cols] * b
            for k in range(1, 4):
                out = out + vec_ref[k : k + 1, cols] * pltpu.roll(ext, k, 0)[8:] * same[k - 1]
            conv_ref[pl.ds(t0, seg), cols] = out.astype(BF16)

    gates_pre(rows, 256, conv_ref, w_ref, pre_s)

    @pl.loop(0, 8)
    def _(s):
        t0 = pl.multiple_of(s * seg, seg)
        c = mask_ref[pl.ds(t0, seg), 0:1]
        for j, cols in enumerate(tiles):
            cols_i = slice(width + j * LANES, width + (j + 1) * LANES)
            r = jax.nn.sigmoid(pre_s[pl.ds(t0, seg), cols] + vec_ref[5:6, cols])
            i = jax.nn.sigmoid(pre_s[pl.ds(t0, seg), cols_i] + vec_ref[6:7, cols])
            log_a = (-decay_scale * vec_ref[7:8, cols]) * r
            a = jnp.exp(log_a)
            n = jnp.sqrt(minus_expm1(2.0 * log_a, a * a))
            mult = (1.0 - c) + c * n
            a_s[j, pl.ds(t0, seg), :] = a * c
            b_s[j, pl.ds(t0, seg), :] = mult * i * conv_ref[pl.ds(t0, seg), cols].astype(F32)

    def scan_step(i, carry):
        out = []
        for j in range(len(tiles)):
            h, p = carry[j]
            at = pl.ds(i, 8, stride=seg)
            a = a_s[j, at, :]
            h = a * h + b_s[j, at, :]
            p = a * p
            b_s[j, at, :] = h
            a_s[j, at, :] = p
            out.append((h, p))
        return tuple(out)

    one = jnp.ones((8, LANES), F32)
    lax.fori_loop(0, seg, scan_step, tuple((jnp.zeros((8, LANES), F32), one) for _ in tiles), unroll=4)

    def finish(s, carry):
        t0 = pl.multiple_of(s * seg, seg)
        out = []
        for j, cols in enumerate(tiles):
            st = b_s[j, pl.ds(t0, seg), :] + a_s[j, pl.ds(t0, seg), :] * carry[j]
            states_ref[pl.ds(t0, seg), cols] = st
            act, _ = gelu_parts(gated_ref[pl.ds(t0, seg), cols])
            product_ref[pl.ds(t0, seg), cols] = (st * act).astype(BF16)
            out.append(st[seg - 1 : seg, :])
        return tuple(out)

    lax.fori_loop(0, 8, finish, tuple(jnp.zeros((1, LANES), F32) for _ in tiles))


def mixer_forward(branch_pre, gated_pre, masks, vecs, w_cat):
    rows, width = branch_pre.shape
    lanes = width // LANES
    return pl.pallas_call(
        mixer_forward_kernel,
        out_shape=[
            jax.ShapeDtypeStruct((rows, width), BF16),
            jax.ShapeDtypeStruct((rows, width), F32),
            jax.ShapeDtypeStruct((rows, width), BF16),
        ],
        scratch_shapes=[
            pltpu.VMEM((rows, 2 * width), F32),
            pltpu.VMEM((lanes, rows, LANES), F32),
            pltpu.VMEM((lanes, rows, LANES), F32),
        ],
        compiler_params=pltpu.CompilerParams(vmem_limit_bytes=VMEM_BYTES),
        cost_estimate=pl.CostEstimate(flops=4 * rows * width * width, bytes_accessed=rows * width * 16, transcendentals=6 * rows * width),
        name="mixer_forward",
    )(branch_pre, gated_pre, masks, vecs, w_cat)


def mixer_backward_kernel(
    dprod_ref, gated_ref, states_ref, branch_ref, conv_ref, mask_ref, vec_ref, w_ref,
    dgated_ref, dri_ref, dbranch_ref, sums_ref,
    pre_s, a_s, n_s, ac_s, e_s, p_s, dconv_s,
):
    rows, width = branch_ref.shape
    seg = rows // 8
    tiles = lane_tiles(width)
    sums_ref[...] = jnp.zeros_like(sums_ref)
    gates_pre(rows, 256, conv_ref, w_ref, pre_s)

    @pl.loop(0, 8)
    def _(s):
        t0 = pl.multiple_of(s * seg, seg)
        at = pl.ds(t0, seg)
        c = mask_ref[at, 0:1]
        for j, cols in enumerate(tiles):
            cols_i = slice(width + j * LANES, width + (j + 1) * LANES)
            r = jax.nn.sigmoid(pre_s[at, cols] + vec_ref[5:6, cols])
            pre_s[at, cols] = r
            pre_s[at, cols_i] = jax.nn.sigmoid(pre_s[at, cols_i] + vec_ref[6:7, cols])
            log_a = (-decay_scale * vec_ref[7:8, cols]) * r
            a = jnp.exp(log_a)
            a_s[at, cols] = a
            n_s[at, cols] = jnp.sqrt(minus_expm1(2.0 * log_a, a * a))
            ac_s[j, at, :] = a * c
            act, slope = gelu_parts(gated_ref[at, cols])
            d = dprod_ref[at, cols]
            e_s[j, at, :] = d * act
            dgated_ref[at, cols] = (d * states_ref[at, cols] * slope).astype(BF16)

    for j in range(len(tiles)):
        ac_s[j, rows : rows + 8, :] = jnp.zeros((8, LANES), F32)

    def scan_step(q, carry):
        i = seg - 1 - q
        out = []
        for j in range(len(tiles)):
            e, p = carry[j]
            at = pl.ds(i, 8, stride=seg)
            a = ac_s[j, pl.ds(i + 1, 8, stride=seg), :]
            e = a * e + e_s[j, at, :]
            p = a * p
            e_s[j, at, :] = e
            p_s[j, at, :] = p
            out.append((e, p))
        return tuple(out)

    one = jnp.ones((8, LANES), F32)
    lax.fori_loop(0, seg, scan_step, tuple((jnp.zeros((8, LANES), F32), one) for _ in tiles), unroll=4)

    def finish(q, carry):
        s = 7 - q
        t0 = pl.multiple_of(s * seg, seg)
        at = pl.ds(t0, seg)
        before = pl.multiple_of(jnp.maximum(t0 - 8, 0), 8)
        c = mask_ref[at, 0:1]
        out = []
        for j, cols in enumerate(tiles):
            cols_i = slice(width + j * LANES, width + (j + 1) * LANES)
            e = e_s[j, at, :] + p_s[j, at, :] * carry[j]
            out.append(e[0:1, :])
            ext = jnp.concatenate([states_ref[pl.ds(before, 8), cols], states_ref[at, cols]], axis=0)
            earlier = pltpu.roll(ext, 1, 0)[8:]
            r, i, a, n = pre_s[at, cols], pre_s[at, cols_i], a_s[at, cols], n_s[at, cols]
            cv = conv_ref[at, cols].astype(F32)
            ec = e * c
            d_log = a * (ec * earlier) - ec * i * cv * (a * a / n)
            rr = d_log * r
            dr = ((-decay_scale * vec_ref[7:8, cols]) * rr * (1.0 - r)).astype(BF16)
            em = e * ((1.0 - c) + c * n) * i
            di = (em * cv * (1.0 - i)).astype(BF16)
            dri_ref[at, cols] = dr
            dri_ref[at, cols_i] = di
            dconv_s[at, cols] = em
            sums_ref[5, :, cols] += fold_rows(dr.astype(F32))
            sums_ref[6, :, cols] += fold_rows(di.astype(F32))
            sums_ref[7, :, cols] += fold_rows(rr)
        return tuple(out)

    lax.fori_loop(0, 8, finish, tuple(jnp.zeros((1, LANES), F32) for _ in tiles))

    @pl.loop(0, rows // 256)
    def _(i):
        at = pl.ds(pl.multiple_of(i * 256, 256), 256)
        dconv_s[at, :] += lax.dot_general(dri_ref[at, :], w_ref[...], (((1,), (1,)), ((), ())), preferred_element_type=F32)

    dconv_s[rows : rows + 8, :] = jnp.zeros((8, width), F32)

    @pl.loop(0, 8)
    def _(s):
        t0 = pl.multiple_of(s * seg, seg)
        at, ext = pl.ds(t0, seg), pl.ds(t0, seg + 8)
        same = [mask_ref[ext, k : k + 1] for k in range(3)]
        for cols in tiles:
            d = dconv_s[ext, cols]
            b = branch_ref[at, cols]
            sums_ref[4, :, cols] += fold_rows(d[:seg])
            sums_ref[0, :, cols] += fold_rows(d[:seg] * b)
            total = vec_ref[0:1, cols] * d[:seg]
            for k in range(1, 4):
                moved = pltpu.roll(d * same[k - 1], seg + 8 - k, 0)[:seg]
                total = total + vec_ref[k : k + 1, cols] * moved
                sums_ref[k, :, cols] += fold_rows(moved * b)
            dbranch_ref[at, cols] = total.astype(BF16)


def mixer_backward(d_product, gated_pre, states, branch_pre, conv_out, masks, vecs, w_cat):
    rows, width = branch_pre.shape
    lanes = width // LANES
    return pl.pallas_call(
        mixer_backward_kernel,
        out_shape=[
            jax.ShapeDtypeStruct((rows, width), BF16),
            jax.ShapeDtypeStruct((rows, 2 * width), BF16),
            jax.ShapeDtypeStruct((rows, width), BF16),
            jax.ShapeDtypeStruct((8, 8, width), F32),
        ],
        scratch_shapes=[
            pltpu.VMEM((rows, 2 * width), F32),
            pltpu.VMEM((rows, width), F32),
            pltpu.VMEM((rows, width), F32),
            pltpu.VMEM((lanes, rows + 8, LANES), F32),
            pltpu.VMEM((lanes, rows, LANES), F32),
            pltpu.VMEM((lanes, rows, LANES), F32),
            pltpu.VMEM((rows + 8, width), F32),
        ],
        compiler_params=pltpu.CompilerParams(vmem_limit_bytes=VMEM_BYTES),
        cost_estimate=pl.CostEstimate(flops=8 * rows * width * width, bytes_accessed=rows * width * 26, transcendentals=8 * rows * width),
        name="mixer_backward",
    )(d_product, gated_pre, states, branch_pre, conv_out, masks, vecs, w_cat)


class Stage:
    def __init__(self, stride, size, later):
        self.stride, self.size, self.later = stride, size, later
        self.blocks = 1
        for s in later:
            self.blocks *= s.size
        self.digit = lax.rem(lax.axis_index("dp") // stride, size)

    def offset(self, position):
        total = 0
        for s in reversed(self.later):
            total = total + lax.rem(position, s.size) * s.stride
            position = position // s.size
        return total


def digit_sizes(n):
    if n == 8:
        return [2, 4]
    sizes = []
    while n > 1:
        m = 4 if n % 4 == 0 else 2 if n % 2 == 0 else n
        sizes.append(m)
        n //= m
    return sizes


def make_stages(n, last_first):
    digits, stride = [], 1
    for m in digit_sizes(n):
        digits.append((stride, m))
        stride *= m
    if last_first:
        digits = digits[1:] + digits[:1]
    stages = []
    for stride, m in reversed(digits):
        stages.insert(0, Stage(stride, m, list(stages)))
    return stages


class Item:
    def __init__(self, number, stages, left, right, width, refs):
        self.number, self.stages, self.left, self.right, self.width = number, stages, left, right, width
        self.columns = right.shape[1]
        self.out, self.recv, self.send, self.send_sem, self.recv_sem = refs

    def message(self, t, back, k, slot):
        stage = self.stages[t]
        step = jnp.where(back, -stage.stride, stage.stride)
        return pltpu.make_async_remote_copy(
            src_ref=self.send[t].at[slot],
            dst_ref=self.recv[t].at[back, k - 1],
            send_sem=self.send_sem[t].at[slot],
            recv_sem=self.recv_sem[t].at[back, k - 1],
            device_id={"dp": lax.axis_index("dp") + step},
            device_id_type=pl.DeviceIdType.MESH,
        )


class Engine:
    def __init__(self, left_s, got_s, sem):
        self.left_s, self.got_s, self.sem = left_s, got_s, sem

    def fetch_left(self, item, block):
        source = item.left.at[block] if len(item.left.shape) == 3 else item.left.at[:, pl.ds(pl.multiple_of(block * item.width, item.width), item.width)]
        return pltpu.make_async_copy(source, self.left_s, self.sem.at[0])

    def product(self, item, block, gots, store):
        fetch = self.fetch_left(item, block)
        fetch.start()
        views = []
        for i, (condition, source) in enumerate(gots):
            view = self.got_s.at[i, :, pl.ds(0, item.columns)]
            views.append(view)

            @pl.when(condition)
            def _(view=view, source=source, i=i):
                pltpu.make_async_copy(source, view, self.sem.at[1 + i]).start()

        for i, (condition, source) in enumerate(gots):

            @pl.when(condition)
            def _(view=views[i], source=source, i=i):
                pltpu.make_async_copy(source, view, self.sem.at[1 + i]).wait()

        fetch.wait()
        tile = 512 if item.columns % 512 == 0 else item.columns
        for c in range(item.columns // tile):
            cols = pl.ds(c * tile, tile)
            total = lax.dot_general(self.left_s[...], item.right[:, cols], (((0,), (0,)), ((), ())), preferred_element_type=F32)
            for (condition, _), view in zip(gots, views):
                total = total + jnp.where(condition, view[:, cols].astype(F32), 0.0)
            store(cols, total)

    def arrived(self, item, t, position):
        found = []
        for u in range(t):
            stage = item.stages[u]
            spot = position
            rows = None
            scale = 1
            for s in item.stages[t:]:
                scale *= s.size
            lead = 0
            for s in item.stages[u + 1 : t]:
                lead = lead * s.size + s.digit
            rows = pl.ds((lead * scale + spot) * item.width, item.width)
            last = stage.size - 2
            if stage.size == 2:
                back = jnp.where(stage.digit == 0, 1, 0)
                found.append((stage.digit >= 0, item.recv[u].at[back, last, rows]))
            else:
                found.append((stage.digit >= 1, item.recv[u].at[0, last, rows]))
                found.append((stage.digit <= stage.size - 2, item.recv[u].at[1, last, rows]))
        return found

    def own_base(self, item, t):
        base = 0
        for s in item.stages[:t]:
            base = base + s.digit * s.stride
        return base

    def wait_last(self, item, t):
        stage = item.stages[t]
        for back in range(2):
            me = stage.digit if back == 0 else stage.size - 1 - stage.digit

            @pl.when(me >= 1)
            def _(back=back):
                item.message(t, back, stage.size - 1, 0).wait_recv()

    def round(self, item, t, k):
        stage = item.stages[t]
        if k == 1 and t > 0:
            self.wait_last(item, t - 1)
        base = self.own_base(item, t)

        @pl.loop(0, 2)
        def _(back):
            me = jnp.where(back == 0, stage.digit, stage.size - 1 - stage.digit)

            @pl.when(me <= k - 1)
            def _():
                there = me + stage.size - k
                value = jnp.where(back == 0, there, stage.size - 1 - there)
                slot = jnp.where(value > stage.digit, value - 1, value)
                if k > 1:

                    @pl.when(me >= 1)
                    def _():
                        item.message(t, back, k - 1, 0).wait_recv()

                @pl.loop(0, stage.blocks)
                def _(p):
                    block = base + value * stage.stride + stage.offset(p)
                    rows = pl.ds(p * item.width, item.width)
                    gots = self.arrived(item, t, value * stage.blocks + p)
                    if k > 1:
                        gots.append((me >= 1, item.recv[t].at[back, k - 2, rows]))

                    def store(cols, total):
                        item.send[t][slot, rows, cols] = total.astype(BF16)

                    self.product(item, block, gots, store)

                item.message(t, back, k, slot).start()

    def finish(self, item, out_s):
        t = len(item.stages)
        self.wait_last(item, t - 1)

        def store(cols, total):
            out_s[:, cols] = total

        self.product(item, self.own_base(item, t), self.arrived(item, t, 0), store)
        copy = pltpu.make_async_copy(out_s.at[:, pl.ds(0, item.columns)], item.out, self.sem.at[0])
        copy.start()
        copy.wait()

    def drain(self, item):
        for t, stage in enumerate(item.stages):
            for slot in range(stage.size - 1):
                item.message(t, 0, 1, slot).wait_send()


def dp_scatter_kernel(plan, order, lefts_of, widths, *refs):
    count = len(plan)
    n_left = max(lefts_of) + 1
    lefts, refs = refs[:n_left], refs[n_left:]
    rights_hbm, refs = refs[:count], refs[count:]
    outs, refs = refs[:count], refs[count:]
    all_stages = [make_stages(lax.axis_size("dp"), last_first) for last_first in plan]
    recv, sends, send_sems, recv_sems = [], [], [], []
    for stages in all_stages:
        recv.append(refs[: len(stages)])
        refs = refs[len(stages) :]
    rights, refs = refs[:count], refs[count:]
    for stages in all_stages:
        sends.append(refs[: len(stages)])
        refs = refs[len(stages) :]
    for stages in all_stages:
        send_sems.append(refs[: len(stages)])
        recv_sems.append(refs[len(stages) : 2 * len(stages)])
        refs = refs[2 * len(stages) :]
    left_s, got_s, out_s, right_sem, sem = refs
    loads = [pltpu.make_async_copy(rights_hbm[i], rights[i], right_sem.at[i]) for i in range(count)]
    for load in loads:
        load.start()
    items = [
        Item(i, all_stages[i], lefts[lefts_of[i]], rights[i], widths, (outs[i], recv[i], sends[i], send_sems[i], recv_sems[i]))
        for i in range(count)
    ]
    engine = Engine(left_s, got_s, sem)
    loaded = set()
    for i, t, k in order:
        if i not in loaded:
            loads[i].wait()
            loaded.add(i)
        if t < len(all_stages[i]):
            engine.round(items[i], t, k)
        else:
            engine.finish(items[i], out_s)
    for item in items:
        engine.drain(item)


def task_order(plan, names, n):
    tasks = []
    for i, last_first in enumerate(plan):
        sizes = digit_sizes(n)
        if last_first:
            sizes = sizes[1:] + sizes[:1]
        tasks.append([(i, t, k) for t, m in enumerate(sizes) for k in range(1, m)] + [(i, len(sizes), 0)])
    out, at = [], [0] * len(plan)
    for i in names:
        if at[i] < len(tasks[i]):
            out.append(tasks[i][at[i]])
            at[i] += 1
    for i in range(len(plan)):
        out += tasks[i][at[i] :]
    return out


def dp_scatter(lefts, lefts_of, rights, plan, names):
    n = lax.axis_size("dp")
    tokens, features = lefts[0].shape
    width = features // n
    if width % LANES:
        lefts = [v.reshape(tokens, n, width).transpose(1, 0, 2) for v in lefts]
    widest = max(r.shape[1] for r in rights)
    hbm = pl.BlockSpec(memory_space=pl.ANY)
    out_shape = [jax.ShapeDtypeStruct((width, r.shape[1]), F32) for r in rights]
    send_shapes, semaphores = [], []
    for r, last_first in zip(rights, plan):
        sizes = digit_sizes(n)
        if last_first:
            sizes = sizes[1:] + sizes[:1]
        left_over, sends, recvs = n, [], []
        for m in sizes:
            left_over //= m
            out_shape.append(jax.ShapeDtypeStruct((2, m - 1, left_over * width, r.shape[1]), BF16))
            send_shapes.append(pltpu.VMEM((m - 1, left_over * width, r.shape[1]), BF16))
            sends.append(pltpu.SemaphoreType.DMA((m - 1,)))
            recvs.append(pltpu.SemaphoreType.DMA((2, m - 1)))
        semaphores += sends + recvs
    gots = 2 * len(digit_sizes(n))
    scratch = [pltpu.VMEM(r.shape, BF16) for r in rights] + send_shapes + semaphores
    scratch += [
        pltpu.VMEM((tokens, width), BF16),
        pltpu.VMEM((gots, width, widest), BF16),
        pltpu.VMEM((width, widest), F32),
        pltpu.SemaphoreType.DMA((len(rights),)),
        pltpu.SemaphoreType.DMA((1 + gots,)),
    ]
    columns = sum(r.shape[1] for r in rights)
    results = pl.pallas_call(
        functools.partial(dp_scatter_kernel, plan, task_order(plan, names, n), lefts_of, width),
        out_shape=out_shape,
        in_specs=[hbm] * (len(lefts) + len(rights)),
        out_specs=[hbm] * len(out_shape),
        scratch_shapes=scratch,
        compiler_params=pltpu.CompilerParams(vmem_limit_bytes=VMEM_BYTES, has_side_effects=True),
        cost_estimate=pl.CostEstimate(flops=2 * tokens * features * columns, bytes_accessed=4 * features * columns, transcendentals=0),
        name="dp_scatter",
    )(*lefts, *rights)
    return results[: len(rights)]

DP_PLAN = [True, False, False, False, False, False]
DP_ORDER = [0, 1, 2, 0, 1, 0, 1, 3, 4, 5, 1, 0, 1, 2, 2, 0, 2, 2, 3, 3, 3, 3, 4, 4, 4, 4, 5, 5, 5, 5]


def rms_stats(values):
    return lax.rsqrt(jnp.mean(values * values, axis=-1, keepdims=True) + epsilon)


def rms_back(values, inverse, gain, d_normed):
    weighted = gain * d_normed
    inner = jnp.mean(weighted * values, axis=-1, keepdims=True)
    d_values = inverse * weighted - values * (inverse * inverse * inverse * inner)
    return d_values, jnp.sum(d_normed * values * inverse, axis=0)


def dot(left, right, dims, out=F32):
    return lax.dot_general(left, right, (dims, ((), ())), preferred_element_type=F32).astype(out)


def spread_heads(weight):
    heads, width = weight.shape[:2]
    eye = jnp.eye(heads, dtype=weight.dtype)
    return (weight[:, :, None, :] * eye[:, None, :, None]).reshape(heads * width, heads * width)


def head_blocks(dense, heads, width):
    return jnp.stack([dense[h * width : (h + 1) * width, h * width : (h + 1) * width] for h in range(heads)])


def on_device(
    stream_in, segments, first_gain, gelu_gate_weight, recurrent_branch_weight, conv_kernel, conv_bias, recur_weight, recur_bias,
    inlet_weight, inlet_bias, decay_param, recurrent_output_weight, second_gain, gate_projection_weight, up_projection_weight,
    down_projection_weight, cotangent,
):
    values = stream_in[0].astype(F32)
    seq_len = segments.shape[1]
    heads, head_width = recur_weight.shape[:2]
    gather = lambda v: lax.all_gather(v, "tensor", axis=0, tiled=True)
    reduce = lambda v: lax.psum_scatter(v, "tensor", scatter_dimension=0, tiled=True).astype(F32)

    ids = jnp.pad(segments[0], (3, 8), constant_values=-1)
    same = [(ids[3 - k : 3 - k + seq_len] == segments[0]).astype(F32) for k in range(1, 4)]
    masks = jnp.pad(jnp.stack(same, axis=1), ((0, 8), (0, 5)))
    softplus = jax.nn.softplus(-decay_param)
    vecs = jnp.concatenate([conv_kernel, jnp.stack([conv_bias, recur_bias, inlet_bias, softplus])])
    w_cat = jnp.concatenate([spread_heads(recur_weight), spread_heads(inlet_weight)], axis=1)

    first_inverse = rms_stats(values)
    normed = gather((values * first_inverse * first_gain).astype(BF16))
    cot = gather(cotangent[0])
    gated_pre = dot(normed, gelu_gate_weight, ((1,), (0,)))
    branch_pre = dot(normed, recurrent_branch_weight, ((1,), (0,)))
    conv_out, states, product = mixer_forward(branch_pre, gated_pre, masks, vecs, w_cat)
    attended = reduce(dot(product, recurrent_output_weight, ((1,), (0,)), BF16))
    middle = values + attended
    second_inverse = rms_stats(middle)
    normed_two = gather((middle * second_inverse * second_gain).astype(BF16))
    gate_pre = dot(normed_two, gate_projection_weight, ((1,), (0,)))
    up_pre = dot(normed_two, up_projection_weight, ((1,), (0,)))
    gate_act, gate_slope = gelu_parts(gate_pre)
    hidden = (gate_act * up_pre).astype(BF16)
    d_hidden = dot(cot, down_projection_weight, ((1,), (1,)))
    d_gate = (d_hidden * up_pre * gate_slope).astype(BF16)
    d_up = (d_hidden * gate_act).astype(BF16)
    d_normed_two = reduce(
        (dot(d_gate, gate_projection_weight, ((1,), (1,))) + dot(d_up, up_projection_weight, ((1,), (1,)))).astype(BF16)
    )
    ffn_out = reduce(dot(hidden, down_projection_weight, ((1,), (0,)), BF16))
    stream_out = middle + ffn_out
    d_middle, grad_second = rms_back(middle, second_inverse, second_gain, d_normed_two)
    d_middle = cotangent[0].astype(F32) + d_middle
    d_attended = gather(d_middle.astype(BF16))
    d_product = dot(d_attended, recurrent_output_weight, ((1,), (1,)))
    d_gated, d_ri, d_branch, sums = mixer_backward(
        d_product, gated_pre, states, branch_pre, conv_out, masks, vecs, w_cat
    )
    d_normed = reduce(
        (dot(d_gated, gelu_gate_weight, ((1,), (1,))) + dot(d_branch, recurrent_branch_weight, ((1,), (1,)))).astype(BF16)
    )
    d_values, grad_first = rms_back(values, first_inverse, first_gain, d_normed)
    stream_grad = d_middle + d_values

    down_gradient, gate_gradient, up_gradient, output_gradient, gated_gradient, branch_gradient = dp_scatter(
        [cot, normed_two, d_attended, normed],
        [0, 1, 1, 2, 3, 3],
        [hidden, d_gate, d_up, product, d_gated, d_branch],
        DP_PLAN,
        DP_ORDER,
    )

    width = heads * head_width
    dense = dot(conv_out, d_ri, ((0,), (0,)))
    grad_recur = head_blocks(dense[:, :width], heads, head_width)
    grad_inlet = head_blocks(dense[:, width:], heads, head_width)
    sums = jnp.sum(sums, axis=1)
    small = jnp.concatenate([sums.reshape(-1), grad_recur.reshape(-1), grad_inlet.reshape(-1)])
    small = lax.psum(small, "dp")
    sums = small[: 8 * width].reshape(8, width)
    grad_recur, grad_inlet = small[8 * width :].reshape(2, heads, head_width, head_width)
    grad_decay = decay_scale * jax.nn.sigmoid(-decay_param) * sums[7]
    gains = lax.psum(jnp.concatenate([grad_first, grad_second]), ("dp", "tensor"))
    model = grad_first.shape[0]
    return (
        stream_out[None], stream_grad[None], gains[:model], gated_gradient, branch_gradient, sums[:4], sums[4], grad_recur, sums[5],
        grad_inlet, sums[6], grad_decay, output_gradient.T, gains[model:], gate_gradient, up_gradient, down_gradient.T,
    )


def solution(mesh):
    in_specs = (
        P("dp", "tensor", None),
        P("dp", None),
        P(),
        P(None, "tensor"),
        P(None, "tensor"),
        P(None, "tensor"),
        P("tensor"),
        P("tensor", None, None),
        P("tensor"),
        P("tensor", None, None),
        P("tensor"),
        P("tensor"),
        P("tensor", None),
        P(),
        P(None, "tensor"),
        P(None, "tensor"),
        P("tensor", None),
        P("dp", "tensor", None),
    )
    out_specs = (
        P("dp", "tensor", None),
        P("dp", "tensor", None),
        P(),
        P("dp", "tensor"),
        P("dp", "tensor"),
        P(None, "tensor"),
        P("tensor"),
        P("tensor", None, None),
        P("tensor"),
        P("tensor", None, None),
        P("tensor"),
        P("tensor"),
        P("tensor", "dp"),
        P(),
        P("dp", "tensor"),
        P("dp", "tensor"),
        P("tensor", "dp"),
    )
    return jax.shard_map(
        on_device, mesh=mesh, in_specs=in_specs, out_specs=out_specs, check_vma=False
    )
```

```python
import functools

import jax
import jax.numpy as jnp
from jax import lax
from jax.experimental import pallas as pl
from jax.experimental.pallas import tpu as pltpu
from jax.sharding import PartitionSpec as P

epsilon = 1e-06
decay_scale = 8.0
LANES = 128
GELU_C = 0.7978845608028654
GELU_K = 0.044715
F32 = jnp.float32
BF16 = jnp.bfloat16
VMEM_BYTES = 60 * 1024 * 1024


def minus_expm1(y, exp_y):
    s = 1.0 + y * (1.0 / 9.0)
    for d in range(8, 1, -1):
        s = 1.0 + (y * (1.0 / d)) * s
    return jnp.where(y > -0.5, -y * s, 1.0 - exp_y)


def gelu_parts(v):
    v2 = v * v
    t = jnp.tanh(GELU_C * v * (1.0 + GELU_K * v2))
    half = 0.5 * (1.0 + t)
    slope = half + 0.5 * v * (1.0 - t * t) * (GELU_C * (1.0 + 3.0 * GELU_K * v2))
    return v * half, slope


def lane_tiles(width):
    return [slice(j * LANES, (j + 1) * LANES) for j in range(width // LANES)]


def fold_rows(v):
    return jnp.sum(v.reshape(v.shape[0] // 8, 8, v.shape[1]), axis=0)


def gates_pre(rows, step, conv_ref, w_ref, pre_s):
    @pl.loop(0, rows // step)
    def _(i):
        r = pl.ds(pl.multiple_of(i * step, step), step)
        pre_s[r, :] = jnp.dot(conv_ref[r, :], w_ref[...], preferred_element_type=F32)


def mixer_forward_kernel(branch_ref, gated_ref, mask_ref, vec_ref, w_ref, conv_ref, states_ref, product_ref, pre_s, a_s, b_s):
    rows, width = branch_ref.shape
    seg = rows // 8
    tiles = lane_tiles(width)

    @pl.loop(0, 8)
    def _(s):
        t0 = pl.multiple_of(s * seg, seg)
        before = pl.multiple_of(jnp.maximum(t0 - 8, 0), 8)
        same = [mask_ref[pl.ds(t0, seg), k : k + 1] for k in range(3)]
        for cols in tiles:
            b = branch_ref[pl.ds(t0, seg), cols]
            ext = jnp.concatenate([branch_ref[pl.ds(before, 8), cols], b], axis=0)
            out = vec_ref[4:5, cols] + vec_ref[0:1, cols] * b
            for k in range(1, 4):
                out = out + vec_ref[k : k + 1, cols] * pltpu.roll(ext, k, 0)[8:] * same[k - 1]
            conv_ref[pl.ds(t0, seg), cols] = out.astype(BF16)

    gates_pre(rows, 256, conv_ref, w_ref, pre_s)

    @pl.loop(0, 8)
    def _(s):
        t0 = pl.multiple_of(s * seg, seg)
        c = mask_ref[pl.ds(t0, seg), 0:1]
        for j, cols in enumerate(tiles):
            cols_i = slice(width + j * LANES, width + (j + 1) * LANES)
            r = jax.nn.sigmoid(pre_s[pl.ds(t0, seg), cols] + vec_ref[5:6, cols])
            i = jax.nn.sigmoid(pre_s[pl.ds(t0, seg), cols_i] + vec_ref[6:7, cols])
            log_a = (-decay_scale * vec_ref[7:8, cols]) * r
            a = jnp.exp(log_a)
            n = jnp.sqrt(minus_expm1(2.0 * log_a, a * a))
            mult = (1.0 - c) + c * n
            a_s[j, pl.ds(t0, seg), :] = a * c
            b_s[j, pl.ds(t0, seg), :] = mult * i * conv_ref[pl.ds(t0, seg), cols].astype(F32)

    def scan_step(i, carry):
        out = []
        for j in range(len(tiles)):
            h, p = carry[j]
            at = pl.ds(i, 8, stride=seg)
            a = a_s[j, at, :]
            h = a * h + b_s[j, at, :]
            p = a * p
            b_s[j, at, :] = h
            a_s[j, at, :] = p
            out.append((h, p))
        return tuple(out)

    one = jnp.ones((8, LANES), F32)
    lax.fori_loop(0, seg, scan_step, tuple((jnp.zeros((8, LANES), F32), one) for _ in tiles), unroll=4)

    def finish(s, carry):
        t0 = pl.multiple_of(s * seg, seg)
        out = []
        for j, cols in enumerate(tiles):
            st = b_s[j, pl.ds(t0, seg), :] + a_s[j, pl.ds(t0, seg), :] * carry[j]
            states_ref[pl.ds(t0, seg), cols] = st
            act, _ = gelu_parts(gated_ref[pl.ds(t0, seg), cols])
            product_ref[pl.ds(t0, seg), cols] = (st * act).astype(BF16)
            out.append(st[seg - 1 : seg, :])
        return tuple(out)

    lax.fori_loop(0, 8, finish, tuple(jnp.zeros((1, LANES), F32) for _ in tiles))


class MixerBackward:
    def __init__(self, masks, vecs, w_cat, states, branch, conv, dgated, dri, dbranch, sums, pre_s, a_s, n_s, ac_s, e_s, p_s):
        self.masks, self.vecs, self.w_cat, self.states, self.branch, self.conv = masks, vecs, w_cat, states, branch, conv
        self.dgated, self.dri, self.dbranch, self.sums = dgated, dri, dbranch, sums
        self.pre_s, self.a_s, self.n_s, self.ac_s, self.e_s, self.p_s = pre_s, a_s, n_s, ac_s, e_s, p_s
        self.rows, self.width = states.shape
        self.seg = self.rows // 8
        self.tiles = lane_tiles(self.width)

    @staticmethod
    def scratch(rows, width):
        lanes = width // LANES
        return [
            pltpu.VMEM((rows, 2 * width), F32),
            pltpu.VMEM((rows, width), F32),
            pltpu.VMEM((rows + 8, width), F32),
            pltpu.VMEM((lanes, rows + 8, LANES), F32),
            pltpu.VMEM((lanes, rows, LANES), F32),
            pltpu.VMEM((lanes, rows, LANES), F32),
        ]

    def gates(self):
        self.sums[...] = jnp.zeros_like(self.sums)
        gates_pre(self.rows, 256, self.conv, self.w_cat, self.pre_s)

    def factors(self, gated):
        @pl.loop(0, 8)
        def _(s):
            t0 = pl.multiple_of(s * self.seg, self.seg)
            at = pl.ds(t0, self.seg)
            c = self.masks[at, 0:1]
            for j, cols in enumerate(self.tiles):
                cols_i = slice(self.width + j * LANES, self.width + (j + 1) * LANES)
                r = jax.nn.sigmoid(self.pre_s[at, cols] + self.vecs[5:6, cols])
                self.pre_s[at, cols] = r
                self.pre_s[at, cols_i] = jax.nn.sigmoid(self.pre_s[at, cols_i] + self.vecs[6:7, cols])
                log_a = (-decay_scale * self.vecs[7:8, cols]) * r
                a = jnp.exp(log_a)
                d = self.a_s[at, cols]
                self.a_s[at, cols] = a
                self.n_s[at, cols] = jnp.sqrt(minus_expm1(2.0 * log_a, a * a))
                self.ac_s[j, at, :] = a * c
                act, slope = gelu_parts(gated[at, cols])
                self.e_s[j, at, :] = d * act
                self.dgated[at, cols] = (d * self.states[at, cols] * slope).astype(BF16)

    def scan(self):
        seg, lanes = self.seg, len(self.tiles)
        for j in range(lanes):
            self.ac_s[j, self.rows : self.rows + 8, :] = jnp.zeros((8, LANES), F32)

        def step(q, carry):
            i = seg - 1 - q
            out = []
            for j in range(lanes):
                e, p = carry[j]
                at = pl.ds(i, 8, stride=seg)
                a = self.ac_s[j, pl.ds(i + 1, 8, stride=seg), :]
                e = a * e + self.e_s[j, at, :]
                p = a * p
                self.e_s[j, at, :] = e
                self.p_s[j, at, :] = p
                out.append((e, p))
            return tuple(out)

        one = jnp.ones((8, LANES), F32)
        lax.fori_loop(0, seg, step, tuple((jnp.zeros((8, LANES), F32), one) for _ in self.tiles), unroll=4)

    def gate_gradients(self):
        seg, width = self.seg, self.width

        def finish(q, carry):
            s = 7 - q
            t0 = pl.multiple_of(s * seg, seg)
            at = pl.ds(t0, seg)
            before = pl.multiple_of(jnp.maximum(t0 - 8, 0), 8)
            c = self.masks[at, 0:1]
            out = []
            for j, cols in enumerate(self.tiles):
                cols_i = slice(width + j * LANES, width + (j + 1) * LANES)
                e = self.e_s[j, at, :] + self.p_s[j, at, :] * carry[j]
                out.append(e[0:1, :])
                ext = jnp.concatenate([self.states[pl.ds(before, 8), cols], self.states[at, cols]], axis=0)
                earlier = pltpu.roll(ext, 1, 0)[8:]
                r, i, a, n = self.pre_s[at, cols], self.pre_s[at, cols_i], self.a_s[at, cols], self.n_s[at, cols]
                cv = self.conv[at, cols].astype(F32)
                ec = e * c
                d_log = a * (ec * earlier) - ec * i * cv * (a * a / n)
                rr = d_log * r
                dr = ((-decay_scale * self.vecs[7:8, cols]) * rr * (1.0 - r)).astype(BF16)
                em = e * ((1.0 - c) + c * n) * i
                di = (em * cv * (1.0 - i)).astype(BF16)
                self.dri[at, cols] = dr
                self.dri[at, cols_i] = di
                self.n_s[at, cols] = em
                self.sums[5, :, cols] += fold_rows(dr.astype(F32))
                self.sums[6, :, cols] += fold_rows(di.astype(F32))
                self.sums[7, :, cols] += fold_rows(rr)
            return tuple(out)

        lax.fori_loop(0, 8, finish, tuple(jnp.zeros((1, LANES), F32) for _ in self.tiles))

        @pl.loop(0, self.rows // 256)
        def _(i):
            at = pl.ds(pl.multiple_of(i * 256, 256), 256)
            self.n_s[at, :] += dot_nt(self.dri[at, :], self.w_cat[...])

        self.n_s[self.rows : self.rows + 8, :] = jnp.zeros((8, width), F32)

    def convolution(self):
        @pl.loop(0, 8)
        def _(s):
            t0 = pl.multiple_of(s * self.seg, self.seg)
            at, ext = pl.ds(t0, self.seg), pl.ds(t0, self.seg + 8)
            same = [self.masks[ext, k : k + 1] for k in range(3)]
            for cols in self.tiles:
                d = self.n_s[ext, cols]
                b = self.branch[at, cols]
                self.sums[4, :, cols] += fold_rows(d[: self.seg])
                self.sums[0, :, cols] += fold_rows(d[: self.seg] * b)
                total = self.vecs[0:1, cols] * d[: self.seg]
                for k in range(1, 4):
                    moved = pltpu.roll(d * same[k - 1], self.seg + 8 - k, 0)[: self.seg]
                    total = total + self.vecs[k : k + 1, cols] * moved
                    self.sums[k, :, cols] += fold_rows(moved * b)
                self.dbranch[at, cols] = total.astype(BF16)


def dot_nt(left, right):
    return lax.dot_general(left, right, (((1,), (1,)), ((), ())), preferred_element_type=F32)


class Stage:
    def __init__(self, stride, size, later):
        self.stride, self.size, self.later = stride, size, later
        self.blocks = 1
        for s in later:
            self.blocks *= s.size
        self.digit = lax.rem(lax.axis_index("dp") // stride, size)

    def offset(self, position):
        total = 0
        for s in reversed(self.later):
            total = total + lax.rem(position, s.size) * s.stride
            position = position // s.size
        return total


def digit_sizes(n):
    if n == 8:
        return [2, 4]
    sizes = []
    while n > 1:
        m = 4 if n % 4 == 0 else 2 if n % 2 == 0 else n
        sizes.append(m)
        n //= m
    return sizes


def make_stages(n, last_first):
    digits, stride = [], 1
    for m in digit_sizes(n):
        digits.append((stride, m))
        stride *= m
    if last_first:
        digits = digits[1:] + digits[:1]
    stages = []
    for stride, m in reversed(digits):
        stages.insert(0, Stage(stride, m, list(stages)))
    return stages


class Item:
    def __init__(self, stages, left, right, width, ready, refs):
        self.stages, self.left, self.right, self.width, self.ready = stages, left, right, width, ready
        self.columns = right.shape[1]
        self.out, self.recv, self.send, self.send_sem, self.recv_sem = refs

    def message(self, t, back, k, slot, rows=None):
        stage = self.stages[t]
        rows = pl.ds(0, stage.blocks * self.width) if rows is None else rows
        step = jnp.where(back, -stage.stride, stage.stride)
        return pltpu.make_async_remote_copy(
            src_ref=self.send[t].at[slot, rows],
            dst_ref=self.recv[t].at[back, k - 1, rows],
            send_sem=self.send_sem[t].at[slot],
            recv_sem=self.recv_sem[t].at[back, k - 1],
            device_id={"dp": lax.axis_index("dp") + step},
            device_id_type=pl.DeviceIdType.MESH,
        )


class Engine:
    def __init__(self, left_s, got_s, total_s, sem):
        self.left_s, self.got_s, self.total_s, self.sem = left_s, got_s, total_s, sem

    def product(self, item, block, store):
        if len(item.left.shape) == 3:
            source = item.left.at[block]
        else:
            source = item.left.at[:, pl.ds(pl.multiple_of(block * item.width, item.width), item.width)]
        fetch = pltpu.make_async_copy(source, self.left_s, self.sem.at[0])
        fetch.start()
        fetch.wait()
        tile = 512 if item.columns % 512 == 0 else item.columns
        for c in range(item.columns // tile):
            cols = pl.ds(c * tile, tile)
            store(cols, lax.dot_general(self.left_s[...], item.right[:, cols], (((0,), (0,)), ((), ())), preferred_element_type=F32))

    def add_gots(self, item, rows, gots, store):
        copies = []
        for i, (condition, source) in enumerate(gots):
            copy = pltpu.make_async_copy(source, self.got_s.at[i, :, pl.ds(0, item.columns)], self.sem.at[1 + i])
            copies.append(copy)

            @pl.when(condition)
            def _(copy=copy):
                copy.start()

        for (condition, _), copy in zip(gots, copies):

            @pl.when(condition)
            def _(copy=copy):
                copy.wait()

        @pl.loop(0, item.width // 16)
        def _(r):
            at = pl.ds(pl.multiple_of(r * 16, 16), 16)
            here = pl.ds(pl.multiple_of(rows + r * 16, 16), 16)
            total = self.total_s[here, pl.ds(0, item.columns)]
            for i, (condition, _) in enumerate(gots):
                total = total + jnp.where(condition, self.got_s[i, at, pl.ds(0, item.columns)].astype(F32), 0.0)
            store(here, total)

    def arrived(self, item, t, position):
        found = []
        for u in range(t):
            stage = item.stages[u]
            spot = position
            rows = None
            scale = 1
            for s in item.stages[t:]:
                scale *= s.size
            lead = 0
            for s in item.stages[u + 1 : t]:
                lead = lead * s.size + s.digit
            rows = pl.ds((lead * scale + spot) * item.width, item.width)
            last = stage.size - 2
            if stage.size == 2:
                back = jnp.where(stage.digit == 0, 1, 0)
                found.append((stage.digit >= 0, item.recv[u].at[back, last, rows]))
            else:
                found.append((stage.digit >= 1, item.recv[u].at[0, last, rows]))
                found.append((stage.digit <= stage.size - 2, item.recv[u].at[1, last, rows]))
        return found

    def own_base(self, item, t):
        base = 0
        for s in item.stages[:t]:
            base = base + s.digit * s.stride
        return base

    def wait_last(self, item, t):
        if t < item.ready:
            return
        stage = item.stages[t]
        for back in range(2):
            me = stage.digit if back == 0 else stage.size - 1 - stage.digit

            @pl.when(me >= 1)
            def _(back=back):
                item.message(t, back, stage.size - 1, 0).wait_recv()

    def round(self, item, t, k):
        stage = item.stages[t]
        base = self.own_base(item, t)
        alone = t == 0 and k == 1

        @pl.loop(0, 2)
        def _(back):
            me = jnp.where(back == 0, stage.digit, stage.size - 1 - stage.digit)
            there = me + stage.size - k
            value = jnp.where(back == 0, there, stage.size - 1 - there)
            slot = jnp.where(value > stage.digit, value - 1, value)

            @pl.when(me <= k - 1)
            def _():
                @pl.loop(0, stage.blocks)
                def _(p):
                    at = pl.ds(pl.multiple_of(p * item.width, item.width), item.width)

                    def store(cols, total):
                        if alone:
                            item.send[t][slot, at, cols] = total.astype(BF16)
                        else:
                            self.total_s[at, cols] = total

                    self.product(item, base + value * stage.stride + stage.offset(p), store)
                    if alone:
                        item.message(t, back, k, slot, at).start()

            if k == 1 and t > 0:

                @pl.when(back == 0)
                def _():
                    self.wait_last(item, t - 1)

            if not alone:

                @pl.when(me <= k - 1)
                def _():
                    if k > 1:

                        @pl.when(me >= 1)
                        def _():
                            item.message(t, back, k - 1, 0).wait_recv()

                    @pl.loop(0, stage.blocks)
                    def _(p):
                        rows = pl.multiple_of(p * item.width, item.width)
                        at = pl.ds(rows, item.width)
                        gots = self.arrived(item, t, value * stage.blocks + p)
                        if k > 1:
                            gots.append((me >= 1, item.recv[t].at[back, k - 2, at]))

                        def store(here, total):
                            item.send[t][slot, here, :] = total.astype(BF16)

                        self.add_gots(item, rows, gots, store)
                        item.message(t, back, k, slot, at).start()

    def finish(self, item):
        t = len(item.stages)

        def store(cols, total):
            self.total_s[pl.ds(0, item.width), cols] = total

        self.product(item, self.own_base(item, t), store)
        self.wait_last(item, t - 1)

        def store_sum(here, total):
            self.total_s[here, pl.ds(0, item.columns)] = total

        self.add_gots(item, 0, self.arrived(item, t, 0), store_sum)
        copy = pltpu.make_async_copy(self.total_s.at[pl.ds(0, item.width), pl.ds(0, item.columns)], item.out, self.sem.at[0])
        copy.start()
        copy.wait()

    def drain(self, item, stages):
        for t in stages:
            for slot in range(item.stages[t].size - 1):
                item.message(t, 0, 1, slot).wait_send()


def stage_shapes(n, last_first, width, columns):
    sizes = digit_sizes(n)
    if last_first:
        sizes = sizes[1:] + sizes[:1]
    left, found = n, []
    for t, m in enumerate(sizes):
        left //= m
        found.append(
            (
                jax.ShapeDtypeStruct((2, m - 1, left * width, columns), BF16),
                pltpu.VMEM((m - 1, left * width, columns), BF16),
                pltpu.SemaphoreType.DMA((m - 1,)),
                pltpu.SemaphoreType.DMA((2, m - 1)),
                left * width if t > 0 or m > 2 else width,
            )
        )
    return found


class Reader:
    def __init__(self, refs):
        self.refs, self.at = refs, 0

    def __call__(self, count=None):
        start = self.at
        self.at += 1 if count is None else count
        return self.refs[start] if count is None else list(self.refs[start : self.at])


def column_blocks(left, n):
    tokens, features = left.shape
    width = features // n
    return left.reshape(tokens, n, width).transpose(1, 0, 2) if width % LANES else left


class TensorLine:
    def __init__(self):
        self.index = lax.axis_index("tensor")
        self.mate, self.peer, self.cross = self.index ^ 1, self.index ^ 2, self.index ^ 3


def copy_in(source, target, sem):
    copy = pltpu.make_async_copy(source, target, sem)
    copy.start()
    return copy


def remote(source, target, send_sem, recv_sem, axis, index):
    return pltpu.make_async_remote_copy(
        src_ref=source, dst_ref=target, send_sem=send_sem, recv_sem=recv_sem,
        device_id={axis: index}, device_id_type=pl.DeviceIdType.MESH,
    )


class TensorReduce:
    def __init__(self, line, part, from_mate, from_peer, own_v, got_v, send_v, send_sem, recv_sem, sem):
        self.line, self.part, self.from_mate, self.from_peer = line, part, from_mate, from_peer
        self.own_v, self.got_v, self.send_v, self.sem = own_v, got_v, send_v, sem
        self.rows = part.shape[0] // 4
        self.mates = [
            remote(self.block(line.cross), from_mate.at[0], send_sem.at[0], recv_sem.at[0], "tensor", line.mate),
            remote(self.block(line.mate), from_mate.at[1], send_sem.at[1], recv_sem.at[1], "tensor", line.mate),
        ]
        self.over = remote(send_v, from_peer, send_sem.at[2], recv_sem.at[2], "tensor", line.peer)

    def block(self, index):
        return self.part.at[pl.ds(pl.multiple_of(index * self.rows, self.rows), self.rows)]

    def start(self):
        for copy in self.mates:
            copy.start()

    def middle(self):
        own = copy_in(self.block(self.line.peer), self.own_v, self.sem.at[0])
        self.mates[0].wait_recv()
        got = copy_in(self.from_mate.at[0], self.got_v.at[0], self.sem.at[1])
        own.wait()
        got.wait()

        @pl.loop(0, self.rows // 16)
        def _(r):
            at = pl.ds(pl.multiple_of(r * 16, 16), 16)
            self.send_v[at, :] = (self.own_v[at, :].astype(F32) + self.got_v[0, at, :].astype(F32)).astype(BF16)

        self.over.start()

    def end(self, use):
        own = copy_in(self.block(self.line.index), self.own_v, self.sem.at[0])
        self.mates[1].wait_recv()
        got = copy_in(self.from_mate.at[1], self.got_v.at[0], self.sem.at[1])
        self.over.wait_recv()
        over = copy_in(self.from_peer, self.got_v.at[1], self.sem.at[2])
        own.wait()
        got.wait()
        over.wait()

        @pl.loop(0, self.rows // 16)
        def _(r):
            at = pl.ds(pl.multiple_of(r * 16, 16), 16)
            use(at, self.own_v[at, :].astype(F32) + self.got_v[0, at, :].astype(F32) + self.got_v[1, at, :].astype(F32))

    def drain(self):
        for copy in self.mates:
            copy.wait_send()
        self.over.wait_send()

    @staticmethod
    def results(tokens, features):
        return [jax.ShapeDtypeStruct((2, tokens // 4, features), BF16), jax.ShapeDtypeStruct((tokens // 4, features), BF16)]

    @staticmethod
    def semaphores():
        return [pltpu.SemaphoreType.DMA((3,)), pltpu.SemaphoreType.DMA((3,)), pltpu.SemaphoreType.DMA((3,))]

    @staticmethod
    def buffers(tokens, features):
        rows = tokens // 4
        return [pltpu.VMEM((rows, features), BF16), pltpu.VMEM((2, rows, features), BF16), pltpu.VMEM((rows, features), BF16)]


def norm_backward(values, gain, d_normed):
    inverse = lax.rsqrt(jnp.mean(values * values, axis=-1, keepdims=True) + epsilon)
    weighted = gain * d_normed
    inner = jnp.mean(weighted * values, axis=-1, keepdims=True)
    return inverse * weighted - values * (inverse * inverse * inverse * inner), d_normed * values * inverse


HBM = pl.BlockSpec(memory_space=pl.ANY)
IN_VMEM = pl.BlockSpec(memory_space=pltpu.VMEM)


def chain_kernel(n, width, *refs):
    take = Reader(refs)
    part, middle, cot_own, w_out, gated, branch, states, conv = take(8)
    gain, masks, vecs, w_cat = take(4)
    left_down, left_gate, right_down, right_gate = take(4)
    d_middle, att, dgated_o, dri_o, dbranch_o, from_mate, from_peer, down_recv, gate_recv = take(9)
    sums, gain_grad = take(2)
    down_v, down_send, down_ss, down_rs, gate_send, gate_ss, gate_rs = take(7)
    left_s, got_s, total_s, rs_send, rs_recv, rs_sem, ag_send, ag_recv, sem, engine_sem = take(10)
    tokens, features = part.shape
    rows, channels = tokens // 4, conv.shape[1]
    line = TensorLine()
    engine = Engine(left_s, got_s, total_s, engine_sem)
    down_load = copy_in(right_down, down_v, sem.at[6])
    down = Item(make_stages(n, True), left_down, down_v, width, 0, (None, [down_recv], [down_send], [down_ss], [down_rs]))

    def rounds(item):
        return list(range(1, item.stages[0].size))

    def att_rows(index):
        return att.at[pl.ds(pl.multiple_of(index * rows, rows), rows)]

    first, between, last = rounds(down)[:1], rounds(down)[1:-1], rounds(down)[1:][-1:]

    def tensor_phase(gate_v, own_v, got_v, send_v, middle_v, cot_v, dmid_v, att_v):
        reduce = TensorReduce(line, part, from_mate, from_peer, own_v, got_v, send_v, rs_send, rs_recv, rs_sem)
        reduce.start()
        gate_load = copy_in(right_gate, gate_v, sem.at[7])
        loads = [copy_in(middle, middle_v, sem.at[0]), copy_in(cot_own, cot_v, sem.at[1])]
        gate = Item(make_stages(n, False), left_gate, gate_v, width, 0, (None, [gate_recv], [gate_send], [gate_ss], [gate_rs]))
        down_load.wait()
        for k in first:
            engine.round(down, 0, k)
        reduce.middle()
        gate_load.wait()
        for k in rounds(gate):
            engine.round(gate, 0, k)
        for load in loads:
            load.wait()
        gain_grad[...] = jnp.zeros_like(gain_grad)

        def use(at, total):
            back, terms = norm_backward(middle_v[at, :], gain[...], total)
            value = cot_v[at, :].astype(F32) + back
            dmid_v[at, :] = value
            att_v[at, :] = value.astype(BF16)
            gain_grad[...] += fold_rows(terms)

        reduce.end(use)
        across = [
            remote(att_v, att_rows(line.index), ag_send.at[0], ag_recv.at[0], "tensor", line.peer),
            remote(att_v, att_rows(line.index), ag_send.at[1], ag_recv.at[1], "tensor", line.mate),
        ]
        for copy in across:
            copy.start()
        keep = [copy_in(att_v, att_rows(line.index), sem.at[0]), copy_in(dmid_v, d_middle, sem.at[1])]
        for k in between:
            engine.round(down, 0, k)
        across[0].wait_recv()
        forward = remote(att_rows(line.peer), att_rows(line.peer), ag_send.at[2], ag_recv.at[2], "tensor", line.mate)
        forward.start()
        across[1].wait_recv()
        forward.wait_recv()
        for copy in keep:
            copy.wait()
        for copy in [*across, forward]:
            copy.wait_send()
        reduce.drain()
        for t in (0,):
            engine.drain(gate, [t])
            engine.wait_last(gate, t)

    pl.run_scoped(
        tensor_phase,
        pltpu.VMEM(right_gate.shape, BF16),
        *TensorReduce.buffers(tokens, features),
        pltpu.VMEM((rows, features), F32),
        pltpu.VMEM((rows, features), BF16),
        pltpu.VMEM((rows, features), F32),
        pltpu.VMEM((rows, features), BF16),
    )

    def mixer_phase(gated_v, states_v, conv_v, dgated_v, dri_v, dbranch_v, att_v, w_v, *scratch):
        w_load = copy_in(w_out, w_v, sem.at[0])
        blocks = [copy_in(att_rows(0), att_v.at[0], sem.at[4])]
        loads = [copy_in(conv, conv_v, sem.at[1]), copy_in(gated, gated_v, sem.at[2]), copy_in(states, states_v, sem.at[3])]
        mixer = MixerBackward(masks, vecs, w_cat, states_v, gated_v, conv_v, dgated_v, dri_v, dbranch_v, sums, *scratch)
        w_load.wait()
        for b in range(4):
            blocks[b].wait()
            if b < 3:
                blocks.append(copy_in(att_rows(b + 1), att_v.at[(b + 1) % 2], sem.at[4 + (b + 1) % 2]))
            mixer.a_s[pl.ds(b * rows, rows), :] = dot_nt(att_v[b % 2], w_v[...])
        loads[0].wait()
        mixer.gates()
        loads[1].wait()
        loads[2].wait()
        mixer.factors(gated_v)
        again = copy_in(branch, gated_v, sem.at[2])
        outs = [copy_in(dgated_v, dgated_o, sem.at[1])]
        for k in last:
            engine.round(down, 0, k)
        mixer.scan()
        mixer.gate_gradients()
        outs.append(copy_in(dri_v, dri_o, sem.at[3]))
        again.wait()
        mixer.convolution()
        outs.append(copy_in(dbranch_v, dbranch_o, sem.at[0]))
        for copy in outs:
            copy.wait()

    pl.run_scoped(
        mixer_phase,
        pltpu.VMEM((tokens, channels), F32),
        pltpu.VMEM((tokens, channels), F32),
        pltpu.VMEM((tokens, channels), BF16),
        pltpu.VMEM((tokens, channels), BF16),
        pltpu.VMEM((tokens, 2 * channels), BF16),
        pltpu.VMEM((tokens, channels), BF16),
        pltpu.VMEM((2, rows, features), BF16),
        pltpu.VMEM((channels, features), BF16),
        *MixerBackward.scratch(tokens, channels),
    )
    engine.drain(down, [0])
    engine.wait_last(down, 0)


def chain(part, middle, cot_own, w_out, gated_pre, branch_pre, states, conv_out, gain, masks, vecs, w_cat, cot, normed_two, hidden, d_gate):
    n = lax.axis_size("dp")
    tokens, features = part.shape
    channels, width = conv_out.shape[1], features // n
    down = stage_shapes(n, True, width, hidden.shape[1])[0]
    gate = stage_shapes(n, False, width, d_gate.shape[1])[0]
    tall = max(down[4], gate[4])
    dma = pltpu.SemaphoreType.DMA
    return pl.pallas_call(
        functools.partial(chain_kernel, n, width),
        out_shape=[
            jax.ShapeDtypeStruct((tokens // 4, features), F32),
            jax.ShapeDtypeStruct((tokens, features), BF16),
            jax.ShapeDtypeStruct((tokens, channels), BF16),
            jax.ShapeDtypeStruct((tokens, 2 * channels), BF16),
            jax.ShapeDtypeStruct((tokens, channels), BF16),
            *TensorReduce.results(tokens, features),
            down[0],
            gate[0],
            jax.ShapeDtypeStruct((8, 8, channels), F32),
            jax.ShapeDtypeStruct((8, features), F32),
        ],
        in_specs=[HBM] * 8 + [IN_VMEM] * 4 + [HBM] * 4,
        out_specs=[HBM] * 9 + [IN_VMEM] * 2,
        scratch_shapes=[
            pltpu.VMEM(hidden.shape, BF16), down[1], down[2], down[3], gate[1], gate[2], gate[3],
            pltpu.VMEM((tokens, width), BF16),
            pltpu.VMEM((1, width, hidden.shape[1]), BF16),
            pltpu.VMEM((tall, hidden.shape[1]), F32),
            *TensorReduce.semaphores(),
            dma((3,)), dma((3,)), dma((8,)), dma((2,)),
        ],
        compiler_params=pltpu.CompilerParams(vmem_limit_bytes=VMEM_BYTES, has_side_effects=True),
        cost_estimate=pl.CostEstimate(flops=12 * 10**9, bytes_accessed=60 * 10**6, transcendentals=8 * tokens * channels),
        name="chain",
    )(
        part, middle, cot_own, w_out, gated_pre, branch_pre, states, conv_out, gain, masks, vecs, w_cat,
        column_blocks(cot, n), column_blocks(normed_two, n), hidden, d_gate,
    )


def gather_sums(gains, sends, recvs, send_sems, recv_sems):
    n, line = lax.axis_size("dp"), TensorLine()
    hops = [("tensor", line.mate), ("tensor", line.peer)]
    bit = 1
    while bit < n:
        hops.append(("dp", lax.axis_index("dp") ^ bit))
        bit *= 2
    copies = [remote(sends.at[s], recvs.at[s], send_sems.at[s], recv_sems.at[s], *hop) for s, hop in enumerate(hops)]

    def begin(s):
        sends[s] = gains[...] if s == 0 else sends[s - 1] + recvs[s - 1]
        copies[s].start()

    def step(s):
        if s > 0:
            copies[s - 1].wait_recv()
        if s < len(copies):
            begin(s)
        else:
            gains[...] = sends[s - 1] + recvs[s - 1]
            for copy in copies:
                copy.wait_send()

    return [functools.partial(step, s) for s in range(len(copies) + 1)]


def finish_kernel(n, width, plan, order, lefts_of, readies, columns, *refs):
    take = Reader(refs)
    count = len(plan)
    part, part_out, middle, d_middle, stream = take(5)
    gain, gain_grad_two = take(2)
    lefts, rights_hbm = take(max(lefts_of) + 1), take(count)
    shapes = [stage_shapes(n, plan[i], width, columns[i]) for i in range(count)]
    given = [take(readies[i]) for i in range(count)]
    stream_grad_o, stream_out_o = take(2)
    outs = take(count)
    reduces = [take(2), take(2)]
    recv = [given[i] + take(len(shapes[i]) - readies[i]) for i in range(count)]
    (gains,) = take(1)
    rights = take(count)
    nones = [[None] * r for r in readies]
    sends = [nones[i] + take(len(shapes[i]) - readies[i]) for i in range(count)]
    send_sems = [nones[i] + take(len(shapes[i]) - readies[i]) for i in range(count)]
    recv_sems = [nones[i] + take(len(shapes[i]) - readies[i]) for i in range(count)]
    left_s, got_s, total_s, own_v, got_v, send_v, send_w = take(7)
    value_v, base_v, gain_sends, gain_recvs = take(4)
    rs_sems = [take(3), take(3)]
    gain_ss, gain_rs, right_sem, sem, engine_sem = take(5)

    line = TensorLine()
    engine = Engine(left_s, got_s, total_s, engine_sem)
    tensor = [
        TensorReduce(line, source, *reduces[q], own_v, got_v, (send_v, send_w)[q], *rs_sems[q])
        for q, source in enumerate((part, part_out))
    ]
    for reduce in tensor:
        reduce.start()
    loads = [copy_in(rights_hbm[i], rights[i], right_sem.at[i]) for i in range(count)]
    items = [
        Item(make_stages(n, plan[i]), lefts[lefts_of[i]], rights[i], width, readies[i], (outs[i], recv[i], sends[i], send_sems[i], recv_sems[i]))
        for i in range(count)
    ]

    def grad_end():
        copies = [copy_in(stream, value_v, sem.at[0]), copy_in(d_middle, base_v, sem.at[1])]
        for copy in copies:
            copy.wait()
        gains[...] = jnp.zeros_like(gains)

        def use(at, total):
            back, terms = norm_backward(value_v[at, :].astype(F32), gain[...], total)
            base_v[at, :] = base_v[at, :] + back
            gains[...] += fold_rows(terms)

        tensor[0].end(use)
        copy_in(base_v, stream_grad_o, sem.at[0]).wait()
        first = jnp.sum(gains[...], axis=0, keepdims=True)
        second = jnp.sum(gain_grad_two[...], axis=0, keepdims=True)
        pick = lax.broadcasted_iota(jnp.int32, gains.shape, 0)
        gains[...] = jnp.where(pick == 0, first, jnp.where(pick == 1, second, 0.0))

    def out_end():
        copy_in(middle, base_v, sem.at[0]).wait()

        def use(at, total):
            base_v[at, :] = base_v[at, :] + total

        tensor[1].end(use)
        copy_in(base_v, stream_out_o, sem.at[0]).wait()

    extra = [tensor[0].middle, tensor[1].middle, grad_end, out_end]
    extra += gather_sums(gains, gain_sends, gain_recvs, gain_ss, gain_rs)
    loaded = set()
    for i, t, k in order:
        if i < 0:
            if extra:
                extra.pop(0)()
            continue
        if i not in loaded:
            loads[i].wait()
            loaded.add(i)
        if t < len(shapes[i]):
            engine.round(items[i], t, k)
        else:
            engine.finish(items[i])
    for step in extra:
        step()
    for i, item in enumerate(items):
        engine.drain(item, range(readies[i], len(shapes[i])))
    for reduce in tensor:
        reduce.drain()


def task_order(plan, readies, names, n):
    tasks = []
    for last_first, ready in zip(plan, readies):
        sizes = digit_sizes(n)
        if last_first:
            sizes = sizes[1:] + sizes[:1]
        i = len(tasks)
        tasks.append([(i, t, k) for t, m in enumerate(sizes) for k in range(1, m) if t >= ready] + [(i, len(sizes), 0)])
    out, at = [], [0] * len(plan)
    for i in names:
        if i < 0:
            out.append((-1, 0, 0))
        elif at[i] < len(tasks[i]):
            out.append(tasks[i][at[i]])
            at[i] += 1
    for i in range(len(plan)):
        out += tasks[i][at[i] :]
    return out


def finish(part, part_out, middle, d_middle, stream, gain, gain_grad_two, lefts, lefts_of, rights, given, plan, names):
    n = lax.axis_size("dp")
    tokens, features = part.shape
    width, rows = features // n, tokens // 4
    readies = [len(g) for g in given]
    columns = [r.shape[1] for r in rights]
    widest = max(columns)
    shapes = [stage_shapes(n, last_first, width, c)[ready:] for last_first, c, ready in zip(plan, columns, readies)]
    steps = 2 + (n - 1).bit_length()
    dma = pltpu.SemaphoreType.DMA
    stream_shape = jax.ShapeDtypeStruct((rows, features), F32)
    out_shape = [stream_shape, stream_shape] + [jax.ShapeDtypeStruct((width, c), F32) for c in columns]
    out_shape += TensorReduce.results(tokens, features) * 2 + [s[0] for item in shapes for s in item]
    results = pl.pallas_call(
        functools.partial(finish_kernel, n, width, plan, task_order(plan, readies, names, n), lefts_of, readies, columns),
        out_shape=[*out_shape, jax.ShapeDtypeStruct((8, features), F32)],
        in_specs=[HBM] * 5 + [IN_VMEM] * 2 + [HBM] * (len(lefts) + len(rights) + sum(readies)),
        out_specs=[HBM] * len(out_shape) + [IN_VMEM],
        scratch_shapes=[
            *[pltpu.VMEM(r.shape, BF16) for r in rights],
            *[s[1] for item in shapes for s in item],
            *[s[2] for item in shapes for s in item],
            *[s[3] for item in shapes for s in item],
            pltpu.VMEM((tokens, width), BF16),
            pltpu.VMEM((2 * len(digit_sizes(n)), width, widest), BF16),
            pltpu.VMEM((max(s[4] for item in shapes for s in item), widest), F32),
            *TensorReduce.buffers(tokens, features),
            pltpu.VMEM((rows, features), BF16),
            pltpu.VMEM((rows, features), BF16),
            pltpu.VMEM((rows, features), F32),
            pltpu.VMEM((steps, 8, features), F32),
            pltpu.VMEM((steps, 8, features), F32),
            *TensorReduce.semaphores(),
            *TensorReduce.semaphores(),
            dma((steps,)), dma((steps,)), dma((len(rights),)), dma((2,)), dma((1 + 2 * len(digit_sizes(n)),)),
        ],
        compiler_params=pltpu.CompilerParams(vmem_limit_bytes=VMEM_BYTES, has_side_effects=True),
        cost_estimate=pl.CostEstimate(
            flops=2 * tokens * features * sum(columns), bytes_accessed=4 * features * sum(columns), transcendentals=0
        ),
        name="finish",
    )(
        part, part_out, middle, d_middle, stream, gain, gain_grad_two,
        *[column_blocks(v, n) for v in lefts], *rights, *[g for item in given for g in item],
    )
    return results[0], results[1], results[2 : 2 + len(rights)], results[-1]


class TensorGather:
    def __init__(self, line, own_v, out, send_sem, recv_sem):
        self.line, self.own_v, self.out, self.rows = line, own_v, out, own_v.shape[0]
        self.over = remote(own_v, self.block(line.index), send_sem.at[0], recv_sem.at[0], "tensor", line.peer)
        self.aside = remote(own_v, self.block(line.index), send_sem.at[1], recv_sem.at[1], "tensor", line.mate)
        self.onward = remote(self.block(line.peer), self.block(line.peer), send_sem.at[2], recv_sem.at[2], "tensor", line.mate)

    def block(self, index):
        return self.out.at[pl.ds(pl.multiple_of(index * self.rows, self.rows), self.rows)]

    def start(self):
        self.over.start()
        self.aside.start()

    def forward(self):
        self.over.wait_recv()
        self.onward.start()

    def drain(self):
        for copy in (self.over, self.aside, self.onward):
            copy.wait_send()

    @staticmethod
    def semaphores():
        return [pltpu.SemaphoreType.DMA((3,)), pltpu.SemaphoreType.DMA((3,))]


def forward_kernel(*refs):
    take = Reader(refs)
    cot_own, w_gate, w_branch, w_out = take(4)
    stream, gain, gain_two, masks, vecs, w_cat = take(6)
    normed, cot, gated_o, branch_o, conv_o, states_o, product_o, middle_o, normed_two, from_mate, from_peer = take(11)
    wg_v, wb_v, wo_v, own_v, cot_v, block_v, gated_v, branch_v, conv_v, states_v, product_v = take(11)
    pre_s, a_s, b_s, part_v, rs_own, rs_got, rs_send_v, middle_v, two_v = take(9)
    ag_sems, cot_sems, two_sems = take(2), take(2), take(2)
    rs_send, rs_recv, rs_sem, sem = take(4)
    rows, features = stream.shape
    line = TensorLine()
    gather = TensorGather(line, own_v, normed, *ag_sems)
    cots = TensorGather(line, cot_v, cot, *cot_sems)
    twos = TensorGather(line, two_v, normed_two, *two_sems)
    reduce = TensorReduce(line, part_v, from_mate, from_peer, rs_own, rs_got, rs_send_v, rs_send, rs_recv, rs_sem)
    loads = [copy_in(w_gate, wg_v, sem.at[0]), copy_in(w_branch, wb_v, sem.at[1]), copy_in(w_out, wo_v, sem.at[2])]
    cot_load = copy_in(cot_own, cot_v, sem.at[3])

    def chunks(body):
        @pl.loop(0, rows // 16)
        def _(r):
            body(pl.ds(pl.multiple_of(r * 16, 16), 16))

    def norm(values, gains):
        inverse = lax.rsqrt(jnp.mean(values * values, axis=-1, keepdims=True) + epsilon)
        return (values * inverse * gains).astype(BF16)

    def first_norm(at):
        own_v[at, :] = norm(stream[at, :].astype(F32), gain[...])

    chunks(first_norm)
    gather.start()
    keep = [copy_in(own_v, gather.block(line.index), sem.at[4])]
    cot_load.wait()
    cots.start()
    keep.append(copy_in(cot_v, cots.block(line.index), sem.at[5]))

    def project(source, index):
        at = pl.ds(pl.multiple_of(index * rows, rows), rows)
        branch_v[at, :] = jnp.dot(source, wb_v[...], preferred_element_type=F32)
        gated_v[at, :] = jnp.dot(source, wg_v[...], preferred_element_type=F32)

    loads[0].wait()
    loads[1].wait()
    project(own_v[...], line.index)
    gather.aside.wait_recv()
    copy_in(gather.block(line.mate), block_v.at[0], sem.at[6]).wait()
    project(block_v[0], line.mate)
    gather.forward()
    copy_in(gather.block(line.peer), block_v.at[1], sem.at[6]).wait()
    project(block_v[1], line.peer)
    gather.onward.wait_recv()
    copy_in(gather.block(line.cross), block_v.at[0], sem.at[6]).wait()
    project(block_v[0], line.cross)
    outs = [copy_in(branch_v, branch_o, sem.at[7]), copy_in(gated_v, gated_o, sem.at[8])]
    mixer_forward_kernel(branch_v, gated_v, masks, vecs, w_cat, conv_v, states_v, product_v, pre_s, a_s, b_s)
    outs += [copy_in(conv_v, conv_o, sem.at[9]), copy_in(states_v, states_o, sem.at[10]), copy_in(product_v, product_o, sem.at[11])]
    loads[2].wait()

    def out_block(index):
        at = pl.ds(pl.multiple_of(index * rows, rows), rows)
        part_v[at, :] = jnp.dot(product_v[at, :], wo_v[...], preferred_element_type=F32).astype(BF16)

    out_block(line.cross)
    reduce.mates[0].start()
    out_block(line.peer)
    reduce.middle()
    out_block(line.mate)
    reduce.mates[1].start()
    out_block(line.index)
    cots.forward()

    def second_norm(at, total):
        values = stream[at, :].astype(F32) + total
        middle_v[at, :] = values
        two_v[at, :] = norm(values, gain_two[...])

    reduce.end(second_norm)
    twos.start()
    keep += [copy_in(two_v, twos.block(line.index), sem.at[12]), copy_in(middle_v, middle_o, sem.at[13])]
    cots.aside.wait_recv()
    cots.onward.wait_recv()
    twos.forward()
    twos.aside.wait_recv()
    twos.onward.wait_recv()
    for copy in keep + outs:
        copy.wait()
    for gathered in (gather, cots, twos):
        gathered.drain()
    reduce.drain()


def forward(cot_own, w_gate, w_branch, w_out, stream, gain, gain_two, masks, vecs, w_cat):
    rows, features = stream.shape
    tokens, channels = 4 * rows, w_gate.shape[1]
    lanes = channels // LANES
    whole = jax.ShapeDtypeStruct((tokens, features), BF16)
    wide = jax.ShapeDtypeStruct((tokens, channels), F32)
    narrow = jax.ShapeDtypeStruct((tokens, channels), BF16)
    results = [whole, whole, wide, wide, narrow, wide, narrow, jax.ShapeDtypeStruct((rows, features), F32), whole]
    results += TensorReduce.results(tokens, features)
    block = pltpu.VMEM((rows, features), BF16)
    return pl.pallas_call(
        forward_kernel,
        out_shape=results,
        in_specs=[HBM] * 4 + [IN_VMEM] * 6,
        out_specs=[HBM] * len(results),
        scratch_shapes=[
            pltpu.VMEM(w_gate.shape, BF16), pltpu.VMEM(w_branch.shape, BF16), pltpu.VMEM(w_out.shape, BF16),
            block, block, pltpu.VMEM((2, rows, features), BF16),
            pltpu.VMEM((tokens, channels), F32), pltpu.VMEM((tokens, channels), F32),
            pltpu.VMEM((tokens, channels), BF16), pltpu.VMEM((tokens, channels), F32), pltpu.VMEM((tokens, channels), BF16),
            pltpu.VMEM((tokens, 2 * channels), F32),
            pltpu.VMEM((lanes, tokens, LANES), F32), pltpu.VMEM((lanes, tokens, LANES), F32),
            pltpu.VMEM((tokens, features), BF16), *TensorReduce.buffers(tokens, features),
            pltpu.VMEM((rows, features), F32), block,
            *TensorGather.semaphores(), *TensorGather.semaphores(), *TensorGather.semaphores(),
            *TensorReduce.semaphores(), pltpu.SemaphoreType.DMA((14,)),
        ],
        compiler_params=pltpu.CompilerParams(vmem_limit_bytes=VMEM_BYTES, has_side_effects=True),
        cost_estimate=pl.CostEstimate(flops=9 * 10**9, bytes_accessed=40 * 10**6, transcendentals=6 * tokens * channels),
        name="forward",
    )(cot_own, w_gate, w_branch, w_out, stream, gain, gain_two, masks, vecs, w_cat)

DP_PLAN = [True, False, False, False, False, False]
DP_ORDER = [2, -1, 1, 1, -1, 4, 5, 3, 1, 2, 2, -1, -1, 4, -1, 4, 0, 2, 5, -1, 1, -1, 5, 4, 3, -1, 5, 2, -1, 3, 0, 4, 3, -1, 5, 3]


def dot(left, right, dims, out=F32):
    return lax.dot_general(left, right, (dims, ((), ())), preferred_element_type=F32).astype(out)


def spread_heads(*weights):
    heads, width = weights[0].shape[:2]
    total = len(weights) * heads * width
    rows = []
    for h in range(heads):
        row = 0
        for q, weight in enumerate(weights):
            before = (q * heads + h) * width
            row = row + jnp.pad(weight[h], ((0, 0), (before, total - before - width)))
        rows.append(row)
    return jnp.concatenate(rows)


def head_blocks(dense, heads, width):
    return jnp.stack([dense[h * width : (h + 1) * width, h * width : (h + 1) * width] for h in range(heads)])


def on_device(
    stream_in, segments, first_gain, gelu_gate_weight, recurrent_branch_weight, conv_kernel, conv_bias, recur_weight, recur_bias,
    inlet_weight, inlet_bias, decay_param, recurrent_output_weight, second_gain, gate_projection_weight, up_projection_weight,
    down_projection_weight, cotangent,
):
    seq_len = segments.shape[1]
    heads, head_width = recur_weight.shape[:2]
    ids = jnp.pad(segments[0], (3, 8), constant_values=-1)
    same = [(ids[3 - k : 3 - k + seq_len] == segments[0]).astype(F32) for k in range(1, 4)]
    masks = jnp.pad(jnp.stack(same, axis=1), ((0, 8), (0, 5)))
    softplus = jax.nn.softplus(-decay_param)
    vecs = jnp.concatenate([conv_kernel, jnp.stack([conv_bias, recur_bias, inlet_bias, softplus])])
    w_cat = spread_heads(recur_weight, inlet_weight)

    normed, cot, gated_pre, branch_pre, conv_out, states, product, middle, normed_two, _, _ = forward(
        cotangent[0], gelu_gate_weight, recurrent_branch_weight, recurrent_output_weight, stream_in[0], first_gain[None],
        second_gain[None], masks, vecs, w_cat,
    )
    gate_pre = dot(normed_two, gate_projection_weight, ((1,), (0,)))
    up_pre = dot(normed_two, up_projection_weight, ((1,), (0,)))
    gate_act, gate_slope = gelu_parts(gate_pre)
    hidden = (gate_act * up_pre).astype(BF16)
    d_hidden = dot(cot, down_projection_weight, ((1,), (1,)))
    d_gate = (d_hidden * up_pre * gate_slope).astype(BF16)
    d_up = (d_hidden * gate_act).astype(BF16)
    part_two = (dot(d_gate, gate_projection_weight, ((1,), (1,))) + dot(d_up, up_projection_weight, ((1,), (1,)))).astype(BF16)
    part_out = dot(hidden, down_projection_weight, ((1,), (0,)), BF16)
    d_middle, d_attended, d_gated, d_ri, d_branch, _, _, down_got, gate_got, sums, gain_two = chain(
        part_two, middle, cotangent[0], recurrent_output_weight, gated_pre, branch_pre, states, conv_out,
        second_gain[None], masks, vecs, w_cat, cot, normed_two, hidden, d_gate,
    )
    part_one = (dot(d_gated, gelu_gate_weight, ((1,), (1,))) + dot(d_branch, recurrent_branch_weight, ((1,), (1,)))).astype(BF16)
    stream_grad, stream_out, gradients, gains = finish(
        part_one, part_out, middle, d_middle, stream_in[0], first_gain[None], gain_two,
        [cot, normed_two, d_attended, normed], [0, 1, 1, 2, 3, 3], [hidden, d_gate, d_up, product, d_gated, d_branch],
        [[down_got], [gate_got], [], [], [], []], DP_PLAN, DP_ORDER,
    )
    down_gradient, gate_gradient, up_gradient, output_gradient, gated_gradient, branch_gradient = gradients

    width = heads * head_width
    dense = dot(conv_out, d_ri, ((0,), (0,)))
    grad_recur = head_blocks(dense[:, :width], heads, head_width)
    grad_inlet = head_blocks(dense[:, width:], heads, head_width)
    sums = jnp.sum(sums, axis=1)
    small = jnp.concatenate([sums.reshape(-1), grad_recur.reshape(-1), grad_inlet.reshape(-1)])
    small = lax.psum(small, "dp")
    sums = small[: 8 * width].reshape(8, width)
    grad_recur, grad_inlet = small[8 * width :].reshape(2, heads, head_width, head_width)
    grad_decay = decay_scale * jax.nn.sigmoid(-decay_param) * sums[7]
    return (
        stream_out[None], stream_grad[None], gains[0], gated_gradient, branch_gradient, sums[:4], sums[4], grad_recur, sums[5],
        grad_inlet, sums[6], grad_decay, output_gradient.T, gains[1], gate_gradient, up_gradient, down_gradient.T,
    )


def solution(mesh):
    in_specs = (
        P("dp", "tensor", None),
        P("dp", None),
        P(),
        P(None, "tensor"),
        P(None, "tensor"),
        P(None, "tensor"),
        P("tensor"),
        P("tensor", None, None),
        P("tensor"),
        P("tensor", None, None),
        P("tensor"),
        P("tensor"),
        P("tensor", None),
        P(),
        P(None, "tensor"),
        P(None, "tensor"),
        P("tensor", None),
        P("dp", "tensor", None),
    )
    out_specs = (
        P("dp", "tensor", None),
        P("dp", "tensor", None),
        P(),
        P("dp", "tensor"),
        P("dp", "tensor"),
        P(None, "tensor"),
        P("tensor"),
        P("tensor", None, None),
        P("tensor"),
        P("tensor", None, None),
        P("tensor"),
        P("tensor"),
        P("tensor", "dp"),
        P(),
        P("dp", "tensor"),
        P("dp", "tensor"),
        P("tensor", "dp"),
    )
    return jax.shard_map(
        on_device, mesh=mesh, in_specs=in_specs, out_specs=out_specs, check_vma=False
    )
```

```python
import functools

import jax
import jax.numpy as jnp
from jax import lax
from jax.experimental import pallas as pl
from jax.experimental.pallas import tpu as pltpu
from jax.sharding import PartitionSpec as P

epsilon = 1e-06
decay_scale = 8.0
LANES = 128
GELU_C = 0.7978845608028654
GELU_K = 0.044715
F32 = jnp.float32
BF16 = jnp.bfloat16
VMEM_BYTES = 60 * 1024 * 1024


def minus_expm1(y, exp_y):
    s = 1.0 + y * (1.0 / 9.0)
    for d in range(8, 1, -1):
        s = 1.0 + (y * (1.0 / d)) * s
    return jnp.where(y > -0.5, -y * s, 1.0 - exp_y)


def gelu_parts(v):
    v2 = v * v
    t = jnp.tanh(GELU_C * v * (1.0 + GELU_K * v2))
    half = 0.5 * (1.0 + t)
    slope = half + 0.5 * v * (1.0 - t * t) * (GELU_C * (1.0 + 3.0 * GELU_K * v2))
    return v * half, slope


def lane_tiles(width):
    return [slice(j * LANES, (j + 1) * LANES) for j in range(width // LANES)]


def fold_rows(v):
    return jnp.sum(v.reshape(v.shape[0] // 8, 8, v.shape[1]), axis=0)


def gates_pre(rows, step, conv_ref, w_ref, pre_s):
    @pl.loop(0, rows // step)
    def _(i):
        r = pl.ds(pl.multiple_of(i * step, step), step)
        pre_s[r, :] = jnp.dot(conv_ref[r, :], w_ref[...], preferred_element_type=F32)


def mixer_forward_kernel(branch_ref, gated_ref, mask_ref, vec_ref, w_ref, conv_ref, states_ref, product_ref, pre_s, a_s, b_s):
    rows, width = branch_ref.shape
    seg = rows // 8
    tiles = lane_tiles(width)

    @pl.loop(0, 8)
    def _(s):
        t0 = pl.multiple_of(s * seg, seg)
        before = pl.multiple_of(jnp.maximum(t0 - 8, 0), 8)
        same = [mask_ref[pl.ds(t0, seg), k : k + 1] for k in range(3)]
        for cols in tiles:
            b = branch_ref[pl.ds(t0, seg), cols]
            ext = jnp.concatenate([branch_ref[pl.ds(before, 8), cols], b], axis=0)
            out = vec_ref[4:5, cols] + vec_ref[0:1, cols] * b
            for k in range(1, 4):
                out = out + vec_ref[k : k + 1, cols] * pltpu.roll(ext, k, 0)[8:] * same[k - 1]
            conv_ref[pl.ds(t0, seg), cols] = out.astype(BF16)

    gates_pre(rows, 256, conv_ref, w_ref, pre_s)

    @pl.loop(0, 8)
    def _(s):
        t0 = pl.multiple_of(s * seg, seg)
        c = mask_ref[pl.ds(t0, seg), 0:1]
        for j, cols in enumerate(tiles):
            cols_i = slice(width + j * LANES, width + (j + 1) * LANES)
            r = jax.nn.sigmoid(pre_s[pl.ds(t0, seg), cols] + vec_ref[5:6, cols])
            i = jax.nn.sigmoid(pre_s[pl.ds(t0, seg), cols_i] + vec_ref[6:7, cols])
            log_a = (-decay_scale * vec_ref[7:8, cols]) * r
            a = jnp.exp(log_a)
            n = jnp.sqrt(minus_expm1(2.0 * log_a, a * a))
            mult = (1.0 - c) + c * n
            a_s[j, pl.ds(t0, seg), :] = a * c
            b_s[j, pl.ds(t0, seg), :] = mult * i * conv_ref[pl.ds(t0, seg), cols].astype(F32)

    def scan_step(i, carry):
        out = []
        for j in range(len(tiles)):
            h, p = carry[j]
            at = pl.ds(i, 8, stride=seg)
            a = a_s[j, at, :]
            h = a * h + b_s[j, at, :]
            p = a * p
            b_s[j, at, :] = h
            a_s[j, at, :] = p
            out.append((h, p))
        return tuple(out)

    one = jnp.ones((8, LANES), F32)
    lax.fori_loop(0, seg, scan_step, tuple((jnp.zeros((8, LANES), F32), one) for _ in tiles), unroll=4)

    def finish(s, carry):
        t0 = pl.multiple_of(s * seg, seg)
        out = []
        for j, cols in enumerate(tiles):
            st = b_s[j, pl.ds(t0, seg), :] + a_s[j, pl.ds(t0, seg), :] * carry[j]
            states_ref[pl.ds(t0, seg), cols] = st
            act, _ = gelu_parts(gated_ref[pl.ds(t0, seg), cols])
            product_ref[pl.ds(t0, seg), cols] = (st * act).astype(BF16)
            out.append(st[seg - 1 : seg, :])
        return tuple(out)

    lax.fori_loop(0, 8, finish, tuple(jnp.zeros((1, LANES), F32) for _ in tiles))


class MixerBackward:
    def __init__(self, masks, vecs, w_cat, states, branch, conv, dgated, dri, dbranch, sums, pre_s, a_s, n_s, ac_s, e_s, p_s):
        self.masks, self.vecs, self.w_cat, self.states, self.branch, self.conv = masks, vecs, w_cat, states, branch, conv
        self.dgated, self.dri, self.dbranch, self.sums = dgated, dri, dbranch, sums
        self.pre_s, self.a_s, self.n_s, self.ac_s, self.e_s, self.p_s = pre_s, a_s, n_s, ac_s, e_s, p_s
        self.rows, self.width = states.shape
        self.seg = self.rows // 8
        self.tiles = lane_tiles(self.width)

    @staticmethod
    def scratch(rows, width):
        lanes = width // LANES
        return [
            pltpu.VMEM((rows, 2 * width), F32),
            pltpu.VMEM((rows, width), F32),
            pltpu.VMEM((rows + 8, width), F32),
            pltpu.VMEM((lanes, rows + 8, LANES), F32),
            pltpu.VMEM((lanes, rows, LANES), F32),
            pltpu.VMEM((lanes, rows, LANES), F32),
        ]

    def gates(self):
        self.sums[...] = jnp.zeros_like(self.sums)
        gates_pre(self.rows, 256, self.conv, self.w_cat, self.pre_s)

    def factors(self, gated):
        @pl.loop(0, 8)
        def _(s):
            t0 = pl.multiple_of(s * self.seg, self.seg)
            at = pl.ds(t0, self.seg)
            c = self.masks[at, 0:1]
            for j, cols in enumerate(self.tiles):
                cols_i = slice(self.width + j * LANES, self.width + (j + 1) * LANES)
                r = jax.nn.sigmoid(self.pre_s[at, cols] + self.vecs[5:6, cols])
                self.pre_s[at, cols] = r
                self.pre_s[at, cols_i] = jax.nn.sigmoid(self.pre_s[at, cols_i] + self.vecs[6:7, cols])
                log_a = (-decay_scale * self.vecs[7:8, cols]) * r
                a = jnp.exp(log_a)
                d = self.a_s[at, cols]
                self.a_s[at, cols] = a
                self.n_s[at, cols] = jnp.sqrt(minus_expm1(2.0 * log_a, a * a))
                self.ac_s[j, at, :] = a * c
                act, slope = gelu_parts(gated[at, cols])
                self.e_s[j, at, :] = d * act
                self.dgated[at, cols] = (d * self.states[at, cols] * slope).astype(BF16)

    def scan(self):
        seg, lanes = self.seg, len(self.tiles)
        for j in range(lanes):
            self.ac_s[j, self.rows : self.rows + 8, :] = jnp.zeros((8, LANES), F32)

        def step(q, carry):
            i = seg - 1 - q
            out = []
            for j in range(lanes):
                e, p = carry[j]
                at = pl.ds(i, 8, stride=seg)
                a = self.ac_s[j, pl.ds(i + 1, 8, stride=seg), :]
                e = a * e + self.e_s[j, at, :]
                p = a * p
                self.e_s[j, at, :] = e
                self.p_s[j, at, :] = p
                out.append((e, p))
            return tuple(out)

        one = jnp.ones((8, LANES), F32)
        lax.fori_loop(0, seg, step, tuple((jnp.zeros((8, LANES), F32), one) for _ in self.tiles), unroll=4)

    def gate_gradients(self):
        seg, width = self.seg, self.width

        def finish(q, carry):
            s = 7 - q
            t0 = pl.multiple_of(s * seg, seg)
            at = pl.ds(t0, seg)
            before = pl.multiple_of(jnp.maximum(t0 - 8, 0), 8)
            c = self.masks[at, 0:1]
            out = []
            for j, cols in enumerate(self.tiles):
                cols_i = slice(width + j * LANES, width + (j + 1) * LANES)
                e = self.e_s[j, at, :] + self.p_s[j, at, :] * carry[j]
                out.append(e[0:1, :])
                ext = jnp.concatenate([self.states[pl.ds(before, 8), cols], self.states[at, cols]], axis=0)
                earlier = pltpu.roll(ext, 1, 0)[8:]
                r, i, a, n = self.pre_s[at, cols], self.pre_s[at, cols_i], self.a_s[at, cols], self.n_s[at, cols]
                cv = self.conv[at, cols].astype(F32)
                ec = e * c
                d_log = a * (ec * earlier) - ec * i * cv * (a * a / n)
                rr = d_log * r
                dr = ((-decay_scale * self.vecs[7:8, cols]) * rr * (1.0 - r)).astype(BF16)
                em = e * ((1.0 - c) + c * n) * i
                di = (em * cv * (1.0 - i)).astype(BF16)
                self.dri[at, cols] = dr
                self.dri[at, cols_i] = di
                self.n_s[at, cols] = em
                self.sums[5, :, cols] += fold_rows(dr.astype(F32))
                self.sums[6, :, cols] += fold_rows(di.astype(F32))
                self.sums[7, :, cols] += fold_rows(rr)
            return tuple(out)

        lax.fori_loop(0, 8, finish, tuple(jnp.zeros((1, LANES), F32) for _ in self.tiles))

        @pl.loop(0, self.rows // 256)
        def _(i):
            at = pl.ds(pl.multiple_of(i * 256, 256), 256)
            self.n_s[at, :] += dot_nt(self.dri[at, :], self.w_cat[...])

        self.n_s[self.rows : self.rows + 8, :] = jnp.zeros((8, width), F32)

    def convolution(self):
        @pl.loop(0, 8)
        def _(s):
            t0 = pl.multiple_of(s * self.seg, self.seg)
            at, ext = pl.ds(t0, self.seg), pl.ds(t0, self.seg + 8)
            same = [self.masks[ext, k : k + 1] for k in range(3)]
            for cols in self.tiles:
                d = self.n_s[ext, cols]
                b = self.branch[at, cols]
                self.sums[4, :, cols] += fold_rows(d[: self.seg])
                self.sums[0, :, cols] += fold_rows(d[: self.seg] * b)
                total = self.vecs[0:1, cols] * d[: self.seg]
                for k in range(1, 4):
                    moved = pltpu.roll(d * same[k - 1], self.seg + 8 - k, 0)[: self.seg]
                    total = total + self.vecs[k : k + 1, cols] * moved
                    self.sums[k, :, cols] += fold_rows(moved * b)
                self.dbranch[at, cols] = total.astype(BF16)


def dot_nt(left, right):
    return lax.dot_general(left, right, (((1,), (1,)), ((), ())), preferred_element_type=F32)


class Stage:
    def __init__(self, stride, size, later):
        self.stride, self.size, self.later = stride, size, later
        self.blocks = 1
        for s in later:
            self.blocks *= s.size
        self.digit = lax.rem(lax.axis_index("dp") // stride, size)

    def offset(self, position):
        total = 0
        for s in reversed(self.later):
            total = total + lax.rem(position, s.size) * s.stride
            position = position // s.size
        return total


def digit_sizes(n):
    if n == 8:
        return [2, 4]
    sizes = []
    while n > 1:
        m = 4 if n % 4 == 0 else 2 if n % 2 == 0 else n
        sizes.append(m)
        n //= m
    return sizes


def make_stages(n, last_first):
    digits, stride = [], 1
    for m in digit_sizes(n):
        digits.append((stride, m))
        stride *= m
    if last_first:
        digits = digits[1:] + digits[:1]
    stages = []
    for stride, m in reversed(digits):
        stages.insert(0, Stage(stride, m, list(stages)))
    return stages


class Item:
    def __init__(self, stages, left, right, width, ready, refs):
        self.stages, self.left, self.right, self.width, self.ready = stages, left, right, width, ready
        self.columns = right.shape[1]
        self.out, self.recv, self.send, self.send_sem, self.recv_sem = refs

    def message(self, t, back, k, slot, rows=None):
        stage = self.stages[t]
        rows = pl.ds(0, stage.blocks * self.width) if rows is None else rows
        step = jnp.where(back, -stage.stride, stage.stride)
        return pltpu.make_async_remote_copy(
            src_ref=self.send[t].at[slot, rows],
            dst_ref=self.recv[t].at[back, k - 1, rows],
            send_sem=self.send_sem[t].at[slot],
            recv_sem=self.recv_sem[t].at[back, k - 1],
            device_id={"dp": lax.axis_index("dp") + step},
            device_id_type=pl.DeviceIdType.MESH,
        )


class Engine:
    def __init__(self, left_s, got_s, total_s, sem):
        self.left_s, self.got_s, self.total_s, self.sem = left_s, got_s, total_s, sem

    def product(self, item, block, store):
        if len(item.left.shape) == 3:
            source = item.left.at[block]
        else:
            source = item.left.at[:, pl.ds(pl.multiple_of(block * item.width, item.width), item.width)]
        fetch = pltpu.make_async_copy(source, self.left_s, self.sem.at[0])
        fetch.start()
        fetch.wait()
        tile = 512 if item.columns % 512 == 0 else item.columns
        for c in range(item.columns // tile):
            cols = pl.ds(c * tile, tile)
            store(cols, lax.dot_general(self.left_s[...], item.right[:, cols], (((0,), (0,)), ((), ())), preferred_element_type=F32))

    def add_gots(self, item, rows, gots, store):
        copies = []
        for i, (condition, source) in enumerate(gots):
            copy = pltpu.make_async_copy(source, self.got_s.at[i, :, pl.ds(0, item.columns)], self.sem.at[1 + i])
            copies.append(copy)

            @pl.when(condition)
            def _(copy=copy):
                copy.start()

        for (condition, _), copy in zip(gots, copies):

            @pl.when(condition)
            def _(copy=copy):
                copy.wait()

        @pl.loop(0, item.width // 16)
        def _(r):
            at = pl.ds(pl.multiple_of(r * 16, 16), 16)
            here = pl.ds(pl.multiple_of(rows + r * 16, 16), 16)
            total = self.total_s[here, pl.ds(0, item.columns)]
            for i, (condition, _) in enumerate(gots):
                total = total + jnp.where(condition, self.got_s[i, at, pl.ds(0, item.columns)].astype(F32), 0.0)
            store(here, total)

    def arrived(self, item, t, position):
        found = []
        for u in range(t):
            stage = item.stages[u]
            spot = position
            rows = None
            scale = 1
            for s in item.stages[t:]:
                scale *= s.size
            lead = 0
            for s in item.stages[u + 1 : t]:
                lead = lead * s.size + s.digit
            rows = pl.ds((lead * scale + spot) * item.width, item.width)
            last = stage.size - 2
            if stage.size == 2:
                back = jnp.where(stage.digit == 0, 1, 0)
                found.append((stage.digit >= 0, item.recv[u].at[back, last, rows]))
            else:
                found.append((stage.digit >= 1, item.recv[u].at[0, last, rows]))
                found.append((stage.digit <= stage.size - 2, item.recv[u].at[1, last, rows]))
        return found

    def own_base(self, item, t):
        base = 0
        for s in item.stages[:t]:
            base = base + s.digit * s.stride
        return base

    def wait_last(self, item, t):
        if t < item.ready:
            return
        stage = item.stages[t]
        for back in range(2):
            me = stage.digit if back == 0 else stage.size - 1 - stage.digit

            @pl.when(me >= 1)
            def _(back=back):
                item.message(t, back, stage.size - 1, 0).wait_recv()

    def round(self, item, t, k):
        stage = item.stages[t]
        base = self.own_base(item, t)
        alone = t == 0 and k == 1

        @pl.loop(0, 2)
        def _(back):
            me = jnp.where(back == 0, stage.digit, stage.size - 1 - stage.digit)
            there = me + stage.size - k
            value = jnp.where(back == 0, there, stage.size - 1 - there)
            slot = jnp.where(value > stage.digit, value - 1, value)

            @pl.when(me <= k - 1)
            def _():
                @pl.loop(0, stage.blocks)
                def _(p):
                    at = pl.ds(pl.multiple_of(p * item.width, item.width), item.width)

                    def store(cols, total):
                        if alone:
                            item.send[t][slot, at, cols] = total.astype(BF16)
                        else:
                            self.total_s[at, cols] = total

                    self.product(item, base + value * stage.stride + stage.offset(p), store)
                    if alone:
                        item.message(t, back, k, slot, at).start()

            if k == 1 and t > 0:

                @pl.when(back == 0)
                def _():
                    self.wait_last(item, t - 1)

            if not alone:

                @pl.when(me <= k - 1)
                def _():
                    if k > 1:

                        @pl.when(me >= 1)
                        def _():
                            item.message(t, back, k - 1, 0).wait_recv()

                    @pl.loop(0, stage.blocks)
                    def _(p):
                        rows = pl.multiple_of(p * item.width, item.width)
                        at = pl.ds(rows, item.width)
                        gots = self.arrived(item, t, value * stage.blocks + p)
                        if k > 1:
                            gots.append((me >= 1, item.recv[t].at[back, k - 2, at]))

                        def store(here, total):
                            item.send[t][slot, here, :] = total.astype(BF16)

                        self.add_gots(item, rows, gots, store)
                        item.message(t, back, k, slot, at).start()

    def finish(self, item):
        t = len(item.stages)

        def store(cols, total):
            self.total_s[pl.ds(0, item.width), cols] = total

        self.product(item, self.own_base(item, t), store)
        self.wait_last(item, t - 1)

        def store_sum(here, total):
            self.total_s[here, pl.ds(0, item.columns)] = total

        self.add_gots(item, 0, self.arrived(item, t, 0), store_sum)
        copy = pltpu.make_async_copy(self.total_s.at[pl.ds(0, item.width), pl.ds(0, item.columns)], item.out, self.sem.at[0])
        copy.start()
        copy.wait()

    def drain(self, item, stages):
        for t in stages:
            for slot in range(item.stages[t].size - 1):
                item.message(t, 0, 1, slot).wait_send()


def stage_shapes(n, last_first, width, columns):
    sizes = digit_sizes(n)
    if last_first:
        sizes = sizes[1:] + sizes[:1]
    left, found = n, []
    for t, m in enumerate(sizes):
        left //= m
        found.append(
            (
                jax.ShapeDtypeStruct((2, m - 1, left * width, columns), BF16),
                pltpu.VMEM((m - 1, left * width, columns), BF16),
                pltpu.SemaphoreType.DMA((m - 1,)),
                pltpu.SemaphoreType.DMA((2, m - 1)),
                left * width if t > 0 or m > 2 else width,
            )
        )
    return found


class Reader:
    def __init__(self, refs):
        self.refs, self.at = refs, 0

    def __call__(self, count=None):
        start = self.at
        self.at += 1 if count is None else count
        return self.refs[start] if count is None else list(self.refs[start : self.at])


def column_blocks(left, n):
    tokens, features = left.shape
    width = features // n
    return left.reshape(tokens, n, width).transpose(1, 0, 2) if width % LANES else left


class TensorLine:
    def __init__(self):
        self.index = lax.axis_index("tensor")
        self.mate, self.peer, self.cross = self.index ^ 1, self.index ^ 2, self.index ^ 3


def copy_in(source, target, sem):
    copy = pltpu.make_async_copy(source, target, sem)
    copy.start()
    return copy


def remote(source, target, send_sem, recv_sem, axis, index):
    return pltpu.make_async_remote_copy(
        src_ref=source, dst_ref=target, send_sem=send_sem, recv_sem=recv_sem,
        device_id={axis: index}, device_id_type=pl.DeviceIdType.MESH,
    )


class TensorReduce:
    def __init__(self, line, part, from_mate, from_peer, own_v, got_v, send_v, send_sem, recv_sem, sem):
        self.line, self.part, self.from_mate, self.from_peer = line, part, from_mate, from_peer
        self.own_v, self.got_v, self.send_v, self.sem = own_v, got_v, send_v, sem
        self.rows = part.shape[0] // 4
        self.mates = [
            remote(self.block(line.cross), from_mate.at[0], send_sem.at[0], recv_sem.at[0], "tensor", line.mate),
            remote(self.block(line.mate), from_mate.at[1], send_sem.at[1], recv_sem.at[1], "tensor", line.mate),
        ]
        self.over = remote(send_v, from_peer, send_sem.at[2], recv_sem.at[2], "tensor", line.peer)

    def block(self, index):
        return self.part.at[pl.ds(pl.multiple_of(index * self.rows, self.rows), self.rows)]

    def start(self):
        for copy in self.mates:
            copy.start()

    def middle(self):
        own = copy_in(self.block(self.line.peer), self.own_v, self.sem.at[0])
        self.mates[0].wait_recv()
        got = copy_in(self.from_mate.at[0], self.got_v.at[0], self.sem.at[1])
        own.wait()
        got.wait()

        @pl.loop(0, self.rows // 16)
        def _(r):
            at = pl.ds(pl.multiple_of(r * 16, 16), 16)
            self.send_v[at, :] = (self.own_v[at, :].astype(F32) + self.got_v[0, at, :].astype(F32)).astype(BF16)

        self.over.start()

    def end(self, use):
        own = copy_in(self.block(self.line.index), self.own_v, self.sem.at[0])
        self.mates[1].wait_recv()
        got = copy_in(self.from_mate.at[1], self.got_v.at[0], self.sem.at[1])
        self.over.wait_recv()
        over = copy_in(self.from_peer, self.got_v.at[1], self.sem.at[2])
        own.wait()
        got.wait()
        over.wait()

        @pl.loop(0, self.rows // 16)
        def _(r):
            at = pl.ds(pl.multiple_of(r * 16, 16), 16)
            use(at, self.own_v[at, :].astype(F32) + self.got_v[0, at, :].astype(F32) + self.got_v[1, at, :].astype(F32))

    def drain(self):
        for copy in self.mates:
            copy.wait_send()
        self.over.wait_send()

    @staticmethod
    def results(tokens, features):
        return [jax.ShapeDtypeStruct((2, tokens // 4, features), BF16), jax.ShapeDtypeStruct((tokens // 4, features), BF16)]

    @staticmethod
    def semaphores():
        return [pltpu.SemaphoreType.DMA((3,)), pltpu.SemaphoreType.DMA((3,)), pltpu.SemaphoreType.DMA((3,))]

    @staticmethod
    def buffers(tokens, features):
        rows = tokens // 4
        return [pltpu.VMEM((rows, features), BF16), pltpu.VMEM((2, rows, features), BF16), pltpu.VMEM((rows, features), BF16)]


def norm_backward(values, gain, d_normed):
    inverse = lax.rsqrt(jnp.mean(values * values, axis=-1, keepdims=True) + epsilon)
    weighted = gain * d_normed
    inner = jnp.mean(weighted * values, axis=-1, keepdims=True)
    return inverse * weighted - values * (inverse * inverse * inverse * inner), d_normed * values * inverse


HBM = pl.BlockSpec(memory_space=pl.ANY)
IN_VMEM = pl.BlockSpec(memory_space=pltpu.VMEM)


def middle_kernel(n, width, *refs):
    take = Reader(refs)
    middle, cot, normed_two, w_gate, w_up, w_down, w_out, gated, branch, states, conv = take(11)
    left_down, left_gate = take(2)
    gain, masks, vecs, w_cat = take(4)
    d_middle, att, hidden_o, dgate_o, dup_o, dgated_o, dri_o, dbranch_o, part, part_out, from_mate, from_peer = take(12)
    down_recv, gate_recv, up_recv = take(3)
    sums, gain_grad = take(2)
    hidden, down_send, down_ss, down_rs, gate_send, gate_ss, gate_rs, up_send, up_ss, up_rs = take(10)
    left_s, got_s, total_s, rs_send, rs_recv, rs_sem, ag_send, ag_recv, sem, engine_sem = take(10)
    tokens, features = cot.shape
    rows, channels, units = tokens // 4, conv.shape[1], hidden.shape[1]
    tile = 512
    line = TensorLine()
    engine = Engine(left_s, got_s, total_s, engine_sem)
    down = Item(make_stages(n, True), left_down, hidden, width, 0, (None, [down_recv], [down_send], [down_ss], [down_rs]))

    def rounds(item):
        return list(range(1, item.stages[0].size))

    def row_block(ref, index):
        return ref.at[pl.ds(pl.multiple_of(index * rows, rows), rows)]

    first, between, last = rounds(down)[:1], rounds(down)[1:-1], rounds(down)[1:][-1:]
    gate = Item(make_stages(n, False), left_gate, hidden, width, 0, (None, [gate_recv], [gate_send], [gate_ss], [gate_rs]))
    half = hidden.at[:, pl.ds(0, units // 2)]
    up = Item(make_stages(n, False), left_gate, half, width, 0, (None, [up_recv], [up_send], [up_ss], [up_rs]))

    def tensor_phase(wg_v, wu_v, wd_v, dgate, dup, x_v, c_v, stage_v, own_v, got_v, send_v, dmid_v, cot_v, att_v):
        gate.right, up.right = dgate, dup.at[:, pl.ds(0, units // 2)]
        weights = [copy_in(w_gate, wg_v, sem.at[0]), copy_in(w_up, wu_v, sem.at[1]), copy_in(w_down, wd_v, sem.at[2])]
        loads = [copy_in(middle, dmid_v, sem.at[3]), copy_in(row_block(cot, line.index), cot_v, sem.at[4])]
        copy_in(row_block(normed_two, 0), x_v, sem.at[5])
        copy_in(row_block(cot, 0), c_v, sem.at[6])
        for load in weights:
            load.wait()

        @pl.loop(0, 4)
        def _(b):
            at = pl.ds(pl.multiple_of(b * rows, rows), rows)
            pltpu.make_async_copy(row_block(normed_two, b), x_v, sem.at[5]).wait()
            pltpu.make_async_copy(row_block(cot, b), c_v, sem.at[6]).wait()

            @pl.loop(0, units // tile)
            def _(j):
                cols = pl.ds(pl.multiple_of(j * tile, tile), tile)
                gate_pre = jnp.dot(x_v[...], wg_v[:, cols], preferred_element_type=F32)
                up_pre = jnp.dot(x_v[...], wu_v[:, cols], preferred_element_type=F32)
                d_hidden = dot_nt(c_v[...], wd_v[cols, :])
                act, slope = gelu_parts(gate_pre)
                hidden[at, cols] = (act * up_pre).astype(BF16)
                dgate[at, cols] = (d_hidden * up_pre * slope).astype(BF16)
                dup[at, cols] = (d_hidden * act).astype(BF16)

            @pl.when(b < 3)
            def _():
                copy_in(row_block(normed_two, b + 1), x_v, sem.at[5])
                copy_in(row_block(cot, b + 1), c_v, sem.at[6])

        outs = [copy_in(hidden, hidden_o, sem.at[0]), copy_in(dgate, dgate_o, sem.at[1]), copy_in(dup, dup_o, sem.at[2])]
        for k in first:
            engine.round(down, 0, k)

        def stage(index, target, value):
            @pl.loop(0, features // tile)
            def _(j):
                cols = pl.ds(pl.multiple_of(j * tile, tile), tile)
                stage_v[:, cols] = value(pl.ds(pl.multiple_of(index * rows, rows), rows), cols).astype(BF16)

            copy_in(stage_v, row_block(target, index), sem.at[7]).wait()

        def two(at, cols):
            return dot_nt(dgate[at, :], wg_v[cols, :]) + dot_nt(dup[at, :], wu_v[cols, :])

        def out(at, cols):
            return jnp.dot(hidden[at, :], wd_v[:, cols], preferred_element_type=F32)

        reduce = TensorReduce(line, part, from_mate, from_peer, own_v, got_v, send_v, rs_send, rs_recv, rs_sem)
        stage(line.cross, part, two)
        reduce.mates[0].start()
        stage(line.peer, part, two)
        reduce.middle()
        for k in rounds(gate):
            engine.round(gate, 0, k)
        stage(line.mate, part, two)
        reduce.mates[1].start()
        stage(line.index, part, two)
        for load in loads:
            load.wait()
        gain_grad[...] = jnp.zeros_like(gain_grad)

        def use(at, total):
            back, terms = norm_backward(dmid_v[at, :], gain[...], total)
            value = cot_v[at, :].astype(F32) + back
            dmid_v[at, :] = value
            att_v[at, :] = value.astype(BF16)
            gain_grad[...] += fold_rows(terms)

        reduce.end(use)
        gather = TensorGather(line, att_v, att, ag_send, ag_recv)
        gather.start()
        keep = [copy_in(att_v, gather.block(line.index), sem.at[3]), copy_in(dmid_v, d_middle, sem.at[4])]
        for k in rounds(up):
            engine.round(up, 0, k)
        for k in between:
            engine.round(down, 0, k)
        for b in range(2):
            stage(b, part_out, out)
        gather.forward()
        for b in range(2, 4):
            stage(b, part_out, out)
        gather.aside.wait_recv()
        gather.onward.wait_recv()
        for copy in outs + keep:
            copy.wait()
        gather.drain()
        reduce.drain()

    weight = pltpu.VMEM((features, units), BF16)
    block = pltpu.VMEM((rows, features), BF16)
    pl.run_scoped(
        tensor_phase,
        weight, weight, pltpu.VMEM((units, features), BF16),
        pltpu.VMEM((tokens, units), BF16), pltpu.VMEM((tokens, units), BF16),
        block, block, block,
        *TensorReduce.buffers(tokens, features),
        pltpu.VMEM((rows, features), F32), block, block,
    )

    def mixer_phase(gated_v, states_v, conv_v, dgated_v, dri_v, dbranch_v, att_v, w_v, *scratch):
        w_load = copy_in(w_out, w_v, sem.at[0])
        blocks = [copy_in(row_block(att, 0), att_v.at[0], sem.at[4])]
        loads = [copy_in(conv, conv_v, sem.at[1]), copy_in(gated, gated_v, sem.at[2]), copy_in(states, states_v, sem.at[3])]
        mixer = MixerBackward(masks, vecs, w_cat, states_v, gated_v, conv_v, dgated_v, dri_v, dbranch_v, sums, *scratch)
        w_load.wait()
        for b in range(4):
            blocks[b].wait()
            if b < 3:
                blocks.append(copy_in(row_block(att, b + 1), att_v.at[(b + 1) % 2], sem.at[4 + (b + 1) % 2]))
            mixer.a_s[pl.ds(b * rows, rows), :] = dot_nt(att_v[b % 2], w_v[...])
        loads[0].wait()
        mixer.gates()
        loads[1].wait()
        loads[2].wait()
        mixer.factors(gated_v)
        again = copy_in(branch, gated_v, sem.at[2])
        outs = [copy_in(dgated_v, dgated_o, sem.at[1])]
        for k in last:
            engine.round(down, 0, k)
        mixer.scan()
        mixer.gate_gradients()
        outs.append(copy_in(dri_v, dri_o, sem.at[3]))
        again.wait()
        mixer.convolution()
        outs.append(copy_in(dbranch_v, dbranch_o, sem.at[0]))
        for copy in outs:
            copy.wait()

    pl.run_scoped(
        mixer_phase,
        pltpu.VMEM((tokens, channels), F32),
        pltpu.VMEM((tokens, channels), F32),
        pltpu.VMEM((tokens, channels), BF16),
        pltpu.VMEM((tokens, channels), BF16),
        pltpu.VMEM((tokens, 2 * channels), BF16),
        pltpu.VMEM((tokens, channels), BF16),
        pltpu.VMEM((2, rows, features), BF16),
        pltpu.VMEM((channels, features), BF16),
        *MixerBackward.scratch(tokens, channels),
    )
    for item in (down, gate, up):
        engine.drain(item, [0])
        engine.wait_last(item, 0)


def middle_part(middle, cot, normed_two, w_gate, w_up, w_down, w_out, gated_pre, branch_pre, states, conv_out, gain, masks, vecs, w_cat):
    n = lax.axis_size("dp")
    tokens, features = cot.shape
    channels, units, width = conv_out.shape[1], w_gate.shape[1], features // n
    rows = tokens // 4
    down = stage_shapes(n, True, width, units)[0]
    gate = stage_shapes(n, False, width, units)[0]
    up = stage_shapes(n, False, width, units // 2)[0]
    tall = max(down[4], gate[4])
    dma = pltpu.SemaphoreType.DMA
    whole = jax.ShapeDtypeStruct((tokens, features), BF16)
    hide = jax.ShapeDtypeStruct((tokens, units), BF16)
    narrow = jax.ShapeDtypeStruct((tokens, channels), BF16)
    results = [jax.ShapeDtypeStruct((rows, features), F32), whole, hide, hide, hide, narrow]
    results += [jax.ShapeDtypeStruct((tokens, 2 * channels), BF16), narrow, whole, whole, *TensorReduce.results(tokens, features)]
    results += [down[0], gate[0], up[0]]
    return pl.pallas_call(
        functools.partial(middle_kernel, n, width),
        out_shape=[*results, jax.ShapeDtypeStruct((8, 8, channels), F32), jax.ShapeDtypeStruct((8, features), F32)],
        in_specs=[HBM] * 13 + [IN_VMEM] * 4,
        out_specs=[HBM] * len(results) + [IN_VMEM] * 2,
        scratch_shapes=[
            pltpu.VMEM((tokens, units), BF16), *down[1:4], *gate[1:4], *up[1:4],
            pltpu.VMEM((tokens, width), BF16),
            pltpu.VMEM((1, width, units), BF16),
            pltpu.VMEM((tall, units), F32),
            *TensorReduce.semaphores(), *TensorGather.semaphores(), dma((8,)), dma((2,)),
        ],
        compiler_params=pltpu.CompilerParams(vmem_limit_bytes=VMEM_BYTES, has_side_effects=True),
        cost_estimate=pl.CostEstimate(flops=50 * 10**9, bytes_accessed=90 * 10**6, transcendentals=8 * tokens * channels),
        name="middle_part",
    )(
        middle, cot, normed_two, w_gate, w_up, w_down, w_out, gated_pre, branch_pre, states, conv_out,
        column_blocks(cot, n), column_blocks(normed_two, n), gain, masks, vecs, w_cat,
    )


def gather_sums(gains, sends, recvs, send_sems, recv_sems):
    n, line = lax.axis_size("dp"), TensorLine()
    hops = [("tensor", line.mate), ("tensor", line.peer)]
    bit = 1
    while bit < n:
        hops.append(("dp", lax.axis_index("dp") ^ bit))
        bit *= 2
    copies = [remote(sends.at[s], recvs.at[s], send_sems.at[s], recv_sems.at[s], *hop) for s, hop in enumerate(hops)]

    def begin(s):
        sends[s] = gains[...] if s == 0 else sends[s - 1] + recvs[s - 1]
        copies[s].start()

    def step(s):
        if s > 0:
            copies[s - 1].wait_recv()
        if s < len(copies):
            begin(s)
        else:
            gains[...] = sends[s - 1] + recvs[s - 1]
            for copy in copies:
                copy.wait_send()

    return [functools.partial(step, s) for s in range(len(copies) + 1)]


def finish_kernel(n, width, plan, order, lefts_of, readies, columns, out_of, *refs):
    take = Reader(refs)
    count, n_outs = len(plan), max(o for o, _ in out_of) + 1
    part_out, middle, d_middle, stream, w_gate, w_branch = take(6)
    gain, gain_grad_two = take(2)
    lefts, rights_hbm = take(max(lefts_of) + 1), take(n_outs)
    shapes = [stage_shapes(n, plan[i], width, columns[i]) for i in range(count)]
    given = [take(readies[i]) for i in range(count)]
    stream_grad_o, stream_out_o = take(2)
    outs = take(n_outs)
    (part,) = take(1)
    reduces = [take(2), take(2)]
    recv = [given[i] + take(len(shapes[i]) - readies[i]) for i in range(count)]
    (gains,) = take(1)
    rights = take(n_outs)
    wg_v, wb_v, stage_v = take(3)
    nones = [[None] * r for r in readies]
    sends = [nones[i] + take(len(shapes[i]) - readies[i]) for i in range(count)]
    send_sems = [nones[i] + take(len(shapes[i]) - readies[i]) for i in range(count)]
    recv_sems = [nones[i] + take(len(shapes[i]) - readies[i]) for i in range(count)]
    left_s, got_s, total_s, own_v, got_v, send_v, send_w = take(7)
    value_v, base_v, gain_sends, gain_recvs = take(4)
    rs_sems = [take(3), take(3)]
    gain_ss, gain_rs, right_sem, sem, engine_sem = take(5)

    line = TensorLine()
    engine = Engine(left_s, got_s, total_s, engine_sem)
    tensor = [
        TensorReduce(line, source, *reduces[q], own_v, got_v, (send_v, send_w)[q], *rs_sems[q])
        for q, source in enumerate((part, part_out))
    ]
    tensor[1].start()
    loads = [copy_in(rights_hbm[i], rights[i], right_sem.at[i]) for i in range(n_outs)]
    weights = [copy_in(w_gate, wg_v, right_sem.at[n_outs]), copy_in(w_branch, wb_v, right_sem.at[n_outs + 1])]
    loaded = set()

    def load(i):
        if i not in loaded:
            loads[i].wait()
            loaded.add(i)

    def columns_of(i):
        return pl.ds(out_of[i][1], columns[i])

    items = [
        Item(
            make_stages(n, plan[i]), lefts[lefts_of[i]], rights[out_of[i][0]].at[:, columns_of(i)], width, readies[i],
            (outs[out_of[i][0]].at[:, columns_of(i)], recv[i], sends[i], send_sems[i], recv_sems[i]),
        )
        for i in range(count)
    ]

    rows, features = stream.shape

    def stage(index):
        at = pl.ds(pl.multiple_of(index * rows, rows), rows)

        @pl.loop(0, features // 512)
        def _(j):
            cols = pl.ds(pl.multiple_of(j * 512, 512), 512)
            total = dot_nt(rights[n_outs - 2][at, :], wg_v[cols, :]) + dot_nt(rights[n_outs - 1][at, :], wb_v[cols, :])
            stage_v[:, cols] = total.astype(BF16)

        copy_in(stage_v, tensor[0].block(index), sem.at[0]).wait()

    def part_first():
        for i in (n_outs - 2, n_outs - 1):
            load(i)
        for copy in weights:
            copy.wait()
        stage(line.cross)
        tensor[0].mates[0].start()
        stage(line.peer)

    def part_second():
        stage(line.mate)
        tensor[0].mates[1].start()
        stage(line.index)

    def grad_end():
        copies = [copy_in(stream, value_v, sem.at[0]), copy_in(d_middle, base_v, sem.at[1])]
        for copy in copies:
            copy.wait()
        gains[...] = jnp.zeros_like(gains)

        def use(at, total):
            back, terms = norm_backward(value_v[at, :].astype(F32), gain[...], total)
            base_v[at, :] = base_v[at, :] + back
            gains[...] += fold_rows(terms)

        tensor[0].end(use)
        copy_in(base_v, stream_grad_o, sem.at[0]).wait()
        first = jnp.sum(gains[...], axis=0, keepdims=True)
        second = jnp.sum(gain_grad_two[...], axis=0, keepdims=True)
        pick = lax.broadcasted_iota(jnp.int32, gains.shape, 0)
        gains[...] = jnp.where(pick == 0, first, jnp.where(pick == 1, second, 0.0))

    def out_end():
        copy_in(middle, base_v, sem.at[0]).wait()

        def use(at, total):
            base_v[at, :] = base_v[at, :] + total

        tensor[1].end(use)
        copy_in(base_v, stream_out_o, sem.at[0]).wait()

    extra = [part_first, tensor[0].middle, part_second, tensor[1].middle, grad_end, out_end]
    extra += gather_sums(gains, gain_sends, gain_recvs, gain_ss, gain_rs)
    for i, t, k in order:
        if i < 0:
            if extra:
                extra.pop(0)()
            continue
        load(out_of[i][0])
        if t < len(shapes[i]):
            engine.round(items[i], t, k)
        else:
            engine.finish(items[i])
    for step in extra:
        step()
    for i, item in enumerate(items):
        engine.drain(item, range(readies[i], len(shapes[i])))
    for reduce in tensor:
        reduce.drain()


def task_order(plan, readies, names, n):
    tasks = []
    for last_first, ready in zip(plan, readies):
        sizes = digit_sizes(n)
        if last_first:
            sizes = sizes[1:] + sizes[:1]
        i = len(tasks)
        tasks.append([(i, t, k) for t, m in enumerate(sizes) for k in range(1, m) if t >= ready] + [(i, len(sizes), 0)])
    out, at = [], [0] * len(plan)
    for i in names:
        if i < 0:
            out.append((-1, 0, 0))
        elif at[i] < len(tasks[i]):
            out.append(tasks[i][at[i]])
            at[i] += 1
    for i in range(len(plan)):
        out += tasks[i][at[i] :]
    return out


def finish(part_out, middle, d_middle, stream, w_gate, w_branch, gain, gain_grad_two, lefts, lefts_of, rights, given, plan, out_of, names):
    n = lax.axis_size("dp")
    tokens, features = part_out.shape
    width, rows = features // n, tokens // 4
    readies = [len(g) for g in given]
    pieces = [sum(o == q for o, _ in out_of) for q in range(len(rights))]
    columns = [rights[o].shape[1] // pieces[o] for o, _ in out_of]
    out_of = [(o, q * c) for (o, q), c in zip(out_of, columns)]
    widest = max(columns)
    shapes = [stage_shapes(n, last_first, width, c)[ready:] for last_first, c, ready in zip(plan, columns, readies)]
    steps = 2 + (n - 1).bit_length()
    dma = pltpu.SemaphoreType.DMA
    stream_shape = jax.ShapeDtypeStruct((rows, features), F32)
    out_shape = [stream_shape, stream_shape] + [jax.ShapeDtypeStruct((width, r.shape[1]), F32) for r in rights]
    out_shape += [jax.ShapeDtypeStruct((tokens, features), BF16)]
    out_shape += TensorReduce.results(tokens, features) * 2 + [s[0] for item in shapes for s in item]
    results = pl.pallas_call(
        functools.partial(finish_kernel, n, width, plan, task_order(plan, readies, names, n), lefts_of, readies, columns, out_of),
        out_shape=[*out_shape, jax.ShapeDtypeStruct((8, features), F32)],
        in_specs=[HBM] * 6 + [IN_VMEM] * 2 + [HBM] * (len(lefts) + len(rights) + sum(readies)),
        out_specs=[HBM] * len(out_shape) + [IN_VMEM],
        scratch_shapes=[
            *[pltpu.VMEM(r.shape, BF16) for r in rights],
            pltpu.VMEM(w_gate.shape, BF16), pltpu.VMEM(w_branch.shape, BF16), pltpu.VMEM((rows, features), BF16),
            *[s[1] for item in shapes for s in item],
            *[s[2] for item in shapes for s in item],
            *[s[3] for item in shapes for s in item],
            pltpu.VMEM((tokens, width), BF16),
            pltpu.VMEM((2 * len(digit_sizes(n)), width, widest), BF16),
            pltpu.VMEM((max(s[4] for item in shapes for s in item), widest), F32),
            *TensorReduce.buffers(tokens, features),
            pltpu.VMEM((rows, features), BF16),
            pltpu.VMEM((rows, features), BF16),
            pltpu.VMEM((rows, features), F32),
            pltpu.VMEM((steps, 8, features), F32),
            pltpu.VMEM((steps, 8, features), F32),
            *TensorReduce.semaphores(),
            *TensorReduce.semaphores(),
            dma((steps,)), dma((steps,)), dma((len(rights) + 2,)), dma((2,)), dma((1 + 2 * len(digit_sizes(n)),)),
        ],
        compiler_params=pltpu.CompilerParams(vmem_limit_bytes=VMEM_BYTES, has_side_effects=True),
        cost_estimate=pl.CostEstimate(
            flops=2 * tokens * features * sum(columns), bytes_accessed=4 * features * sum(columns), transcendentals=0
        ),
        name="finish",
    )(
        part_out, middle, d_middle, stream, w_gate, w_branch, gain, gain_grad_two,
        *[column_blocks(v, n) for v in lefts], *rights, *[g for item in given for g in item],
    )
    return results[0], results[1], results[2 : 2 + len(rights)], results[-1]


class TensorGather:
    def __init__(self, line, own_v, out, send_sem, recv_sem):
        self.line, self.own_v, self.out, self.rows = line, own_v, out, own_v.shape[0]
        self.over = remote(own_v, self.block(line.index), send_sem.at[0], recv_sem.at[0], "tensor", line.peer)
        self.aside = remote(own_v, self.block(line.index), send_sem.at[1], recv_sem.at[1], "tensor", line.mate)
        self.onward = remote(self.block(line.peer), self.block(line.peer), send_sem.at[2], recv_sem.at[2], "tensor", line.mate)

    def block(self, index):
        return self.out.at[pl.ds(pl.multiple_of(index * self.rows, self.rows), self.rows)]

    def start(self):
        self.over.start()
        self.aside.start()

    def forward(self):
        self.over.wait_recv()
        self.onward.start()

    def drain(self):
        for copy in (self.over, self.aside, self.onward):
            copy.wait_send()

    @staticmethod
    def semaphores():
        return [pltpu.SemaphoreType.DMA((3,)), pltpu.SemaphoreType.DMA((3,))]


def forward_kernel(*refs):
    take = Reader(refs)
    cot_own, w_gate, w_branch, w_out = take(4)
    stream, gain, gain_two, masks, vecs, w_cat = take(6)
    normed, cot, gated_o, branch_o, conv_o, states_o, product_o, middle_o, normed_two, from_mate, from_peer = take(11)
    wg_v, wb_v, wo_v, own_v, cot_v, block_v, gated_v, branch_v, conv_v, states_v, product_v = take(11)
    pre_s, a_s, b_s, part_v, rs_own, rs_got, rs_send_v, middle_v, two_v = take(9)
    ag_sems, cot_sems, two_sems = take(2), take(2), take(2)
    rs_send, rs_recv, rs_sem, sem = take(4)
    rows, features = stream.shape
    line = TensorLine()
    gather = TensorGather(line, own_v, normed, *ag_sems)
    cots = TensorGather(line, cot_v, cot, *cot_sems)
    twos = TensorGather(line, two_v, normed_two, *two_sems)
    reduce = TensorReduce(line, part_v, from_mate, from_peer, rs_own, rs_got, rs_send_v, rs_send, rs_recv, rs_sem)
    loads = [copy_in(w_gate, wg_v, sem.at[0]), copy_in(w_branch, wb_v, sem.at[1]), copy_in(w_out, wo_v, sem.at[2])]
    cot_load = copy_in(cot_own, cot_v, sem.at[3])

    def chunks(body):
        @pl.loop(0, rows // 16)
        def _(r):
            body(pl.ds(pl.multiple_of(r * 16, 16), 16))

    def norm(values, gains):
        inverse = lax.rsqrt(jnp.mean(values * values, axis=-1, keepdims=True) + epsilon)
        return (values * inverse * gains).astype(BF16)

    def first_norm(at):
        own_v[at, :] = norm(stream[at, :].astype(F32), gain[...])

    chunks(first_norm)
    gather.start()
    keep = [copy_in(own_v, gather.block(line.index), sem.at[4])]
    cot_load.wait()
    cots.start()
    keep.append(copy_in(cot_v, cots.block(line.index), sem.at[5]))

    def project(source, index):
        at = pl.ds(pl.multiple_of(index * rows, rows), rows)
        branch_v[at, :] = jnp.dot(source, wb_v[...], preferred_element_type=F32)
        gated_v[at, :] = jnp.dot(source, wg_v[...], preferred_element_type=F32)

    loads[0].wait()
    loads[1].wait()
    project(own_v[...], line.index)
    gather.aside.wait_recv()
    copy_in(gather.block(line.mate), block_v.at[0], sem.at[6]).wait()
    project(block_v[0], line.mate)
    gather.forward()
    copy_in(gather.block(line.peer), block_v.at[1], sem.at[6]).wait()
    project(block_v[1], line.peer)
    gather.onward.wait_recv()
    copy_in(gather.block(line.cross), block_v.at[0], sem.at[6]).wait()
    project(block_v[0], line.cross)
    outs = [copy_in(branch_v, branch_o, sem.at[7]), copy_in(gated_v, gated_o, sem.at[8])]
    mixer_forward_kernel(branch_v, gated_v, masks, vecs, w_cat, conv_v, states_v, product_v, pre_s, a_s, b_s)
    outs += [copy_in(conv_v, conv_o, sem.at[9]), copy_in(states_v, states_o, sem.at[10]), copy_in(product_v, product_o, sem.at[11])]
    loads[2].wait()

    def out_block(index):
        at = pl.ds(pl.multiple_of(index * rows, rows), rows)
        part_v[at, :] = jnp.dot(product_v[at, :], wo_v[...], preferred_element_type=F32).astype(BF16)

    out_block(line.cross)
    reduce.mates[0].start()
    out_block(line.peer)
    reduce.middle()
    out_block(line.mate)
    reduce.mates[1].start()
    out_block(line.index)
    cots.forward()

    def second_norm(at, total):
        values = stream[at, :].astype(F32) + total
        middle_v[at, :] = values
        two_v[at, :] = norm(values, gain_two[...])

    reduce.end(second_norm)
    twos.start()
    keep += [copy_in(two_v, twos.block(line.index), sem.at[12]), copy_in(middle_v, middle_o, sem.at[13])]
    cots.aside.wait_recv()
    cots.onward.wait_recv()
    twos.forward()
    twos.aside.wait_recv()
    twos.onward.wait_recv()
    for copy in keep + outs:
        copy.wait()
    for gathered in (gather, cots, twos):
        gathered.drain()
    reduce.drain()


def forward(cot_own, w_gate, w_branch, w_out, stream, gain, gain_two, masks, vecs, w_cat):
    rows, features = stream.shape
    tokens, channels = 4 * rows, w_gate.shape[1]
    lanes = channels // LANES
    whole = jax.ShapeDtypeStruct((tokens, features), BF16)
    wide = jax.ShapeDtypeStruct((tokens, channels), F32)
    narrow = jax.ShapeDtypeStruct((tokens, channels), BF16)
    results = [whole, whole, wide, wide, narrow, wide, narrow, jax.ShapeDtypeStruct((rows, features), F32), whole]
    results += TensorReduce.results(tokens, features)
    block = pltpu.VMEM((rows, features), BF16)
    return pl.pallas_call(
        forward_kernel,
        out_shape=results,
        in_specs=[HBM] * 4 + [IN_VMEM] * 6,
        out_specs=[HBM] * len(results),
        scratch_shapes=[
            pltpu.VMEM(w_gate.shape, BF16), pltpu.VMEM(w_branch.shape, BF16), pltpu.VMEM(w_out.shape, BF16),
            block, block, pltpu.VMEM((2, rows, features), BF16),
            pltpu.VMEM((tokens, channels), F32), pltpu.VMEM((tokens, channels), F32),
            pltpu.VMEM((tokens, channels), BF16), pltpu.VMEM((tokens, channels), F32), pltpu.VMEM((tokens, channels), BF16),
            pltpu.VMEM((tokens, 2 * channels), F32),
            pltpu.VMEM((lanes, tokens, LANES), F32), pltpu.VMEM((lanes, tokens, LANES), F32),
            pltpu.VMEM((tokens, features), BF16), *TensorReduce.buffers(tokens, features),
            pltpu.VMEM((rows, features), F32), block,
            *TensorGather.semaphores(), *TensorGather.semaphores(), *TensorGather.semaphores(),
            *TensorReduce.semaphores(), pltpu.SemaphoreType.DMA((14,)),
        ],
        compiler_params=pltpu.CompilerParams(vmem_limit_bytes=VMEM_BYTES, has_side_effects=True),
        cost_estimate=pl.CostEstimate(flops=9 * 10**9, bytes_accessed=40 * 10**6, transcendentals=6 * tokens * channels),
        name="forward",
    )(cot_own, w_gate, w_branch, w_out, stream, gain, gain_two, masks, vecs, w_cat)

DP_PLAN = [True, False, False, False, False, False, False]
DP_OUTS = [(0, 0), (1, 0), (2, 0), (2, 1), (3, 0), (4, 0), (5, 0)]
DP_ORDER = [2, 6, 2, 1, -1, 2, -1, 3, 6, 1, 5, -1, 6, -1, 4, 3, 1, 2, 6, 0, -1, -1, -1, 5, 3, 6, -1, 5, 4, 1, -1, 5, 4, -1, 3, 0, 4, -1, 5, 3, -1, 4]


def dot(left, right, dims, out=F32):
    return lax.dot_general(left, right, (dims, ((), ())), preferred_element_type=F32).astype(out)


def spread_heads(*weights):
    heads, width = weights[0].shape[:2]
    total = len(weights) * heads * width
    rows = []
    for h in range(heads):
        row = 0
        for q, weight in enumerate(weights):
            before = (q * heads + h) * width
            row = row + jnp.pad(weight[h], ((0, 0), (before, total - before - width)))
        rows.append(row)
    return jnp.concatenate(rows)


def head_blocks(dense, heads, width):
    return jnp.stack([dense[h * width : (h + 1) * width, h * width : (h + 1) * width] for h in range(heads)])


def on_device(
    stream_in, segments, first_gain, gelu_gate_weight, recurrent_branch_weight, conv_kernel, conv_bias, recur_weight, recur_bias,
    inlet_weight, inlet_bias, decay_param, recurrent_output_weight, second_gain, gate_projection_weight, up_projection_weight,
    down_projection_weight, cotangent,
):
    seq_len = segments.shape[1]
    heads, head_width = recur_weight.shape[:2]
    ids = jnp.pad(segments[0], (3, 8), constant_values=-1)
    same = [(ids[3 - k : 3 - k + seq_len] == segments[0]).astype(F32) for k in range(1, 4)]
    masks = jnp.pad(jnp.stack(same, axis=1), ((0, 8), (0, 5)))
    softplus = jax.nn.softplus(-decay_param)
    vecs = jnp.concatenate([conv_kernel, jnp.stack([conv_bias, recur_bias, inlet_bias, softplus])])
    w_cat = spread_heads(recur_weight, inlet_weight)

    normed, cot, gated_pre, branch_pre, conv_out, states, product, middle, normed_two, _, _ = forward(
        cotangent[0], gelu_gate_weight, recurrent_branch_weight, recurrent_output_weight, stream_in[0], first_gain[None],
        second_gain[None], masks, vecs, w_cat,
    )
    (
        d_middle, d_attended, hidden, d_gate, d_up, d_gated, d_ri, d_branch, _, part_out, _, _, down_got, gate_got, up_got, sums, gain_two,
    ) = middle_part(
        middle, cot, normed_two, gate_projection_weight, up_projection_weight, down_projection_weight, recurrent_output_weight,
        gated_pre, branch_pre, states, conv_out, second_gain[None], masks, vecs, w_cat,
    )
    stream_grad, stream_out, gradients, gains = finish(
        part_out, middle, d_middle, stream_in[0], gelu_gate_weight, recurrent_branch_weight, first_gain[None], gain_two,
        [cot, normed_two, d_attended, normed], [0, 1, 1, 1, 2, 3, 3], [hidden, d_gate, d_up, product, d_gated, d_branch],
        [[down_got], [gate_got], [up_got], [], [], [], []], DP_PLAN, DP_OUTS, DP_ORDER,
    )
    down_gradient, gate_gradient, up_gradient, output_gradient, gated_gradient, branch_gradient = gradients

    width = heads * head_width
    dense = dot(conv_out, d_ri, ((0,), (0,)))
    grad_recur = head_blocks(dense[:, :width], heads, head_width)
    grad_inlet = head_blocks(dense[:, width:], heads, head_width)
    sums = jnp.sum(sums, axis=1)
    small = jnp.concatenate([sums.reshape(-1), grad_recur.reshape(-1), grad_inlet.reshape(-1)])
    small = lax.psum(small, "dp")
    sums = small[: 8 * width].reshape(8, width)
    grad_recur, grad_inlet = small[8 * width :].reshape(2, heads, head_width, head_width)
    grad_decay = decay_scale * jax.nn.sigmoid(-decay_param) * sums[7]
    return (
        stream_out[None], stream_grad[None], gains[0], gated_gradient, branch_gradient, sums[:4], sums[4], grad_recur, sums[5],
        grad_inlet, sums[6], grad_decay, output_gradient.T, gains[1], gate_gradient, up_gradient, down_gradient.T,
    )


def solution(mesh):
    in_specs = (
        P("dp", "tensor", None),
        P("dp", None),
        P(),
        P(None, "tensor"),
        P(None, "tensor"),
        P(None, "tensor"),
        P("tensor"),
        P("tensor", None, None),
        P("tensor"),
        P("tensor", None, None),
        P("tensor"),
        P("tensor"),
        P("tensor", None),
        P(),
        P(None, "tensor"),
        P(None, "tensor"),
        P("tensor", None),
        P("dp", "tensor", None),
    )
    out_specs = (
        P("dp", "tensor", None),
        P("dp", "tensor", None),
        P(),
        P("dp", "tensor"),
        P("dp", "tensor"),
        P(None, "tensor"),
        P("tensor"),
        P("tensor", None, None),
        P("tensor"),
        P("tensor", None, None),
        P("tensor"),
        P("tensor"),
        P("tensor", "dp"),
        P(),
        P("dp", "tensor"),
        P("dp", "tensor"),
        P("tensor", "dp"),
    )
    return jax.shard_map(
        on_device, mesh=mesh, in_specs=in_specs, out_specs=out_specs, check_vma=False
    )
```

```python
import functools

import jax
import jax.numpy as jnp
from jax import lax
from jax.experimental import pallas as pl
from jax.experimental.pallas import tpu as pltpu
from jax.sharding import PartitionSpec as P

epsilon = 1e-06
decay_scale = 8.0
LANES = 128
GELU_C = 0.7978845608028654
GELU_K = 0.044715
F32 = jnp.float32
BF16 = jnp.bfloat16
VMEM_BYTES = 60 * 1024 * 1024


def minus_expm1(y, exp_y):
    s = 1.0 + y * (1.0 / 9.0)
    for d in range(8, 1, -1):
        s = 1.0 + (y * (1.0 / d)) * s
    return jnp.where(y > -0.5, -y * s, 1.0 - exp_y)


def gelu_parts(v):
    v2 = v * v
    t = jnp.tanh(GELU_C * v * (1.0 + GELU_K * v2))
    half = 0.5 * (1.0 + t)
    slope = half + 0.5 * v * (1.0 - t * t) * (GELU_C * (1.0 + 3.0 * GELU_K * v2))
    return v * half, slope


def lane_tiles(width):
    return [slice(j * LANES, (j + 1) * LANES) for j in range(width // LANES)]


def fold_rows(v):
    return jnp.sum(v.reshape(v.shape[0] // 8, 8, v.shape[1]), axis=0)


def gates_pre(rows, step, conv_ref, w_ref, pre_s):
    @pl.loop(0, rows // step)
    def _(i):
        r = pl.ds(pl.multiple_of(i * step, step), step)
        pre_s[r, :] = jnp.dot(conv_ref[r, :], w_ref[...], preferred_element_type=F32)


def mixer_forward_kernel(branch_ref, gated_ref, mask_ref, vec_ref, w_ref, conv_ref, states_ref, product_ref, pre_s, a_s, b_s):
    rows, width = branch_ref.shape
    seg = rows // 8
    tiles = lane_tiles(width)

    @pl.loop(0, 8)
    def _(s):
        t0 = pl.multiple_of(s * seg, seg)
        before = pl.multiple_of(jnp.maximum(t0 - 8, 0), 8)
        same = [mask_ref[pl.ds(t0, seg), k : k + 1] for k in range(3)]
        for cols in tiles:
            b = branch_ref[pl.ds(t0, seg), cols]
            ext = jnp.concatenate([branch_ref[pl.ds(before, 8), cols], b], axis=0)
            out = vec_ref[4:5, cols] + vec_ref[0:1, cols] * b
            for k in range(1, 4):
                out = out + vec_ref[k : k + 1, cols] * pltpu.roll(ext, k, 0)[8:] * same[k - 1]
            conv_ref[pl.ds(t0, seg), cols] = out.astype(BF16)

    gates_pre(rows, 256, conv_ref, w_ref, pre_s)

    @pl.loop(0, 8)
    def _(s):
        t0 = pl.multiple_of(s * seg, seg)
        c = mask_ref[pl.ds(t0, seg), 0:1]
        for j, cols in enumerate(tiles):
            cols_i = slice(width + j * LANES, width + (j + 1) * LANES)
            r = jax.nn.sigmoid(pre_s[pl.ds(t0, seg), cols] + vec_ref[5:6, cols])
            i = jax.nn.sigmoid(pre_s[pl.ds(t0, seg), cols_i] + vec_ref[6:7, cols])
            log_a = (-decay_scale * vec_ref[7:8, cols]) * r
            a = jnp.exp(log_a)
            n = jnp.sqrt(minus_expm1(2.0 * log_a, a * a))
            mult = (1.0 - c) + c * n
            a_s[j, pl.ds(t0, seg), :] = a * c
            b_s[j, pl.ds(t0, seg), :] = mult * i * conv_ref[pl.ds(t0, seg), cols].astype(F32)

    row = lax.broadcasted_iota(jnp.int32, (8, LANES), 0)

    def scan_step(i, carry):
        at = pl.ds(pl.multiple_of(i * 8, 8), 8)
        out = []
        for j, cols in enumerate(tiles):
            a, b = a_s[j, at, :], b_s[j, at, :]
            for s in (1, 2, 4):
                b = b + a * jnp.where(row >= s, pltpu.roll(b, s, 0), 0.0)
                a = a * jnp.where(row >= s, pltpu.roll(a, s, 0), 1.0)
            b = b + a * carry[j]
            states_ref[at, cols] = b
            out.append(jnp.broadcast_to(b[7:8, :], (8, LANES)))
        return tuple(out)

    lax.fori_loop(0, rows // 8, scan_step, tuple(jnp.zeros((8, LANES), F32) for _ in tiles), unroll=4)

    @pl.loop(0, 8)
    def _(s):
        at = pl.ds(pl.multiple_of(s * seg, seg), seg)
        for cols in tiles:
            act, _ = gelu_parts(gated_ref[at, cols])
            product_ref[at, cols] = (states_ref[at, cols] * act).astype(BF16)


class MixerBackward:
    def __init__(self, masks, vecs, w_cat, states, branch, conv, dgated, dri, dbranch, sums, pre_s, a_s, n_s, ac_s, e_s):
        self.masks, self.vecs, self.w_cat, self.states, self.branch, self.conv = masks, vecs, w_cat, states, branch, conv
        self.dgated, self.dri, self.dbranch, self.sums = dgated, dri, dbranch, sums
        self.pre_s, self.a_s, self.n_s, self.ac_s, self.e_s = pre_s, a_s, n_s, ac_s, e_s
        self.rows, self.width = states.shape
        self.seg = self.rows // 8
        self.tiles = lane_tiles(self.width)

    @staticmethod
    def scratch(rows, width):
        lanes = width // LANES
        return [
            pltpu.VMEM((rows, 2 * width), F32),
            pltpu.VMEM((rows, width), F32),
            pltpu.VMEM((rows + 8, width), F32),
            pltpu.VMEM((lanes, rows, LANES), F32),
            pltpu.VMEM((lanes, rows, LANES), F32),
        ]

    def gates(self):
        self.sums[...] = jnp.zeros_like(self.sums)
        gates_pre(self.rows, 256, self.conv, self.w_cat, self.pre_s)

    def factors(self, gated):
        @pl.loop(0, 8)
        def _(s):
            t0 = pl.multiple_of(s * self.seg, self.seg)
            at = pl.ds(t0, self.seg)
            c = self.masks[at, 0:1]
            for j, cols in enumerate(self.tiles):
                cols_i = slice(self.width + j * LANES, self.width + (j + 1) * LANES)
                r = jax.nn.sigmoid(self.pre_s[at, cols] + self.vecs[5:6, cols])
                self.pre_s[at, cols] = r
                self.pre_s[at, cols_i] = jax.nn.sigmoid(self.pre_s[at, cols_i] + self.vecs[6:7, cols])
                log_a = (-decay_scale * self.vecs[7:8, cols]) * r
                a = jnp.exp(log_a)
                d = self.a_s[at, cols]
                self.a_s[at, cols] = a
                self.n_s[at, cols] = jnp.sqrt(minus_expm1(2.0 * log_a, a * a))
                self.ac_s[j, at, :] = a * c
                act, slope = gelu_parts(gated[at, cols])
                self.e_s[j, at, :] = d * act
                self.dgated[at, cols] = (d * self.states[at, cols] * slope).astype(BF16)

    def scan(self):
        row = lax.broadcasted_iota(jnp.int32, (8, LANES), 0)

        def step(q, carry):
            at = pl.ds(pl.multiple_of((self.rows // 8 - 1 - q) * 8, 8), 8)
            out = []
            for j in range(len(self.tiles)):
                e, later = carry[j]
                now = self.ac_s[j, at, :]
                a = jnp.where(row == 7, later, pltpu.roll(now, 7, 0))
                b = self.e_s[j, at, :]
                for s in (1, 2, 4):
                    b = b + a * jnp.where(row < 8 - s, pltpu.roll(b, 8 - s, 0), 0.0)
                    a = a * jnp.where(row < 8 - s, pltpu.roll(a, 8 - s, 0), 1.0)
                b = b + a * e
                self.e_s[j, at, :] = b
                out.append((jnp.broadcast_to(b[0:1, :], (8, LANES)), jnp.broadcast_to(now[0:1, :], (8, LANES))))
            return tuple(out)

        none = jnp.zeros((8, LANES), F32)
        lax.fori_loop(0, self.rows // 8, step, tuple((none, none) for _ in self.tiles), unroll=4)

    def gate_gradients(self):
        seg, width = self.seg, self.width

        @pl.loop(0, 8)
        def _(s):
            t0 = pl.multiple_of(s * seg, seg)
            at = pl.ds(t0, seg)
            before = pl.multiple_of(jnp.maximum(t0 - 8, 0), 8)
            c = self.masks[at, 0:1]
            for j, cols in enumerate(self.tiles):
                cols_i = slice(width + j * LANES, width + (j + 1) * LANES)
                e = self.e_s[j, at, :]
                ext = jnp.concatenate([self.states[pl.ds(before, 8), cols], self.states[at, cols]], axis=0)
                earlier = pltpu.roll(ext, 1, 0)[8:]
                r, i, a, n = self.pre_s[at, cols], self.pre_s[at, cols_i], self.a_s[at, cols], self.n_s[at, cols]
                cv = self.conv[at, cols].astype(F32)
                ec = e * c
                d_log = a * (ec * earlier) - ec * i * cv * (a * a / n)
                rr = d_log * r
                dr = ((-decay_scale * self.vecs[7:8, cols]) * rr * (1.0 - r)).astype(BF16)
                em = e * ((1.0 - c) + c * n) * i
                di = (em * cv * (1.0 - i)).astype(BF16)
                self.dri[at, cols] = dr
                self.dri[at, cols_i] = di
                self.n_s[at, cols] = em
                self.sums[5, :, cols] += fold_rows(dr.astype(F32))
                self.sums[6, :, cols] += fold_rows(di.astype(F32))
                self.sums[7, :, cols] += fold_rows(rr)

        @pl.loop(0, self.rows // 256)
        def _(i):
            at = pl.ds(pl.multiple_of(i * 256, 256), 256)
            self.n_s[at, :] += dot_nt(self.dri[at, :], self.w_cat[...])

        self.n_s[self.rows : self.rows + 8, :] = jnp.zeros((8, width), F32)

    def convolution(self):
        @pl.loop(0, 8)
        def _(s):
            t0 = pl.multiple_of(s * self.seg, self.seg)
            at, ext = pl.ds(t0, self.seg), pl.ds(t0, self.seg + 8)
            same = [self.masks[ext, k : k + 1] for k in range(3)]
            for cols in self.tiles:
                d = self.n_s[ext, cols]
                b = self.branch[at, cols]
                self.sums[4, :, cols] += fold_rows(d[: self.seg])
                self.sums[0, :, cols] += fold_rows(d[: self.seg] * b)
                total = self.vecs[0:1, cols] * d[: self.seg]
                for k in range(1, 4):
                    moved = pltpu.roll(d * same[k - 1], self.seg + 8 - k, 0)[: self.seg]
                    total = total + self.vecs[k : k + 1, cols] * moved
                    self.sums[k, :, cols] += fold_rows(moved * b)
                self.dbranch[at, cols] = total.astype(BF16)


def dot_nt(left, right):
    return lax.dot_general(left, right, (((1,), (1,)), ((), ())), preferred_element_type=F32)


class Stage:
    def __init__(self, stride, size, later):
        self.stride, self.size, self.later = stride, size, later
        self.blocks = 1
        for s in later:
            self.blocks *= s.size
        self.digit = lax.rem(lax.axis_index("dp") // stride, size)

    def offset(self, position):
        total = 0
        for s in reversed(self.later):
            total = total + lax.rem(position, s.size) * s.stride
            position = position // s.size
        return total


def digit_sizes(n):
    if n == 8:
        return [2, 4]
    sizes = []
    while n > 1:
        m = 4 if n % 4 == 0 else 2 if n % 2 == 0 else n
        sizes.append(m)
        n //= m
    return sizes


def make_stages(n, last_first):
    digits, stride = [], 1
    for m in digit_sizes(n):
        digits.append((stride, m))
        stride *= m
    if last_first:
        digits = digits[1:] + digits[:1]
    stages = []
    for stride, m in reversed(digits):
        stages.insert(0, Stage(stride, m, list(stages)))
    return stages


class Item:
    def __init__(self, stages, left, right, width, ready, refs, resident=None):
        self.stages, self.left, self.right, self.width, self.ready = stages, left, right, width, ready
        self.resident = resident
        self.columns = right.shape[1]
        self.out, self.recv, self.send, self.send_sem, self.recv_sem = refs

    def message(self, t, back, k, slot, rows=None):
        stage = self.stages[t]
        rows = pl.ds(0, stage.blocks * self.width) if rows is None else rows
        step = jnp.where(back, -stage.stride, stage.stride)
        return pltpu.make_async_remote_copy(
            src_ref=self.send[t].at[slot, rows],
            dst_ref=self.recv[t].at[back, k - 1, rows],
            send_sem=self.send_sem[t].at[slot],
            recv_sem=self.recv_sem[t].at[back, k - 1],
            device_id={"dp": lax.axis_index("dp") + step},
            device_id_type=pl.DeviceIdType.MESH,
        )


class Engine:
    def __init__(self, left_s, got_s, total_s, sem, out_s=None, out_sem=None):
        self.left_s, self.got_s, self.total_s, self.sem = left_s, got_s, total_s, sem
        self.out_s, self.out_sem, self.finished = out_s, out_sem, None

    def fetch(self, item, block, slot):
        if len(item.left.shape) == 3:
            source = item.left.at[block]
        else:
            source = item.left.at[:, pl.ds(pl.multiple_of(block * item.width, item.width), item.width)]
        return pltpu.make_async_copy(source, self.left_s.at[slot], self.sem.at[slot])

    def products(self, item, count, block_of, store):
        if item.resident is not None:

            @pl.loop(0, count)
            def _(p):
                cols = pl.ds(pl.multiple_of(block_of(p) * item.width, item.width), item.width)
                store(p, dot_tn(item.resident[:, cols], item.right[...]))

            return
        self.fetch(item, block_of(0), 0).start()

        @pl.loop(0, count)
        def _(p):
            slot = lax.rem(p, 2)
            if count > 1:

                @pl.when(p + 1 < count)
                def _():
                    self.fetch(item, block_of(p + 1), 1 - slot).start()

            self.fetch(item, block_of(p), slot).wait()
            store(p, dot_tn(self.left_s[slot], item.right[...]))

    def got_copy(self, item, i, source):
        return pltpu.make_async_copy(source, self.got_s.at[i, :, pl.ds(0, item.columns)], self.sem.at[2 + i])

    def start_gots(self, item, first, gots):
        for i, (condition, source) in enumerate(gots):

            @pl.when(condition)
            def _(i=i, source=source):
                self.got_copy(item, first + i, source).start()

    def add_gots(self, item, gots, put):
        for i, (condition, source) in enumerate(gots):

            @pl.when(condition)
            def _(i=i, source=source):
                self.got_copy(item, i, source).wait()

        @pl.loop(0, item.width // 16)
        def _(r):
            at = pl.ds(pl.multiple_of(r * 16, 16), 16)
            total = self.total_s[at, pl.ds(0, item.columns)]
            for i, (condition, _) in enumerate(gots):
                total = total + jnp.where(condition, self.got_s[i, at, pl.ds(0, item.columns)].astype(F32), 0.0)
            put(at, total)

    def arrived(self, item, t, position):
        found, last_found = [], []
        for u in range(t):
            stage = item.stages[u]
            spot = position
            scale = 1
            for s in item.stages[t:]:
                scale *= s.size
            lead = 0
            for s in item.stages[u + 1 : t]:
                lead = lead * s.size + s.digit
            rows = pl.ds((lead * scale + spot) * item.width, item.width)
            last = stage.size - 2
            if stage.size == 2:
                back = jnp.where(stage.digit == 0, 1, 0)
                (last_found if u == t - 1 else found).append((stage.digit >= 0, item.recv[u].at[back, last, rows]))
            else:
                (last_found if u == t - 1 else found).append((stage.digit >= 1, item.recv[u].at[0, last, rows]))
                (last_found if u == t - 1 else found).append((stage.digit <= stage.size - 2, item.recv[u].at[1, last, rows]))
        return found, last_found

    def own_base(self, item, t):
        base = 0
        for s in item.stages[:t]:
            base = base + s.digit * s.stride
        return base

    def wait_last(self, item, t):
        if t < item.ready:
            return
        stage = item.stages[t]
        for back in range(2):
            me = stage.digit if back == 0 else stage.size - 1 - stage.digit

            @pl.when(me >= 1)
            def _(back=back):
                item.message(t, back, stage.size - 1, 0).wait_recv()

    def round(self, item, t, k):
        stage = item.stages[t]
        base = self.own_base(item, t)
        alone = t == 0 and k == 1
        if k == 1 and t > 0:
            self.wait_last(item, t - 1)

        @pl.loop(0, 2)
        def _(back):
            me = jnp.where(back == 0, stage.digit, stage.size - 1 - stage.digit)
            there = me + stage.size - k
            value = jnp.where(back == 0, there, stage.size - 1 - there)
            slot = jnp.where(value > stage.digit, value - 1, value)

            def rows_of(p):
                return pl.ds(pl.multiple_of(p * item.width, item.width), item.width)

            def gots_of(p):
                earlier = sum(self.arrived(item, t, value * stage.blocks + p), [])
                return earlier, [(me >= 1, item.recv[t].at[back, k - 2, rows_of(p)])] if k > 1 else []

            @pl.when(me <= k - 1)
            def _():
                if not alone:
                    self.start_gots(item, 0, gots_of(0)[0])

                def store(p, total):
                    if alone:
                        item.send[t][slot, rows_of(p), :] = total.astype(BF16)
                    else:
                        self.total_s[:, pl.ds(0, item.columns)] = total
                        if k > 1:

                            @pl.when((me >= 1) & (p == 0))
                            def _():
                                item.message(t, back, k - 1, 0).wait_recv()

                        def put(at, value):
                            rows = pl.ds(pl.multiple_of(p * item.width + at.start, 16), 16)
                            item.send[t][slot, rows, :] = value.astype(BF16)

                        earlier, own = gots_of(p)
                        self.start_gots(item, len(earlier), own)
                        self.add_gots(item, earlier + own, put)

                        @pl.when(p + 1 < stage.blocks)
                        def _():
                            self.start_gots(item, 0, gots_of(p + 1)[0])

                    item.message(t, back, k, slot, rows_of(p)).start()

                self.products(item, stage.blocks, lambda p: base + value * stage.stride + stage.offset(p), store)

    def out_copy(self, item):
        return pltpu.make_async_copy(self.out_s.at[:, pl.ds(0, item.columns)], item.out, self.out_sem)

    def finish(self, item):
        t = len(item.stages)
        self.wait_last(item, t - 1)
        gots = sum(self.arrived(item, t, 0), [])
        self.start_gots(item, 0, gots)

        def store(p, total):
            self.total_s[:, pl.ds(0, item.columns)] = total

            def put(at, value):
                self.out_s[at, pl.ds(0, item.columns)] = value

            self.add_gots(item, gots, put)

        self.settle()
        self.products(item, 1, lambda p: self.own_base(item, t), store)
        self.out_copy(item).start()
        self.finished = item

    def settle(self):
        if self.finished is not None:
            self.out_copy(self.finished).wait()
        self.finished = None

    def drain(self, item, stages):
        for t in stages:
            for slot in range(item.stages[t].size - 1):
                item.message(t, 0, 1, slot).wait_send()


def stage_shapes(n, last_first, width, columns):
    sizes = digit_sizes(n)
    if last_first:
        sizes = sizes[1:] + sizes[:1]
    left, found = n, []
    for t, m in enumerate(sizes):
        left //= m
        found.append(
            (
                jax.ShapeDtypeStruct((2, m - 1, left * width, columns), BF16),
                pltpu.VMEM((m - 1, left * width, columns), BF16),
                pltpu.SemaphoreType.DMA((m - 1,)),
                pltpu.SemaphoreType.DMA((2, m - 1)),
            )
        )
    return found


def dot_tn(left, right):
    return lax.dot_general(left, right, (((0,), (0,)), ((), ())), preferred_element_type=F32)


class Reader:
    def __init__(self, refs):
        self.refs, self.at = refs, 0

    def __call__(self, count=None):
        start = self.at
        self.at += 1 if count is None else count
        return self.refs[start] if count is None else list(self.refs[start : self.at])


def column_blocks(left, n):
    tokens, features = left.shape
    width = features // n
    return left.reshape(tokens, n, width).transpose(1, 0, 2) if width % LANES else left


class TensorLine:
    def __init__(self):
        self.index = lax.axis_index("tensor")
        self.mate, self.peer, self.cross = self.index ^ 1, self.index ^ 2, self.index ^ 3


def copy_in(source, target, sem):
    copy = pltpu.make_async_copy(source, target, sem)
    copy.start()
    return copy


def remote(source, target, send_sem, recv_sem, axis, index):
    return pltpu.make_async_remote_copy(
        src_ref=source, dst_ref=target, send_sem=send_sem, recv_sem=recv_sem,
        device_id={axis: index}, device_id_type=pl.DeviceIdType.MESH,
    )


class TensorReduce:
    def __init__(self, line, part, from_mate, from_peer, own_v, got_v, send_v, send_sem, recv_sem, sem):
        self.line, self.part, self.from_mate, self.from_peer = line, part, from_mate, from_peer
        self.own_v, self.got_v, self.send_v, self.sem = own_v, got_v, send_v, sem
        self.rows = part.shape[0] // 4
        self.mates = [
            remote(self.block(line.cross), from_mate.at[0], send_sem.at[0], recv_sem.at[0], "tensor", line.mate),
            remote(self.block(line.mate), from_mate.at[1], send_sem.at[1], recv_sem.at[1], "tensor", line.mate),
        ]
        self.over = remote(send_v, from_peer, send_sem.at[2], recv_sem.at[2], "tensor", line.peer)

    def block(self, index):
        return self.part.at[pl.ds(pl.multiple_of(index * self.rows, self.rows), self.rows)]

    def start(self):
        for copy in self.mates:
            copy.start()

    def own_rows(self, index, at):
        if self.own_v is not None:
            return self.own_v[at, :].astype(F32)
        return self.part[pl.ds(pl.multiple_of(index * self.rows + at.start, 16), 16), :].astype(F32)

    def fetch_own(self, index):
        return [] if self.own_v is None else [copy_in(self.block(index), self.own_v, self.sem.at[0])]

    def middle(self):
        copies = self.fetch_own(self.line.peer)
        self.mates[0].wait_recv()
        copies.append(copy_in(self.from_mate.at[0], self.got_v.at[0], self.sem.at[1]))
        for copy in copies:
            copy.wait()

        @pl.loop(0, self.rows // 16)
        def _(r):
            at = pl.ds(pl.multiple_of(r * 16, 16), 16)
            self.send_v[at, :] = (self.own_rows(self.line.peer, at) + self.got_v[0, at, :].astype(F32)).astype(BF16)

        self.over.start()

    def end(self, use):
        copies = self.fetch_own(self.line.index)
        self.mates[1].wait_recv()
        copies.append(copy_in(self.from_mate.at[1], self.got_v.at[0], self.sem.at[1]))
        self.over.wait_recv()
        copies.append(copy_in(self.from_peer, self.got_v.at[1], self.sem.at[2]))
        for copy in copies:
            copy.wait()

        @pl.loop(0, self.rows // 16)
        def _(r):
            at = pl.ds(pl.multiple_of(r * 16, 16), 16)
            use(at, self.own_rows(self.line.index, at) + self.got_v[0, at, :].astype(F32) + self.got_v[1, at, :].astype(F32))

    def drain(self):
        for copy in self.mates:
            copy.wait_send()
        self.over.wait_send()

    @staticmethod
    def results(tokens, features):
        return [jax.ShapeDtypeStruct((2, tokens // 4, features), BF16), jax.ShapeDtypeStruct((tokens // 4, features), BF16)]

    @staticmethod
    def semaphores():
        return [pltpu.SemaphoreType.DMA((3,)), pltpu.SemaphoreType.DMA((3,)), pltpu.SemaphoreType.DMA((3,))]

    @staticmethod
    def buffers(tokens, features):
        rows = tokens // 4
        return [pltpu.VMEM((2, rows, features), BF16), pltpu.VMEM((rows, features), BF16)]


def norm_backward(values, gain, d_normed):
    inverse = lax.rsqrt(jnp.mean(values * values, axis=-1, keepdims=True) + epsilon)
    weighted = gain * d_normed
    inner = jnp.mean(weighted * values, axis=-1, keepdims=True)
    return inverse * weighted - values * (inverse * inverse * inverse * inner), d_normed * values * inverse


HBM = pl.BlockSpec(memory_space=pl.ANY)
IN_VMEM = pl.BlockSpec(memory_space=pltpu.VMEM)


def middle_kernel(n, width, *refs):
    take = Reader(refs)
    middle, cot, normed_two, w_gate, w_up, w_down, w_out, gated, branch, states, conv = take(11)
    left_down, left_gate = take(2)
    gain, masks, vecs, w_cat = take(4)
    d_middle, att, hidden_o, dgate_o, dup_o, dgated_o, dri_o, dbranch_o, part_out, from_mate, from_peer = take(11)
    down_recv, (gate_recv, up_recv) = take(2), take(2)
    sums, gain_grad = take(2)
    hidden, att_v = take(2)
    halves = [take(3), take(3)]
    gate_send, gate_ss, gate_rs, up_send, up_ss, up_rs = take(6)
    left_s, got_s, total_s, rs_send, rs_recv, rs_sem, ag_send, ag_recv, sem, engine_sem = take(10)
    tokens, features = cot.shape
    rows, channels, units = tokens // 4, conv.shape[1], hidden.shape[1]
    tile = 512
    line = TensorLine()
    engine = Engine(left_s, got_s, total_s, engine_sem)
    downs = [
        Item(
            make_stages(n, True), left_down, hidden.at[:, pl.ds(q * (units // 2), units // 2)], width, 0,
            (None, [down_recv[q]], [send], [send_sem], [recv_sem]),
        )
        for q, (send, send_sem, recv_sem) in enumerate(halves)
    ]
    gather = TensorGather(line, att_v, att, ag_send, ag_recv)

    def rounds(item):
        return list(range(1, item.stages[0].size))

    def row_block(ref, index):
        return ref.at[pl.ds(pl.multiple_of(index * rows, rows), rows)]

    first, between, last = rounds(downs[0])[:1], rounds(downs[0])[1:-1], rounds(downs[0])[1:][-1:]
    gate = Item(make_stages(n, False), left_gate, hidden, width, 0, (None, [gate_recv], [gate_send], [gate_ss], [gate_rs]))
    half = hidden.at[:, pl.ds(0, units // 2)]
    up = Item(make_stages(n, False), left_gate, half, width, 0, (None, [up_recv], [up_send], [up_ss], [up_rs]))

    def take_rounds(item, numbers):
        for k in numbers:
            engine.round(item, 0, k)

    def tensor_phase(wg_v, wu_v, wd_v, dgate, dup, x_v, c_v, part, got_v, send_v, dmid_v, cot_v):
        gate.right, up.right = dgate, dup.at[:, pl.ds(0, units // 2)]
        weights = [copy_in(w_gate, wg_v, sem.at[0]), copy_in(w_up, wu_v, sem.at[1]), copy_in(w_down, wd_v, sem.at[2])]
        loads = [copy_in(middle, dmid_v, sem.at[3]), copy_in(row_block(cot, line.index), cot_v, sem.at[4])]
        copy_in(row_block(normed_two, 0), x_v, sem.at[5])
        copy_in(row_block(cot, 0), c_v, sem.at[6])
        for load in weights:
            load.wait()

        @pl.loop(0, 4)
        def _(b):
            at = pl.ds(pl.multiple_of(b * rows, rows), rows)
            pltpu.make_async_copy(row_block(normed_two, b), x_v, sem.at[5]).wait()
            pltpu.make_async_copy(row_block(cot, b), c_v, sem.at[6]).wait()

            @pl.loop(0, units // tile)
            def _(j):
                cols = pl.ds(pl.multiple_of(j * tile, tile), tile)
                gate_pre = jnp.dot(x_v[...], wg_v[:, cols], preferred_element_type=F32)
                up_pre = jnp.dot(x_v[...], wu_v[:, cols], preferred_element_type=F32)
                d_hidden = dot_nt(c_v[...], wd_v[cols, :])
                act, slope = gelu_parts(gate_pre)
                hidden[at, cols] = (act * up_pre).astype(BF16)
                dgate[at, cols] = (d_hidden * up_pre * slope).astype(BF16)
                dup[at, cols] = (d_hidden * act).astype(BF16)

            @pl.when(b < 3)
            def _():
                copy_in(row_block(normed_two, b + 1), x_v, sem.at[5])
                copy_in(row_block(cot, b + 1), c_v, sem.at[6])

        outs = [copy_in(hidden, hidden_o, sem.at[0]), copy_in(dgate, dgate_o, sem.at[1]), copy_in(dup, dup_o, sem.at[2])]
        for item in downs:
            take_rounds(item, first)
        take_rounds(gate, rounds(gate))

        def stage(index, value):
            @pl.loop(0, features // tile)
            def _(j):
                at, cols = pl.ds(pl.multiple_of(index * rows, rows), rows), pl.ds(pl.multiple_of(j * tile, tile), tile)
                part[at, cols] = value(at, cols).astype(BF16)

        def two(at, cols):
            return dot_nt(dgate[at, :], wg_v[cols, :]) + dot_nt(dup[at, :], wu_v[cols, :])

        def out(at, cols):
            return jnp.dot(hidden[at, :], wd_v[:, cols], preferred_element_type=F32)

        reduce = TensorReduce(line, part, from_mate, from_peer, None, got_v, send_v, rs_send, rs_recv, rs_sem)
        stage(line.cross, two)
        reduce.mates[0].start()
        stage(line.peer, two)
        reduce.middle()
        stage(line.mate, two)
        reduce.mates[1].start()
        stage(line.index, two)
        for item in downs:
            take_rounds(item, between)
        for load in loads:
            load.wait()
        gain_grad[...] = jnp.zeros_like(gain_grad)

        def use(at, total):
            back, terms = norm_backward(dmid_v[at, :], gain[...], total)
            value = cot_v[at, :].astype(F32) + back
            dmid_v[at, :] = value
            att_v[at, :] = value.astype(BF16)
            gain_grad[...] += fold_rows(terms)

        reduce.end(use)
        gather.start()
        keep = [copy_in(att_v, gather.block(line.index), sem.at[3]), copy_in(dmid_v, d_middle, sem.at[4])]
        take_rounds(up, rounds(up))
        reduce.drain()

        @pl.loop(0, 4)
        def _(b):
            stage(b, out)
            copy_in(row_block(part, b), row_block(part_out, b), sem.at[7])

        take_rounds(downs[0], last)
        gather.forward()
        for copy in outs + keep:
            copy.wait()
        pltpu.make_async_copy(part, part_out, sem.at[7]).wait()

    weight = pltpu.VMEM((features, units), BF16)
    block = pltpu.VMEM((rows, features), BF16)
    pl.run_scoped(
        tensor_phase,
        weight, weight, pltpu.VMEM((units, features), BF16),
        pltpu.VMEM((tokens, units), BF16), pltpu.VMEM((tokens, units), BF16),
        block, block, pltpu.VMEM((tokens, features), BF16),
        *TensorReduce.buffers(tokens, features),
        pltpu.VMEM((rows, features), F32), block,
    )

    def mixer_phase(gated_v, states_v, conv_v, dgated_v, dri_v, dbranch_v, block_v, w_v, *scratch):
        loads = [copy_in(conv, conv_v, sem.at[1]), copy_in(w_out, w_v, sem.at[0])]
        loads += [copy_in(gated, gated_v, sem.at[2]), copy_in(states, states_v, sem.at[3])]
        mixer = MixerBackward(masks, vecs, w_cat, states_v, gated_v, conv_v, dgated_v, dri_v, dbranch_v, sums, *scratch)
        loads[0].wait()
        mixer.gates()
        take_rounds(downs[1], last)
        loads[1].wait()

        def product_gradient(index, source):
            mixer.a_s[pl.ds(pl.multiple_of(index * rows, rows), rows), :] = dot_nt(source[...], w_v[...])

        product_gradient(line.index, att_v)
        gather.aside.wait_recv()
        mate = copy_in(row_block(att, line.mate), block_v.at[0], sem.at[4])
        peer = copy_in(row_block(att, line.peer), block_v.at[1], sem.at[5])
        mate.wait()
        product_gradient(line.mate, block_v.at[0])
        peer.wait()
        product_gradient(line.peer, block_v.at[1])
        gather.onward.wait_recv()
        copy_in(row_block(att, line.cross), block_v.at[0], sem.at[4]).wait()
        product_gradient(line.cross, block_v.at[0])
        loads[2].wait()
        loads[3].wait()
        mixer.factors(gated_v)
        again = copy_in(branch, gated_v, sem.at[2])
        outs = [copy_in(dgated_v, dgated_o, sem.at[1])]
        mixer.scan()
        mixer.gate_gradients()
        outs.append(copy_in(dri_v, dri_o, sem.at[3]))
        again.wait()
        mixer.convolution()
        outs.append(copy_in(dbranch_v, dbranch_o, sem.at[0]))
        for copy in outs:
            copy.wait()

    pl.run_scoped(
        mixer_phase,
        pltpu.VMEM((tokens, channels), F32),
        pltpu.VMEM((tokens, channels), F32),
        pltpu.VMEM((tokens, channels), BF16),
        pltpu.VMEM((tokens, channels), BF16),
        pltpu.VMEM((tokens, 2 * channels), BF16),
        pltpu.VMEM((tokens, channels), BF16),
        pltpu.VMEM((2, rows, features), BF16),
        pltpu.VMEM((channels, features), BF16),
        *MixerBackward.scratch(tokens, channels),
    )
    gather.drain()
    for item in (*downs, gate, up):
        engine.drain(item, [0])
        engine.wait_last(item, 0)


def middle_part(middle, cot, normed_two, w_gate, w_up, w_down, w_out, gated_pre, branch_pre, states, conv_out, gain, masks, vecs, w_cat):
    n = lax.axis_size("dp")
    tokens, features = cot.shape
    channels, units, width = conv_out.shape[1], w_gate.shape[1], features // n
    rows = tokens // 4
    down = stage_shapes(n, True, width, units // 2)[0]
    gate = stage_shapes(n, False, width, units)[0]
    up = stage_shapes(n, False, width, units // 2)[0]
    dma = pltpu.SemaphoreType.DMA
    block = pltpu.VMEM((rows, features), BF16)
    whole = jax.ShapeDtypeStruct((tokens, features), BF16)
    hide = jax.ShapeDtypeStruct((tokens, units), BF16)
    narrow = jax.ShapeDtypeStruct((tokens, channels), BF16)
    results = [jax.ShapeDtypeStruct((rows, features), F32), whole, hide, hide, hide, narrow]
    results += [jax.ShapeDtypeStruct((tokens, 2 * channels), BF16), narrow, whole, *TensorReduce.results(tokens, features)]
    results += [down[0], down[0], gate[0], up[0]]
    return pl.pallas_call(
        functools.partial(middle_kernel, n, width),
        out_shape=[*results, jax.ShapeDtypeStruct((8, 8, channels), F32), jax.ShapeDtypeStruct((8, features), F32)],
        in_specs=[HBM] * 13 + [IN_VMEM] * 4,
        out_specs=[HBM] * len(results) + [IN_VMEM] * 2,
        scratch_shapes=[
            pltpu.VMEM((tokens, units), BF16), block, *down[1:4], *down[1:4], *gate[1:4], *up[1:4],
            pltpu.VMEM((2, tokens, width), BF16),
            pltpu.VMEM((2, width, units), BF16),
            pltpu.VMEM((width, units), F32),
            *TensorReduce.semaphores(), *TensorGather.semaphores(), dma((8,)), dma((4,)),
        ],
        compiler_params=pltpu.CompilerParams(vmem_limit_bytes=VMEM_BYTES, has_side_effects=True),
        cost_estimate=pl.CostEstimate(flops=50 * 10**9, bytes_accessed=90 * 10**6, transcendentals=8 * tokens * channels),
        name="middle_part",
    )(
        middle, cot, normed_two, w_gate, w_up, w_down, w_out, gated_pre, branch_pre, states, conv_out,
        column_blocks(cot, n), column_blocks(normed_two, n), gain, masks, vecs, w_cat,
    )


def gather_sums(gains, sends, recvs, send_sems, recv_sems):
    n, line = lax.axis_size("dp"), TensorLine()
    hops = [("tensor", line.mate), ("tensor", line.peer)]
    bit = 1
    while bit < n:
        hops.append(("dp", lax.axis_index("dp") ^ bit))
        bit *= 2
    copies = [remote(sends.at[s], recvs.at[s], send_sems.at[s], recv_sems.at[s], *hop) for s, hop in enumerate(hops)]

    def begin(s):
        sends[s] = gains[...] if s == 0 else sends[s - 1] + recvs[s - 1]
        copies[s].start()

    def step(s):
        if s > 0:
            copies[s - 1].wait_recv()
        if s < len(copies):
            begin(s)
        else:
            gains[...] = sends[s - 1] + recvs[s - 1]
            for copy in copies:
                copy.wait_send()

    return [functools.partial(step, s) for s in range(len(copies) + 1)]


def finish_kernel(n, width, plan, order, lefts_of, keep, readies, columns, out_of, *refs):
    take = Reader(refs)
    count, n_outs = len(plan), max(o for o, _ in out_of) + 1
    part_out, middle, d_middle, stream, w_gate, w_branch = take(6)
    gain, gain_grad_two = take(2)
    lefts, rights_hbm = take(max(lefts_of) + 1), take(n_outs)
    shapes = [stage_shapes(n, plan[i], width, columns[i]) for i in range(count)]
    given = [take(readies[i]) for i in range(count)]
    stream_grad_o, stream_out_o = take(2)
    outs = take(n_outs)
    (part,) = take(1)
    reduces = [take(2), take(2)]
    recv = [given[i] + take(len(shapes[i]) - readies[i]) for i in range(count)]
    (gains,) = take(1)
    rights = take(n_outs)
    wg_v, wb_v, stage_v = take(3)
    nones = [[None] * r for r in readies]
    sends = [nones[i] + take(len(shapes[i]) - readies[i]) for i in range(count)]
    send_sems = [nones[i] + take(len(shapes[i]) - readies[i]) for i in range(count)]
    recv_sems = [nones[i] + take(len(shapes[i]) - readies[i]) for i in range(count)]
    left_vs = take(max(lefts_of) + 1)
    left_s, got_s, total_s, out_s, own_v, got_v, send_v, send_w = take(8)
    value_v, base_v, gain_sends, gain_recvs = take(4)
    rs_sems = [take(3), take(3)]
    gain_ss, gain_rs, right_sem, sem, engine_sem, out_sem = take(6)

    line = TensorLine()
    engine = Engine(left_s, got_s, total_s, engine_sem, out_s, out_sem)
    tensor = [
        TensorReduce(line, source, *reduces[q], own_v, got_v, (send_v, send_w)[q], *rs_sems[q])
        for q, source in enumerate((part, part_out))
    ]
    tensor[1].start()
    loads, weights, left_loads = {}, [], {}

    def issue(kind, i):
        if kind == "left" and i in keep and i not in left_loads:
            left_loads[i] = copy_in(lefts[i], left_vs[i], right_sem.at[n_outs + 2 + i])
        if kind == "right" and i not in loads:
            loads[i] = copy_in(rights_hbm[i], rights[i], right_sem.at[i])

    def issue_for(i):
        if i >= 0:
            issue("right", out_of[i][0])
            issue("left", lefts_of[i])
        elif not weights:
            issue("right", n_outs - 2)
            issue("right", n_outs - 1)
            weights.extend([copy_in(w_gate, wg_v, right_sem.at[n_outs]), copy_in(w_branch, wb_v, right_sem.at[n_outs + 1])])

    loaded = set()

    def load_left(i):
        if left_loads.get(i) is not None:
            left_loads[i].wait()
            left_loads[i] = None

    def load(i):
        if i not in loaded:
            loads[i].wait()
            loaded.add(i)

    def columns_of(i):
        return pl.ds(out_of[i][1], columns[i])

    items = [
        Item(
            make_stages(n, plan[i]), lefts[lefts_of[i]], rights[out_of[i][0]].at[:, columns_of(i)], width, readies[i],
            (outs[out_of[i][0]].at[:, columns_of(i)], recv[i], sends[i], send_sems[i], recv_sems[i]),
            left_vs[lefts_of[i]] if lefts_of[i] in keep else None,
        )
        for i in range(count)
    ]

    rows, features = stream.shape

    def stage(index):
        at = pl.ds(pl.multiple_of(index * rows, rows), rows)

        @pl.loop(0, features // 512)
        def _(j):
            cols = pl.ds(pl.multiple_of(j * 512, 512), 512)
            total = dot_nt(rights[n_outs - 2][at, :], wg_v[cols, :]) + dot_nt(rights[n_outs - 1][at, :], wb_v[cols, :])
            stage_v[:, cols] = total.astype(BF16)

        copy_in(stage_v, tensor[0].block(index), sem.at[0]).wait()

    def part_first():
        for i in (n_outs - 2, n_outs - 1):
            load(i)
        for copy in weights:
            copy.wait()
        stage(line.cross)
        tensor[0].mates[0].start()
        stage(line.peer)

    def part_second():
        stage(line.mate)
        tensor[0].mates[1].start()
        stage(line.index)

    def grad_end():
        copies = [copy_in(stream, value_v, sem.at[0]), copy_in(d_middle, base_v, sem.at[1])]
        for copy in copies:
            copy.wait()
        gains[...] = jnp.zeros_like(gains)

        def use(at, total):
            back, terms = norm_backward(value_v[at, :].astype(F32), gain[...], total)
            base_v[at, :] = base_v[at, :] + back
            gains[...] += fold_rows(terms)

        tensor[0].end(use)
        copy_in(base_v, stream_grad_o, sem.at[0]).wait()
        first = jnp.sum(gains[...], axis=0, keepdims=True)
        second = jnp.sum(gain_grad_two[...], axis=0, keepdims=True)
        pick = lax.broadcasted_iota(jnp.int32, gains.shape, 0)
        gains[...] = jnp.where(pick == 0, first, jnp.where(pick == 1, second, 0.0))

    def out_end():
        copy_in(middle, base_v, sem.at[0]).wait()

        def use(at, total):
            base_v[at, :] = base_v[at, :] + total

        tensor[1].end(use)
        copy_in(base_v, stream_out_o, sem.at[0]).wait()

    extra = [part_first, tensor[0].middle, part_second, tensor[1].middle, grad_end, out_end]
    extra += gather_sums(gains, gain_sends, gain_recvs, gain_ss, gain_rs)
    for at, (i, t, k) in enumerate(order):
        for ahead in order[at : at + 3]:
            issue_for(ahead[0])
        if i < 0:
            if extra:
                extra.pop(0)()
            continue
        load(out_of[i][0])
        load_left(lefts_of[i])
        if t < len(shapes[i]):
            engine.round(items[i], t, k)
        else:
            engine.finish(items[i])
    for step in extra:
        step()
    engine.settle()
    for i, item in enumerate(items):
        engine.drain(item, range(readies[i], len(shapes[i])))
    for reduce in tensor:
        reduce.drain()


def task_order(plan, readies, names, n):
    tasks = []
    for last_first, ready in zip(plan, readies):
        sizes = digit_sizes(n)
        if last_first:
            sizes = sizes[1:] + sizes[:1]
        i = len(tasks)
        tasks.append([(i, t, k) for t, m in enumerate(sizes) for k in range(1, m) if t >= ready] + [(i, len(sizes), 0)])
    out, at = [], [0] * len(plan)
    for i in names:
        if i < 0:
            out.append((-1, 0, 0))
        elif at[i] < len(tasks[i]):
            out.append(tasks[i][at[i]])
            at[i] += 1
    for i in range(len(plan)):
        out += tasks[i][at[i] :]
    return out


def finish(part_out, middle, d_middle, stream, w_gate, w_branch, gain, gain_grad_two, lefts, lefts_of, rights, given, plan, out_of, names, keep):
    n = lax.axis_size("dp")
    tokens, features = part_out.shape
    width, rows = features // n, tokens // 4
    readies = [len(g) for g in given]
    pieces = [sum(o == q for o, _ in out_of) for q in range(len(rights))]
    columns = [rights[o].shape[1] // pieces[o] for o, _ in out_of]
    out_of = [(o, q * c) for (o, q), c in zip(out_of, columns)]
    widest = max(columns)
    keep = () if width % LANES else keep
    shapes = [stage_shapes(n, last_first, width, c)[ready:] for last_first, c, ready in zip(plan, columns, readies)]
    steps = 2 + (n - 1).bit_length()
    dma = pltpu.SemaphoreType.DMA
    stream_shape = jax.ShapeDtypeStruct((rows, features), F32)
    out_shape = [stream_shape, stream_shape] + [jax.ShapeDtypeStruct((width, r.shape[1]), F32) for r in rights]
    out_shape += [jax.ShapeDtypeStruct((tokens, features), BF16)]
    out_shape += TensorReduce.results(tokens, features) * 2 + [s[0] for item in shapes for s in item]
    results = pl.pallas_call(
        functools.partial(finish_kernel, n, width, plan, task_order(plan, readies, names, n), lefts_of, keep, readies, columns, out_of),
        out_shape=[*out_shape, jax.ShapeDtypeStruct((8, features), F32)],
        in_specs=[HBM] * 6 + [IN_VMEM] * 2 + [HBM] * (len(lefts) + len(rights) + sum(readies)),
        out_specs=[HBM] * len(out_shape) + [IN_VMEM],
        scratch_shapes=[
            *[pltpu.VMEM(r.shape, BF16) for r in rights],
            pltpu.VMEM(w_gate.shape, BF16), pltpu.VMEM(w_branch.shape, BF16), pltpu.VMEM((rows, features), BF16),
            *[s[1] for item in shapes for s in item],
            *[s[2] for item in shapes for s in item],
            *[s[3] for item in shapes for s in item],
            *[pltpu.VMEM((tokens, features) if i in keep else (8, features), BF16) for i in range(len(lefts))],
            pltpu.VMEM((2, tokens, width), BF16),
            pltpu.VMEM((2 * len(digit_sizes(n)), width, widest), BF16),
            pltpu.VMEM((width, widest), F32), pltpu.VMEM((width, widest), F32),
            pltpu.VMEM((rows, features), BF16), *TensorReduce.buffers(tokens, features),
            pltpu.VMEM((rows, features), BF16),
            pltpu.VMEM((rows, features), BF16),
            pltpu.VMEM((rows, features), F32),
            pltpu.VMEM((steps, 8, features), F32),
            pltpu.VMEM((steps, 8, features), F32),
            *TensorReduce.semaphores(),
            *TensorReduce.semaphores(),
            dma((steps,)), dma((steps,)), dma((len(rights) + 2 + len(lefts),)), dma((2,)), dma((2 + 2 * len(digit_sizes(n)),)), dma,
        ],
        compiler_params=pltpu.CompilerParams(vmem_limit_bytes=VMEM_BYTES, has_side_effects=True),
        cost_estimate=pl.CostEstimate(
            flops=2 * tokens * features * sum(columns), bytes_accessed=4 * features * sum(columns), transcendentals=0
        ),
        name="finish",
    )(
        part_out, middle, d_middle, stream, w_gate, w_branch, gain, gain_grad_two,
        *[column_blocks(v, n) for v in lefts], *rights, *[g for item in given for g in item],
    )
    return results[0], results[1], results[2 : 2 + len(rights)], results[-1]


class TensorGather:
    def __init__(self, line, own_v, out, send_sem, recv_sem):
        self.line, self.own_v, self.out, self.rows = line, own_v, out, own_v.shape[0]
        self.over = remote(own_v, self.block(line.index), send_sem.at[0], recv_sem.at[0], "tensor", line.peer)
        self.aside = remote(own_v, self.block(line.index), send_sem.at[1], recv_sem.at[1], "tensor", line.mate)
        self.onward = remote(self.block(line.peer), self.block(line.peer), send_sem.at[2], recv_sem.at[2], "tensor", line.mate)

    def block(self, index):
        return self.out.at[pl.ds(pl.multiple_of(index * self.rows, self.rows), self.rows)]

    def start(self):
        self.over.start()
        self.aside.start()

    def forward(self):
        self.over.wait_recv()
        self.onward.start()

    def drain(self):
        for copy in (self.over, self.aside, self.onward):
            copy.wait_send()

    @staticmethod
    def semaphores():
        return [pltpu.SemaphoreType.DMA((3,)), pltpu.SemaphoreType.DMA((3,))]


def forward_kernel(*refs):
    take = Reader(refs)
    cot_own, w_gate, w_branch, w_out = take(4)
    stream, gain, gain_two, masks, vecs, w_cat = take(6)
    normed, cot, gated_o, branch_o, conv_o, states_o, product_o, middle_o, normed_two, from_mate, from_peer = take(11)
    wg_v, wb_v, wo_v, own_v, cot_v, block_v, gated_v, branch_v, conv_v, states_v, product_v = take(11)
    pre_s, a_s, b_s, part_v, rs_got, rs_send_v, middle_v, two_v = take(8)
    ag_sems, cot_sems, two_sems = take(2), take(2), take(2)
    rs_send, rs_recv, rs_sem, sem = take(4)
    rows, features = stream.shape
    line = TensorLine()
    gather = TensorGather(line, own_v, normed, *ag_sems)
    cots = TensorGather(line, cot_v, cot, *cot_sems)
    twos = TensorGather(line, two_v, normed_two, *two_sems)
    reduce = TensorReduce(line, part_v, from_mate, from_peer, None, rs_got, rs_send_v, rs_send, rs_recv, rs_sem)
    loads = [copy_in(w_gate, wg_v, sem.at[0]), copy_in(w_branch, wb_v, sem.at[1]), copy_in(w_out, wo_v, sem.at[2])]
    cot_load = copy_in(cot_own, cot_v, sem.at[3])

    def chunks(body):
        @pl.loop(0, rows // 16)
        def _(r):
            body(pl.ds(pl.multiple_of(r * 16, 16), 16))

    def norm(values, gains):
        inverse = lax.rsqrt(jnp.mean(values * values, axis=-1, keepdims=True) + epsilon)
        return (values * inverse * gains).astype(BF16)

    def first_norm(at):
        own_v[at, :] = norm(stream[at, :].astype(F32), gain[...])

    chunks(first_norm)
    gather.start()
    keep = [copy_in(own_v, gather.block(line.index), sem.at[4])]
    cot_load.wait()
    cots.start()
    keep.append(copy_in(cot_v, cots.block(line.index), sem.at[5]))

    def project(source, index):
        at = pl.ds(pl.multiple_of(index * rows, rows), rows)
        branch_v[at, :] = jnp.dot(source, wb_v[...], preferred_element_type=F32)
        gated_v[at, :] = jnp.dot(source, wg_v[...], preferred_element_type=F32)

    loads[0].wait()
    loads[1].wait()
    project(own_v[...], line.index)
    gather.aside.wait_recv()
    copy_in(gather.block(line.mate), block_v.at[0], sem.at[6]).wait()
    project(block_v[0], line.mate)
    gather.forward()
    copy_in(gather.block(line.peer), block_v.at[1], sem.at[6]).wait()
    project(block_v[1], line.peer)
    gather.onward.wait_recv()
    copy_in(gather.block(line.cross), block_v.at[0], sem.at[6]).wait()
    project(block_v[0], line.cross)
    outs = [copy_in(branch_v, branch_o, sem.at[7]), copy_in(gated_v, gated_o, sem.at[8])]
    mixer_forward_kernel(branch_v, gated_v, masks, vecs, w_cat, conv_v, states_v, product_v, pre_s, a_s, b_s)
    outs += [copy_in(conv_v, conv_o, sem.at[9]), copy_in(states_v, states_o, sem.at[10]), copy_in(product_v, product_o, sem.at[11])]
    loads[2].wait()

    def out_block(index):
        at = pl.ds(pl.multiple_of(index * rows, rows), rows)
        part_v[at, :] = jnp.dot(product_v[at, :], wo_v[...], preferred_element_type=F32).astype(BF16)

    out_block(line.cross)
    reduce.mates[0].start()
    out_block(line.peer)
    reduce.middle()
    out_block(line.mate)
    reduce.mates[1].start()
    out_block(line.index)
    cots.forward()

    def second_norm(at, total):
        values = stream[at, :].astype(F32) + total
        middle_v[at, :] = values
        two_v[at, :] = norm(values, gain_two[...])

    reduce.end(second_norm)
    twos.start()
    keep += [copy_in(two_v, twos.block(line.index), sem.at[12]), copy_in(middle_v, middle_o, sem.at[13])]
    cots.aside.wait_recv()
    cots.onward.wait_recv()
    twos.forward()
    twos.aside.wait_recv()
    twos.onward.wait_recv()
    for copy in keep + outs:
        copy.wait()
    for gathered in (gather, cots, twos):
        gathered.drain()
    reduce.drain()


def forward(cot_own, w_gate, w_branch, w_out, stream, gain, gain_two, masks, vecs, w_cat):
    rows, features = stream.shape
    tokens, channels = 4 * rows, w_gate.shape[1]
    lanes = channels // LANES
    whole = jax.ShapeDtypeStruct((tokens, features), BF16)
    wide = jax.ShapeDtypeStruct((tokens, channels), F32)
    narrow = jax.ShapeDtypeStruct((tokens, channels), BF16)
    results = [whole, whole, wide, wide, narrow, wide, narrow, jax.ShapeDtypeStruct((rows, features), F32), whole]
    results += TensorReduce.results(tokens, features)
    block = pltpu.VMEM((rows, features), BF16)
    return pl.pallas_call(
        forward_kernel,
        out_shape=results,
        in_specs=[HBM] * 4 + [IN_VMEM] * 6,
        out_specs=[HBM] * len(results),
        scratch_shapes=[
            pltpu.VMEM(w_gate.shape, BF16), pltpu.VMEM(w_branch.shape, BF16), pltpu.VMEM(w_out.shape, BF16),
            block, block, pltpu.VMEM((2, rows, features), BF16),
            pltpu.VMEM((tokens, channels), F32), pltpu.VMEM((tokens, channels), F32),
            pltpu.VMEM((tokens, channels), BF16), pltpu.VMEM((tokens, channels), F32), pltpu.VMEM((tokens, channels), BF16),
            pltpu.VMEM((tokens, 2 * channels), F32),
            pltpu.VMEM((lanes, tokens, LANES), F32), pltpu.VMEM((lanes, tokens, LANES), F32),
            pltpu.VMEM((tokens, features), BF16), *TensorReduce.buffers(tokens, features),
            pltpu.VMEM((rows, features), F32), block,
            *TensorGather.semaphores(), *TensorGather.semaphores(), *TensorGather.semaphores(),
            *TensorReduce.semaphores(), pltpu.SemaphoreType.DMA((14,)),
        ],
        compiler_params=pltpu.CompilerParams(vmem_limit_bytes=VMEM_BYTES, has_side_effects=True),
        cost_estimate=pl.CostEstimate(flops=9 * 10**9, bytes_accessed=40 * 10**6, transcendentals=6 * tokens * channels),
        name="forward",
    )(cot_own, w_gate, w_branch, w_out, stream, gain, gain_two, masks, vecs, w_cat)

DP_PLAN = [True, True, False, False, False, False, False, False]
DP_OUTS = [(0, 0), (0, 1), (1, 0), (2, 0), (2, 1), (3, 0), (4, 0), (5, 0)]
DP_ORDER = [3, 6, 2, -1, 5, -1, 3, 3, 7, 6, -1, -1, 2, 6, -1, 2, 4, -1, 7, -1, 1, 5, 7, 3, 5, 2, -1, 6, 4, 7, -1, -1, 1, 6, 4, 0, -1, 5, 7, 4, -1, 5, 0, 4]


def dot(left, right, dims, out=F32):
    return lax.dot_general(left, right, (dims, ((), ())), preferred_element_type=F32).astype(out)


def spread_heads(*weights):
    heads, width = weights[0].shape[:2]
    total = len(weights) * heads * width
    rows = []
    for h in range(heads):
        row = 0
        for q, weight in enumerate(weights):
            before = (q * heads + h) * width
            row = row + jnp.pad(weight[h], ((0, 0), (before, total - before - width)))
        rows.append(row)
    return jnp.concatenate(rows)


def head_blocks(dense, heads, width):
    return jnp.stack([dense[h * width : (h + 1) * width, h * width : (h + 1) * width] for h in range(heads)])


def on_device(
    stream_in, segments, first_gain, gelu_gate_weight, recurrent_branch_weight, conv_kernel, conv_bias, recur_weight, recur_bias,
    inlet_weight, inlet_bias, decay_param, recurrent_output_weight, second_gain, gate_projection_weight, up_projection_weight,
    down_projection_weight, cotangent,
):
    seq_len = segments.shape[1]
    heads, head_width = recur_weight.shape[:2]
    ids = jnp.pad(segments[0], (3, 8), constant_values=-1)
    same = [(ids[3 - k : 3 - k + seq_len] == segments[0]).astype(F32) for k in range(1, 4)]
    masks = jnp.pad(jnp.stack(same, axis=1), ((0, 8), (0, 5)))
    softplus = jax.nn.softplus(-decay_param)
    vecs = jnp.concatenate([conv_kernel, jnp.stack([conv_bias, recur_bias, inlet_bias, softplus])])
    w_cat = spread_heads(recur_weight, inlet_weight)

    normed, cot, gated_pre, branch_pre, conv_out, states, product, middle, normed_two, _, _ = forward(
        cotangent[0], gelu_gate_weight, recurrent_branch_weight, recurrent_output_weight, stream_in[0], first_gain[None],
        second_gain[None], masks, vecs, w_cat,
    )
    (
        d_middle, d_attended, hidden, d_gate, d_up, d_gated, d_ri, d_branch, part_out, _, _, *gots, sums, gain_two,
    ) = middle_part(
        middle, cot, normed_two, gate_projection_weight, up_projection_weight, down_projection_weight, recurrent_output_weight,
        gated_pre, branch_pre, states, conv_out, second_gain[None], masks, vecs, w_cat,
    )
    stream_grad, stream_out, gradients, gains = finish(
        part_out, middle, d_middle, stream_in[0], gelu_gate_weight, recurrent_branch_weight, first_gain[None], gain_two,
        [cot, normed_two, d_attended, normed], [0, 0, 1, 1, 1, 2, 3, 3], [hidden, d_gate, d_up, product, d_gated, d_branch],
        [*([g] for g in gots), [], [], [], []], DP_PLAN, DP_OUTS, DP_ORDER, (1, 3),
    )
    down_gradient, gate_gradient, up_gradient, output_gradient, gated_gradient, branch_gradient = gradients

    width = heads * head_width
    dense = dot(conv_out, d_ri, ((0,), (0,)))
    grad_recur = head_blocks(dense[:, :width], heads, head_width)
    grad_inlet = head_blocks(dense[:, width:], heads, head_width)
    sums = jnp.sum(sums, axis=1)
    small = jnp.concatenate([sums.reshape(-1), grad_recur.reshape(-1), grad_inlet.reshape(-1)])
    small = lax.psum(small.astype(BF16), "dp").astype(F32)
    sums = small[: 8 * width].reshape(8, width)
    grad_recur, grad_inlet = small[8 * width :].reshape(2, heads, head_width, head_width)
    grad_decay = decay_scale * jax.nn.sigmoid(-decay_param) * sums[7]
    return (
        stream_out[None], stream_grad[None], gains[0], gated_gradient, branch_gradient, sums[:4], sums[4], grad_recur, sums[5],
        grad_inlet, sums[6], grad_decay, output_gradient.T, gains[1], gate_gradient, up_gradient, down_gradient.T,
    )


def solution(mesh):
    in_specs = (
        P("dp", "tensor", None),
        P("dp", None),
        P(),
        P(None, "tensor"),
        P(None, "tensor"),
        P(None, "tensor"),
        P("tensor"),
        P("tensor", None, None),
        P("tensor"),
        P("tensor", None, None),
        P("tensor"),
        P("tensor"),
        P("tensor", None),
        P(),
        P(None, "tensor"),
        P(None, "tensor"),
        P("tensor", None),
        P("dp", "tensor", None),
    )
    out_specs = (
        P("dp", "tensor", None),
        P("dp", "tensor", None),
        P(),
        P("dp", "tensor"),
        P("dp", "tensor"),
        P(None, "tensor"),
        P("tensor"),
        P("tensor", None, None),
        P("tensor"),
        P("tensor", None, None),
        P("tensor"),
        P("tensor"),
        P("tensor", "dp"),
        P(),
        P("dp", "tensor"),
        P("dp", "tensor"),
        P("tensor", "dp"),
    )
    return jax.shard_map(
        on_device, mesh=mesh, in_specs=in_specs, out_specs=out_specs, check_vma=False
    )
```

```python
import functools

import jax
import jax.numpy as jnp
from jax import lax
from jax.experimental import pallas as pl
from jax.experimental.pallas import tpu as pltpu
from jax.sharding import PartitionSpec as P

epsilon = 1e-06
decay_scale = 8.0
LANES = 128
GELU_C = 0.7978845608028654
GELU_K = 0.044715
F32 = jnp.float32
BF16 = jnp.bfloat16
VMEM_BYTES = 60 * 1024 * 1024


def minus_expm1(y, exp_y):
    s = 1.0 + y * (1.0 / 9.0)
    for d in range(8, 1, -1):
        s = 1.0 + (y * (1.0 / d)) * s
    return jnp.where(y > -0.5, -y * s, 1.0 - exp_y)


def gelu_parts(v):
    v2 = v * v
    t = jnp.tanh(GELU_C * v * (1.0 + GELU_K * v2))
    half = 0.5 * (1.0 + t)
    slope = half + 0.5 * v * (1.0 - t * t) * (GELU_C * (1.0 + 3.0 * GELU_K * v2))
    return v * half, slope


def lane_tiles(width):
    return [slice(j * LANES, (j + 1) * LANES) for j in range(width // LANES)]


def fold_rows(v):
    return jnp.sum(v.reshape(v.shape[0] // 8, 8, v.shape[1]), axis=0)


def gates_pre(rows, step, conv_ref, w_ref, pre_s):
    @pl.loop(0, rows // step)
    def _(i):
        r = pl.ds(pl.multiple_of(i * step, step), step)
        pre_s[r, :] = jnp.dot(conv_ref[r, :], w_ref[...], preferred_element_type=F32)


def mixer_forward_kernel(branch_ref, gated_ref, mask_ref, vec_ref, w_ref, conv_ref, states_ref, product_ref, pre_s, a_s, b_s):
    rows, width = branch_ref.shape
    seg = rows // 8
    tiles = lane_tiles(width)

    @pl.loop(0, 8)
    def _(s):
        t0 = pl.multiple_of(s * seg, seg)
        before = pl.multiple_of(jnp.maximum(t0 - 8, 0), 8)
        same = [mask_ref[pl.ds(t0, seg), k : k + 1] for k in range(3)]
        for cols in tiles:
            b = branch_ref[pl.ds(t0, seg), cols]
            ext = jnp.concatenate([branch_ref[pl.ds(before, 8), cols], b], axis=0)
            out = vec_ref[4:5, cols] + vec_ref[0:1, cols] * b
            for k in range(1, 4):
                out = out + vec_ref[k : k + 1, cols] * pltpu.roll(ext, k, 0)[8:] * same[k - 1]
            conv_ref[pl.ds(t0, seg), cols] = out.astype(BF16)

    gates_pre(rows, 256, conv_ref, w_ref, pre_s)

    @pl.loop(0, 8)
    def _(s):
        t0 = pl.multiple_of(s * seg, seg)
        c = mask_ref[pl.ds(t0, seg), 0:1]
        for j, cols in enumerate(tiles):
            cols_i = slice(width + j * LANES, width + (j + 1) * LANES)
            r = jax.nn.sigmoid(pre_s[pl.ds(t0, seg), cols] + vec_ref[5:6, cols])
            i = jax.nn.sigmoid(pre_s[pl.ds(t0, seg), cols_i] + vec_ref[6:7, cols])
            log_a = (-decay_scale * vec_ref[7:8, cols]) * r
            a = jnp.exp(log_a)
            n = jnp.sqrt(minus_expm1(2.0 * log_a, a * a))
            mult = (1.0 - c) + c * n
            a_s[j, pl.ds(t0, seg), :] = a * c
            b_s[j, pl.ds(t0, seg), :] = mult * i * conv_ref[pl.ds(t0, seg), cols].astype(F32)

    row = lax.broadcasted_iota(jnp.int32, (8, LANES), 0)

    def scan_step(i, carry):
        at = pl.ds(pl.multiple_of(i * 8, 8), 8)
        out = []
        for j, cols in enumerate(tiles):
            a, b = a_s[j, at, :], b_s[j, at, :]
            for s in (1, 2, 4):
                b = b + a * jnp.where(row >= s, pltpu.roll(b, s, 0), 0.0)
                a = a * jnp.where(row >= s, pltpu.roll(a, s, 0), 1.0)
            b = b + a * carry[j]
            states_ref[at, cols] = b
            out.append(jnp.broadcast_to(b[7:8, :], (8, LANES)))
        return tuple(out)

    lax.fori_loop(0, rows // 8, scan_step, tuple(jnp.zeros((8, LANES), F32) for _ in tiles), unroll=4)

    @pl.loop(0, 8)
    def _(s):
        at = pl.ds(pl.multiple_of(s * seg, seg), seg)
        for cols in tiles:
            act, _ = gelu_parts(gated_ref[at, cols])
            product_ref[at, cols] = (states_ref[at, cols] * act).astype(BF16)


class MixerBackward:
    def __init__(self, masks, vecs, w_cat, states, branch, conv, dgated, dri, dbranch, sums, pre_s, a_s, n_s, ac_s, e_s):
        self.masks, self.vecs, self.w_cat, self.states, self.branch, self.conv = masks, vecs, w_cat, states, branch, conv
        self.dgated, self.dri, self.dbranch, self.sums = dgated, dri, dbranch, sums
        self.pre_s, self.a_s, self.n_s, self.ac_s, self.e_s = pre_s, a_s, n_s, ac_s, e_s
        self.rows, self.width = states.shape
        self.seg = self.rows // 8
        self.tiles = lane_tiles(self.width)

    @staticmethod
    def scratch(rows, width):
        lanes = width // LANES
        return [
            pltpu.VMEM((rows, 2 * width), F32),
            pltpu.VMEM((rows, width), F32),
            pltpu.VMEM((rows + 8, width), F32),
            pltpu.VMEM((lanes, rows, LANES), F32),
            pltpu.VMEM((lanes, rows, LANES), F32),
        ]

    def gates(self):
        self.sums[...] = jnp.zeros_like(self.sums)
        gates_pre(self.rows, 256, self.conv, self.w_cat, self.pre_s)

    def factors(self, gated):
        @pl.loop(0, 8)
        def _(s):
            t0 = pl.multiple_of(s * self.seg, self.seg)
            at = pl.ds(t0, self.seg)
            c = self.masks[at, 0:1]
            for j, cols in enumerate(self.tiles):
                cols_i = slice(self.width + j * LANES, self.width + (j + 1) * LANES)
                r = jax.nn.sigmoid(self.pre_s[at, cols] + self.vecs[5:6, cols])
                self.pre_s[at, cols] = r
                self.pre_s[at, cols_i] = jax.nn.sigmoid(self.pre_s[at, cols_i] + self.vecs[6:7, cols])
                log_a = (-decay_scale * self.vecs[7:8, cols]) * r
                a = jnp.exp(log_a)
                d = self.a_s[at, cols]
                self.a_s[at, cols] = a
                self.n_s[at, cols] = jnp.sqrt(minus_expm1(2.0 * log_a, a * a))
                self.ac_s[j, at, :] = a * c
                act, slope = gelu_parts(gated[at, cols])
                self.e_s[j, at, :] = d * act
                self.dgated[at, cols] = (d * self.states[at, cols] * slope).astype(BF16)

    def scan(self):
        row = lax.broadcasted_iota(jnp.int32, (8, LANES), 0)

        def step(q, carry):
            at = pl.ds(pl.multiple_of((self.rows // 8 - 1 - q) * 8, 8), 8)
            out = []
            for j in range(len(self.tiles)):
                e, later = carry[j]
                now = self.ac_s[j, at, :]
                a = jnp.where(row == 7, later, pltpu.roll(now, 7, 0))
                b = self.e_s[j, at, :]
                for s in (1, 2, 4):
                    b = b + a * jnp.where(row < 8 - s, pltpu.roll(b, 8 - s, 0), 0.0)
                    a = a * jnp.where(row < 8 - s, pltpu.roll(a, 8 - s, 0), 1.0)
                b = b + a * e
                self.e_s[j, at, :] = b
                out.append((jnp.broadcast_to(b[0:1, :], (8, LANES)), jnp.broadcast_to(now[0:1, :], (8, LANES))))
            return tuple(out)

        none = jnp.zeros((8, LANES), F32)
        lax.fori_loop(0, self.rows // 8, step, tuple((none, none) for _ in self.tiles), unroll=4)

    def gate_gradients(self):
        seg, width = self.seg, self.width

        @pl.loop(0, 8)
        def _(s):
            t0 = pl.multiple_of(s * seg, seg)
            at = pl.ds(t0, seg)
            before = pl.multiple_of(jnp.maximum(t0 - 8, 0), 8)
            c = self.masks[at, 0:1]
            for j, cols in enumerate(self.tiles):
                cols_i = slice(width + j * LANES, width + (j + 1) * LANES)
                e = self.e_s[j, at, :]
                ext = jnp.concatenate([self.states[pl.ds(before, 8), cols], self.states[at, cols]], axis=0)
                earlier = pltpu.roll(ext, 1, 0)[8:]
                r, i, a, n = self.pre_s[at, cols], self.pre_s[at, cols_i], self.a_s[at, cols], self.n_s[at, cols]
                cv = self.conv[at, cols].astype(F32)
                ec = e * c
                d_log = a * (ec * earlier) - ec * i * cv * (a * a / n)
                rr = d_log * r
                dr = ((-decay_scale * self.vecs[7:8, cols]) * rr * (1.0 - r)).astype(BF16)
                em = e * ((1.0 - c) + c * n) * i
                di = (em * cv * (1.0 - i)).astype(BF16)
                self.dri[at, cols] = dr
                self.dri[at, cols_i] = di
                self.n_s[at, cols] = em
                self.sums[5, :, cols] += fold_rows(dr.astype(F32))
                self.sums[6, :, cols] += fold_rows(di.astype(F32))
                self.sums[7, :, cols] += fold_rows(rr)

        @pl.loop(0, self.rows // 256)
        def _(i):
            at = pl.ds(pl.multiple_of(i * 256, 256), 256)
            self.n_s[at, :] += dot_nt(self.dri[at, :], self.w_cat[...])

        self.n_s[self.rows : self.rows + 8, :] = jnp.zeros((8, width), F32)

    def convolution(self):
        @pl.loop(0, 8)
        def _(s):
            t0 = pl.multiple_of(s * self.seg, self.seg)
            at, ext = pl.ds(t0, self.seg), pl.ds(t0, self.seg + 8)
            same = [self.masks[ext, k : k + 1] for k in range(3)]
            for cols in self.tiles:
                d = self.n_s[ext, cols]
                b = self.branch[at, cols]
                self.sums[4, :, cols] += fold_rows(d[: self.seg])
                self.sums[0, :, cols] += fold_rows(d[: self.seg] * b)
                total = self.vecs[0:1, cols] * d[: self.seg]
                for k in range(1, 4):
                    moved = pltpu.roll(d * same[k - 1], self.seg + 8 - k, 0)[: self.seg]
                    total = total + self.vecs[k : k + 1, cols] * moved
                    self.sums[k, :, cols] += fold_rows(moved * b)
                self.dbranch[at, cols] = total.astype(BF16)


def dot_nt(left, right):
    return lax.dot_general(left, right, (((1,), (1,)), ((), ())), preferred_element_type=F32)


class Stage:
    def __init__(self, stride, size, later):
        self.stride, self.size, self.later = stride, size, later
        self.blocks = 1
        for s in later:
            self.blocks *= s.size
        self.digit = lax.rem(lax.axis_index("dp") // stride, size)

    def offset(self, position):
        total = 0
        for s in reversed(self.later):
            total = total + lax.rem(position, s.size) * s.stride
            position = position // s.size
        return total


def digit_sizes(n):
    if n == 8:
        return [2, 4]
    sizes = []
    while n > 1:
        m = 4 if n % 4 == 0 else 2 if n % 2 == 0 else n
        sizes.append(m)
        n //= m
    return sizes


def make_stages(n, last_first):
    digits, stride = [], 1
    for m in digit_sizes(n):
        digits.append((stride, m))
        stride *= m
    if last_first:
        digits = digits[1:] + digits[:1]
    stages = []
    for stride, m in reversed(digits):
        stages.insert(0, Stage(stride, m, list(stages)))
    return stages


class Item:
    def __init__(self, stages, left, right, width, ready, refs, resident=None):
        self.stages, self.left, self.right, self.width, self.ready = stages, left, right, width, ready
        self.resident = resident
        self.columns = right.shape[1]
        self.out, self.recv, self.send, self.send_sem, self.recv_sem = refs

    def message(self, t, back, k, slot, rows=None):
        stage = self.stages[t]
        rows = pl.ds(0, stage.blocks * self.width) if rows is None else rows
        step = jnp.where(back, -stage.stride, stage.stride)
        return pltpu.make_async_remote_copy(
            src_ref=self.send[t].at[slot, rows],
            dst_ref=self.recv[t].at[back, k - 1, rows],
            send_sem=self.send_sem[t].at[slot],
            recv_sem=self.recv_sem[t].at[back, k - 1],
            device_id={"dp": lax.axis_index("dp") + step},
            device_id_type=pl.DeviceIdType.MESH,
        )


class Engine:
    def __init__(self, left_s, got_s, total_s, sem, out_s=None, out_sem=None):
        self.left_s, self.got_s, self.total_s, self.sem = left_s, got_s, total_s, sem
        self.out_s, self.out_sem, self.finished = out_s, out_sem, None

    def fetch(self, item, block, slot):
        if len(item.left.shape) == 3:
            source = item.left.at[block]
        else:
            size = max(item.width, LANES)
            source = item.left.at[:, pl.ds(pl.multiple_of(block // (size // item.width) * size, size), size)]
        return pltpu.make_async_copy(source, self.left_s.at[slot], self.sem.at[slot])

    def columns(self, item, block, slot):
        held = self.left_s[slot]
        if held.shape[1] == item.width:
            return held
        pieces = [held[:, i * item.width : (i + 1) * item.width] for i in range(held.shape[1] // item.width)]
        value = pieces[0]
        for i, piece in enumerate(pieces[1:], 1):
            value = jnp.where(lax.rem(block, len(pieces)) == i, piece, value)
        return value

    def products(self, item, count, block_of, store):
        if item.resident is not None:

            @pl.loop(0, count)
            def _(p):
                cols = pl.ds(pl.multiple_of(block_of(p) * item.width, item.width), item.width)
                store(p, dot_tn(item.resident[:, cols], item.right[...]))

            return
        self.fetch(item, block_of(0), 0).start()

        @pl.loop(0, count)
        def _(p):
            slot = lax.rem(p, 2)
            if count > 1:

                @pl.when(p + 1 < count)
                def _():
                    self.fetch(item, block_of(p + 1), 1 - slot).start()

            self.fetch(item, block_of(p), slot).wait()
            store(p, dot_tn(self.columns(item, block_of(p), slot), item.right[...]))

    def got_copy(self, item, i, source):
        return pltpu.make_async_copy(source, self.got_s.at[i, :, pl.ds(0, item.columns)], self.sem.at[2 + i])

    def start_gots(self, item, first, gots):
        for i, (condition, source) in enumerate(gots):

            @pl.when(condition)
            def _(i=i, source=source):
                self.got_copy(item, first + i, source).start()

    def add_gots(self, item, gots, put):
        for i, (condition, source) in enumerate(gots):

            @pl.when(condition)
            def _(i=i, source=source):
                self.got_copy(item, i, source).wait()

        @pl.loop(0, item.width // 16)
        def _(r):
            at = pl.ds(pl.multiple_of(r * 16, 16), 16)
            total = self.total_s[at, pl.ds(0, item.columns)]
            for i, (condition, _) in enumerate(gots):
                total = total + jnp.where(condition, self.got_s[i, at, pl.ds(0, item.columns)].astype(F32), 0.0)
            put(at, total)

    def arrived(self, item, t, position):
        found, last_found = [], []
        for u in range(t):
            stage = item.stages[u]
            spot = position
            scale = 1
            for s in item.stages[t:]:
                scale *= s.size
            lead = 0
            for s in item.stages[u + 1 : t]:
                lead = lead * s.size + s.digit
            rows = pl.ds((lead * scale + spot) * item.width, item.width)
            last = stage.size - 2
            if stage.size == 2:
                back = jnp.where(stage.digit == 0, 1, 0)
                (last_found if u == t - 1 else found).append((stage.digit >= 0, item.recv[u].at[back, last, rows]))
            else:
                (last_found if u == t - 1 else found).append((stage.digit >= 1, item.recv[u].at[0, last, rows]))
                (last_found if u == t - 1 else found).append((stage.digit <= stage.size - 2, item.recv[u].at[1, last, rows]))
        return found, last_found

    def own_base(self, item, t):
        base = 0
        for s in item.stages[:t]:
            base = base + s.digit * s.stride
        return base

    def wait_last(self, item, t):
        if t < item.ready:
            return
        stage = item.stages[t]
        for back in range(2):
            me = stage.digit if back == 0 else stage.size - 1 - stage.digit

            @pl.when(me >= 1)
            def _(back=back):
                item.message(t, back, stage.size - 1, 0).wait_recv()

    def round(self, item, t, k):
        stage = item.stages[t]
        base = self.own_base(item, t)
        alone = t == 0 and k == 1
        if k == 1 and t > 0:
            self.wait_last(item, t - 1)

        @pl.loop(0, 2)
        def _(back):
            me = jnp.where(back == 0, stage.digit, stage.size - 1 - stage.digit)
            there = me + stage.size - k
            value = jnp.where(back == 0, there, stage.size - 1 - there)
            slot = jnp.where(value > stage.digit, value - 1, value)

            def rows_of(p):
                return pl.ds(pl.multiple_of(p * item.width, item.width), item.width)

            def gots_of(p):
                earlier = sum(self.arrived(item, t, value * stage.blocks + p), [])
                return earlier, [(me >= 1, item.recv[t].at[back, k - 2, rows_of(p)])] if k > 1 else []

            @pl.when(me <= k - 1)
            def _():
                if not alone:
                    self.start_gots(item, 0, gots_of(0)[0])

                def store(p, total):
                    if alone:
                        item.send[t][slot, rows_of(p), :] = total.astype(BF16)
                    else:
                        self.total_s[:, pl.ds(0, item.columns)] = total
                        if k > 1:

                            @pl.when((me >= 1) & (p == 0))
                            def _():
                                item.message(t, back, k - 1, 0).wait_recv()

                        def put(at, value):
                            rows = pl.ds(pl.multiple_of(p * item.width + at.start, 16), 16)
                            item.send[t][slot, rows, :] = value.astype(BF16)

                        earlier, own = gots_of(p)
                        self.start_gots(item, len(earlier), own)
                        self.add_gots(item, earlier + own, put)

                        @pl.when(p + 1 < stage.blocks)
                        def _():
                            self.start_gots(item, 0, gots_of(p + 1)[0])

                    item.message(t, back, k, slot, rows_of(p)).start()

                self.products(item, stage.blocks, lambda p: base + value * stage.stride + stage.offset(p), store)

    def out_copy(self, item):
        return pltpu.make_async_copy(self.out_s.at[:, pl.ds(0, item.columns)], item.out, self.out_sem)

    def finish(self, item):
        t = len(item.stages)
        self.wait_last(item, t - 1)
        gots = sum(self.arrived(item, t, 0), [])
        self.start_gots(item, 0, gots)

        def store(p, total):
            self.total_s[:, pl.ds(0, item.columns)] = total

            def put(at, value):
                self.out_s[at, pl.ds(0, item.columns)] = value

            self.add_gots(item, gots, put)

        self.settle()
        self.products(item, 1, lambda p: self.own_base(item, t), store)
        self.out_copy(item).start()
        self.finished = item

    def settle(self):
        if self.finished is not None:
            self.out_copy(self.finished).wait()
        self.finished = None

    def drain(self, item, stages):
        for t in stages:
            for slot in range(item.stages[t].size - 1):
                item.message(t, 0, 1, slot).wait_send()


def stage_shapes(n, last_first, width, columns):
    sizes = digit_sizes(n)
    if last_first:
        sizes = sizes[1:] + sizes[:1]
    left, found = n, []
    for t, m in enumerate(sizes):
        left //= m
        found.append(
            (
                jax.ShapeDtypeStruct((2, m - 1, left * width, columns), BF16),
                pltpu.VMEM((m - 1, left * width, columns), BF16),
                pltpu.SemaphoreType.DMA((m - 1,)),
                pltpu.SemaphoreType.DMA((2, m - 1)),
            )
        )
    return found


def dot_tn(left, right):
    return lax.dot_general(left, right, (((0,), (0,)), ((), ())), preferred_element_type=F32)


class Reader:
    def __init__(self, refs):
        self.refs, self.at = refs, 0

    def __call__(self, count=None):
        start = self.at
        self.at += 1 if count is None else count
        return self.refs[start] if count is None else list(self.refs[start : self.at])


def column_blocks(left, n):
    tokens, features = left.shape
    width = features // n
    return left.reshape(tokens, n, width).transpose(1, 0, 2) if width % LANES else left


class TensorLine:
    def __init__(self):
        self.index = lax.axis_index("tensor")
        self.mate, self.peer, self.cross = self.index ^ 1, self.index ^ 2, self.index ^ 3


def copy_in(source, target, sem):
    copy = pltpu.make_async_copy(source, target, sem)
    copy.start()
    return copy


def remote(source, target, send_sem, recv_sem, axis, index):
    return pltpu.make_async_remote_copy(
        src_ref=source, dst_ref=target, send_sem=send_sem, recv_sem=recv_sem,
        device_id={axis: index}, device_id_type=pl.DeviceIdType.MESH,
    )


class TensorReduce:
    def __init__(self, line, part, from_mate, from_peer, own_v, got_v, send_v, send_sem, recv_sem, sem):
        self.line, self.part, self.from_mate, self.from_peer = line, part, from_mate, from_peer
        self.own_v, self.got_v, self.send_v, self.sem = own_v, got_v, send_v, sem
        self.rows = part.shape[0] // 4
        self.mates = [
            remote(self.block(line.cross), from_mate.at[0], send_sem.at[0], recv_sem.at[0], "tensor", line.mate),
            remote(self.block(line.mate), from_mate.at[1], send_sem.at[1], recv_sem.at[1], "tensor", line.mate),
        ]
        self.over = remote(send_v, from_peer, send_sem.at[2], recv_sem.at[2], "tensor", line.peer)

    def block(self, index):
        return self.part.at[pl.ds(pl.multiple_of(index * self.rows, self.rows), self.rows)]

    def start(self):
        for copy in self.mates:
            copy.start()

    def own_rows(self, index, at):
        if self.own_v is not None:
            return self.own_v[at, :].astype(F32)
        return self.part[pl.ds(pl.multiple_of(index * self.rows + at.start, 16), 16), :].astype(F32)

    def fetch_own(self, index):
        return [] if self.own_v is None else [copy_in(self.block(index), self.own_v, self.sem.at[0])]

    def middle(self):
        copies = self.fetch_own(self.line.peer)
        self.mates[0].wait_recv()
        copies.append(copy_in(self.from_mate.at[0], self.got_v.at[0], self.sem.at[1]))
        for copy in copies:
            copy.wait()

        @pl.loop(0, self.rows // 16)
        def _(r):
            at = pl.ds(pl.multiple_of(r * 16, 16), 16)
            self.send_v[at, :] = (self.own_rows(self.line.peer, at) + self.got_v[0, at, :].astype(F32)).astype(BF16)

        self.over.start()

    def end(self, use):
        copies = self.fetch_own(self.line.index)
        self.mates[1].wait_recv()
        copies.append(copy_in(self.from_mate.at[1], self.got_v.at[0], self.sem.at[1]))
        self.over.wait_recv()
        copies.append(copy_in(self.from_peer, self.got_v.at[1], self.sem.at[2]))
        for copy in copies:
            copy.wait()

        @pl.loop(0, self.rows // 16)
        def _(r):
            at = pl.ds(pl.multiple_of(r * 16, 16), 16)
            use(at, self.own_rows(self.line.index, at) + self.got_v[0, at, :].astype(F32) + self.got_v[1, at, :].astype(F32))

    def drain(self):
        for copy in self.mates:
            copy.wait_send()
        self.over.wait_send()

    @staticmethod
    def results(tokens, features):
        return [jax.ShapeDtypeStruct((2, tokens // 4, features), BF16), jax.ShapeDtypeStruct((tokens // 4, features), BF16)]

    @staticmethod
    def semaphores():
        return [pltpu.SemaphoreType.DMA((3,)), pltpu.SemaphoreType.DMA((3,)), pltpu.SemaphoreType.DMA((3,))]

    @staticmethod
    def buffers(tokens, features):
        rows = tokens // 4
        return [pltpu.VMEM((2, rows, features), BF16), pltpu.VMEM((rows, features), BF16)]


def norm_backward(values, gain, d_normed):
    inverse = lax.rsqrt(jnp.mean(values * values, axis=-1, keepdims=True) + epsilon)
    weighted = gain * d_normed
    inner = jnp.mean(weighted * values, axis=-1, keepdims=True)
    return inverse * weighted - values * (inverse * inverse * inverse * inner), d_normed * values * inverse


HBM = pl.BlockSpec(memory_space=pl.ANY)
IN_VMEM = pl.BlockSpec(memory_space=pltpu.VMEM)


class TensorGather:
    def __init__(self, line, own_v, out, send_sem, recv_sem):
        self.line, self.own_v, self.out, self.rows = line, own_v, out, own_v.shape[0]
        self.over = remote(own_v, self.block(line.index), send_sem.at[0], recv_sem.at[0], "tensor", line.peer)
        self.aside = remote(own_v, self.block(line.index), send_sem.at[1], recv_sem.at[1], "tensor", line.mate)
        self.onward = remote(self.block(line.peer), self.block(line.peer), send_sem.at[2], recv_sem.at[2], "tensor", line.mate)

    def block(self, index):
        return self.out.at[pl.ds(pl.multiple_of(index * self.rows, self.rows), self.rows)]

    def start(self):
        self.over.start()
        self.aside.start()

    def forward(self):
        self.over.wait_recv()
        self.onward.start()

    def drain(self):
        for copy in (self.over, self.aside, self.onward):
            copy.wait_send()

    @staticmethod
    def semaphores():
        return [pltpu.SemaphoreType.DMA((3,)), pltpu.SemaphoreType.DMA((3,))]


def main_kernel(n, width, units, *refs):
    take = Reader(refs)
    cot_own, w_first, w_branch, w_out, w_gate, w_up, w_down = take(7)
    stream, gain_one, gain, masks, vecs, w_cat = take(6)
    normed, cot, gated, branch, conv, states, product, middle, normed_two, from_mate_one, from_peer_one = take(11)
    d_middle, att, hidden_o, dgate_o, dup_o, dgated_o, dri_o, dbranch_o, part_out, from_mate, from_peer = take(11)
    down_recv, (gate_recv, up_recv) = take(2), take(2)
    sums, gain_grad = take(2)
    (att_v,) = take(1)
    one_sems, cot_sems, two_sems, one_rs = take(2), take(2), take(2), take(3)
    one_sem, rs_send, rs_recv, rs_sem, ag_send, ag_recv, sem, engine_sem = take(8)
    item_sems = [take(2) for _ in range(4)]
    rows, features = stream.shape
    tokens, channels = conv.shape
    tile = 512
    line = TensorLine()
    twos = TensorGather(line, att_v, normed_two, *two_sems)
    two_v = att_v

    def forward_phase(
        wg_v, wb_v, wo_v, own_v, cot_v, block_v, gated_v, branch_v, conv_v, states_v, product_v,
        pre_s, a_s, b_s, part_v, rs_got, rs_send_v, middle_v,
    ):
        ones = TensorGather(line, own_v, normed, *one_sems)
        cots = TensorGather(line, cot_v, cot, *cot_sems)
        reduce = TensorReduce(line, part_v, from_mate_one, from_peer_one, None, rs_got, rs_send_v, *one_rs)
        loads = [copy_in(w_first, wg_v, one_sem.at[0]), copy_in(w_branch, wb_v, one_sem.at[1]), copy_in(w_out, wo_v, one_sem.at[2])]
        cot_load = copy_in(cot_own, cot_v, one_sem.at[3])

        def chunks(body):
            @pl.loop(0, rows // 16)
            def _(r):
                body(pl.ds(pl.multiple_of(r * 16, 16), 16))

        def norm(values, gains):
            inverse = lax.rsqrt(jnp.mean(values * values, axis=-1, keepdims=True) + epsilon)
            return (values * inverse * gains).astype(BF16)

        def first_norm(at):
            own_v[at, :] = norm(stream[at, :].astype(F32), gain_one[...])

        chunks(first_norm)
        ones.start()
        keep = [copy_in(own_v, ones.block(line.index), one_sem.at[4])]
        cot_load.wait()
        cots.start()
        keep.append(copy_in(cot_v, cots.block(line.index), one_sem.at[5]))

        def project(source, index):
            at = pl.ds(pl.multiple_of(index * rows, rows), rows)
            branch_v[at, :] = jnp.dot(source, wb_v[...], preferred_element_type=F32)
            gated_v[at, :] = jnp.dot(source, wg_v[...], preferred_element_type=F32)

        loads[0].wait()
        loads[1].wait()
        project(own_v[...], line.index)
        ones.aside.wait_recv()
        copy_in(ones.block(line.mate), block_v.at[0], one_sem.at[6]).wait()
        project(block_v[0], line.mate)
        ones.forward()
        copy_in(ones.block(line.peer), block_v.at[1], one_sem.at[6]).wait()
        project(block_v[1], line.peer)
        ones.onward.wait_recv()
        copy_in(ones.block(line.cross), block_v.at[0], one_sem.at[6]).wait()
        project(block_v[0], line.cross)
        outs = [copy_in(branch_v, branch, one_sem.at[7]), copy_in(gated_v, gated, one_sem.at[8])]
        mixer_forward_kernel(branch_v, gated_v, masks, vecs, w_cat, conv_v, states_v, product_v, pre_s, a_s, b_s)
        outs += [copy_in(conv_v, conv, one_sem.at[9]), copy_in(states_v, states, one_sem.at[10]), copy_in(product_v, product, one_sem.at[11])]
        loads[2].wait()

        def out_block(index):
            at = pl.ds(pl.multiple_of(index * rows, rows), rows)
            part_v[at, :] = jnp.dot(product_v[at, :], wo_v[...], preferred_element_type=F32).astype(BF16)

        out_block(line.cross)
        reduce.mates[0].start()
        out_block(line.peer)
        reduce.middle()
        out_block(line.mate)
        reduce.mates[1].start()
        out_block(line.index)
        cots.forward()

        def second_norm(at, total):
            values = stream[at, :].astype(F32) + total
            middle_v[at, :] = values
            two_v[at, :] = norm(values, gain[...])

        reduce.end(second_norm)
        twos.start()
        keep += [copy_in(two_v, twos.block(line.index), one_sem.at[12]), copy_in(middle_v, middle, one_sem.at[13])]
        cots.aside.wait_recv()
        cots.onward.wait_recv()
        for copy in keep + outs:
            copy.wait()
        for gathered in (ones, cots):
            gathered.drain()
        reduce.drain()

    block = pltpu.VMEM((rows, features), BF16)
    wide = pltpu.VMEM((tokens, channels), F32)
    narrow = pltpu.VMEM((tokens, channels), BF16)
    lanes = pltpu.VMEM((channels // LANES, tokens, LANES), F32)
    pl.run_scoped(
        forward_phase,
        pltpu.VMEM(w_first.shape, BF16), pltpu.VMEM(w_branch.shape, BF16), pltpu.VMEM(w_out.shape, BF16),
        block, block, pltpu.VMEM((2, rows, features), BF16),
        wide, wide, narrow, wide, narrow,
        pltpu.VMEM((tokens, 2 * channels), F32), lanes, lanes,
        pltpu.VMEM((tokens, features), BF16), *TensorReduce.buffers(tokens, features),
        pltpu.VMEM((rows, features), F32),
    )

    def backward_phase(hidden, *held):
        down_one, down_two, gate_send, up_send, left_s, got_s, total_s = held
        halves = [(down_one, *item_sems[0]), (down_two, *item_sems[1])]
        (gate_ss, gate_rs), (up_ss, up_rs) = item_sems[2:]
        engine = Engine(left_s, got_s, total_s, engine_sem)
        downs = [
            Item(
                make_stages(n, True), cot, hidden.at[:, pl.ds(q * (units // 2), units // 2)], width, 0,
                (None, [down_recv[q]], [send], [send_sem], [recv_sem]),
            )
            for q, (send, send_sem, recv_sem) in enumerate(halves)
        ]
        gather = TensorGather(line, att_v, att, ag_send, ag_recv)

        def rounds(item):
            return list(range(1, item.stages[0].size))

        def row_block(ref, index):
            return ref.at[pl.ds(pl.multiple_of(index * rows, rows), rows)]

        first, between, last = rounds(downs[0])[:1], rounds(downs[0])[1:-1], rounds(downs[0])[1:][-1:]
        gate = Item(make_stages(n, False), normed_two, hidden, width, 0, (None, [gate_recv], [gate_send], [gate_ss], [gate_rs]))
        half = hidden.at[:, pl.ds(0, units // 2)]
        up = Item(make_stages(n, False), normed_two, half, width, 0, (None, [up_recv], [up_send], [up_ss], [up_rs]))

        def take_rounds(item, numbers):
            for k in numbers:
                engine.round(item, 0, k)

        def tensor_phase(wg_v, wu_v, wd_v, dgate, dup, x_v, c_v, part, got_v, send_v, dmid_v, cot_v):
            gate.right, up.right = dgate, dup.at[:, pl.ds(0, units // 2)]
            weights = [copy_in(w_gate, wg_v, sem.at[0]), copy_in(w_up, wu_v, sem.at[1]), copy_in(w_down, wd_v, sem.at[2])]
            loads = [copy_in(middle, dmid_v, sem.at[3]), copy_in(row_block(cot, line.index), cot_v, sem.at[4])]
            copy_in(row_block(normed_two, line.index), x_v, sem.at[5])
            copy_in(row_block(cot, line.index), c_v, sem.at[6])
            for load in weights:
                load.wait()

            @pl.loop(0, 4)
            def _(b):
                index = line.index ^ b
                at = pl.ds(pl.multiple_of(index * rows, rows), rows)
                pltpu.make_async_copy(row_block(normed_two, index), x_v, sem.at[5]).wait()
                pltpu.make_async_copy(row_block(cot, index), c_v, sem.at[6]).wait()

                @pl.loop(0, units // tile)
                def _(j):
                    cols = pl.ds(pl.multiple_of(j * tile, tile), tile)
                    gate_pre = jnp.dot(x_v[...], wg_v[:, cols], preferred_element_type=F32)
                    up_pre = jnp.dot(x_v[...], wu_v[:, cols], preferred_element_type=F32)
                    d_hidden = dot_nt(c_v[...], wd_v[cols, :])
                    act, slope = gelu_parts(gate_pre)
                    hidden[at, cols] = (act * up_pre).astype(BF16)
                    dgate[at, cols] = (d_hidden * up_pre * slope).astype(BF16)
                    dup[at, cols] = (d_hidden * act).astype(BF16)

                @pl.when(b == 0)
                def _():
                    twos.aside.wait_recv()

                @pl.when(b == 1)
                def _():
                    twos.forward()

                @pl.when(b == 2)
                def _():
                    twos.onward.wait_recv()

                @pl.when(b < 3)
                def _():
                    following = line.index ^ (b + 1)
                    copy_in(row_block(normed_two, following), x_v, sem.at[5])
                    copy_in(row_block(cot, following), c_v, sem.at[6])

            twos.drain()
            outs = [copy_in(hidden, hidden_o, sem.at[0]), copy_in(dgate, dgate_o, sem.at[1]), copy_in(dup, dup_o, sem.at[2])]
            for item in downs:
                take_rounds(item, first)
            take_rounds(gate, rounds(gate))

            def stage(index, value):
                @pl.loop(0, features // tile)
                def _(j):
                    at, cols = pl.ds(pl.multiple_of(index * rows, rows), rows), pl.ds(pl.multiple_of(j * tile, tile), tile)
                    part[at, cols] = value(at, cols).astype(BF16)

            def two(at, cols):
                return dot_nt(dgate[at, :], wg_v[cols, :]) + dot_nt(dup[at, :], wu_v[cols, :])

            def out(at, cols):
                return jnp.dot(hidden[at, :], wd_v[:, cols], preferred_element_type=F32)

            reduce = TensorReduce(line, part, from_mate, from_peer, None, got_v, send_v, rs_send, rs_recv, rs_sem)
            stage(line.cross, two)
            reduce.mates[0].start()
            stage(line.peer, two)
            reduce.middle()
            stage(line.mate, two)
            reduce.mates[1].start()
            stage(line.index, two)
            for item in downs:
                take_rounds(item, between)
            for load in loads:
                load.wait()
            gain_grad[...] = jnp.zeros_like(gain_grad)

            def use(at, total):
                back, terms = norm_backward(dmid_v[at, :], gain[...], total)
                value = cot_v[at, :].astype(F32) + back
                dmid_v[at, :] = value
                att_v[at, :] = value.astype(BF16)
                gain_grad[...] += fold_rows(terms)

            reduce.end(use)
            gather.start()
            keep = [copy_in(att_v, gather.block(line.index), sem.at[3]), copy_in(dmid_v, d_middle, sem.at[4])]
            take_rounds(up, rounds(up))
            reduce.drain()

            @pl.loop(0, 4)
            def _(b):
                stage(b, out)
                copy_in(row_block(part, b), row_block(part_out, b), sem.at[7])

            take_rounds(downs[0], last)
            gather.forward()
            for copy in outs + keep:
                copy.wait()
            pltpu.make_async_copy(part, part_out, sem.at[7]).wait()

        weight = pltpu.VMEM((features, units), BF16)
        block = pltpu.VMEM((rows, features), BF16)
        pl.run_scoped(
            tensor_phase,
            weight, weight, pltpu.VMEM((units, features), BF16),
            pltpu.VMEM((tokens, units), BF16), pltpu.VMEM((tokens, units), BF16),
            block, block, pltpu.VMEM((tokens, features), BF16),
            *TensorReduce.buffers(tokens, features),
            pltpu.VMEM((rows, features), F32), block,
        )

        def mixer_phase(gated_v, states_v, conv_v, dgated_v, dri_v, dbranch_v, block_v, w_v, *scratch):
            loads = [copy_in(conv, conv_v, sem.at[1]), copy_in(w_out, w_v, sem.at[0])]
            loads += [copy_in(gated, gated_v, sem.at[2]), copy_in(states, states_v, sem.at[3])]
            mixer = MixerBackward(masks, vecs, w_cat, states_v, gated_v, conv_v, dgated_v, dri_v, dbranch_v, sums, *scratch)
            loads[0].wait()
            mixer.gates()
            take_rounds(downs[1], last)
            loads[1].wait()

            def product_gradient(index, source):
                mixer.a_s[pl.ds(pl.multiple_of(index * rows, rows), rows), :] = dot_nt(source[...], w_v[...])

            product_gradient(line.index, att_v)
            gather.aside.wait_recv()
            mate = copy_in(row_block(att, line.mate), block_v.at[0], sem.at[4])
            peer = copy_in(row_block(att, line.peer), block_v.at[1], sem.at[5])
            mate.wait()
            product_gradient(line.mate, block_v.at[0])
            peer.wait()
            product_gradient(line.peer, block_v.at[1])
            gather.onward.wait_recv()
            copy_in(row_block(att, line.cross), block_v.at[0], sem.at[4]).wait()
            product_gradient(line.cross, block_v.at[0])
            loads[2].wait()
            loads[3].wait()
            mixer.factors(gated_v)
            again = copy_in(branch, gated_v, sem.at[2])
            outs = [copy_in(dgated_v, dgated_o, sem.at[1])]
            mixer.scan()
            mixer.gate_gradients()
            outs.append(copy_in(dri_v, dri_o, sem.at[3]))
            again.wait()
            mixer.convolution()
            outs.append(copy_in(dbranch_v, dbranch_o, sem.at[0]))
            for copy in outs:
                copy.wait()

        pl.run_scoped(
            mixer_phase,
            pltpu.VMEM((tokens, channels), F32),
            pltpu.VMEM((tokens, channels), F32),
            pltpu.VMEM((tokens, channels), BF16),
            pltpu.VMEM((tokens, channels), BF16),
            pltpu.VMEM((tokens, 2 * channels), BF16),
            pltpu.VMEM((tokens, channels), BF16),
            pltpu.VMEM((2, rows, features), BF16),
            pltpu.VMEM((channels, features), BF16),
            *MixerBackward.scratch(tokens, channels),
        )
        gather.drain()
        for item in (*downs, gate, up):
            engine.drain(item, [0])
            engine.wait_last(item, 0)

    down = stage_shapes(n, True, width, units // 2)[0][1]
    gate = stage_shapes(n, False, width, units)[0][1]
    up = stage_shapes(n, False, width, units // 2)[0][1]
    pl.run_scoped(
        backward_phase,
        pltpu.VMEM((tokens, units), BF16), down, down, gate, up,
        pltpu.VMEM((2, tokens, max(width, LANES)), BF16),
        pltpu.VMEM((2, width, units), BF16),
        pltpu.VMEM((width, units), F32),
    )


def main_part(cot_own, w_first, w_branch, w_out, w_gate, w_up, w_down, stream, gain_one, gain_two, masks, vecs, w_cat):
    n = lax.axis_size("dp")
    rows, features = stream.shape
    tokens, channels, units, width = 4 * rows, w_first.shape[1], w_gate.shape[1], features // n
    down = stage_shapes(n, True, width, units // 2)[0]
    gate = stage_shapes(n, False, width, units)[0]
    up = stage_shapes(n, False, width, units // 2)[0]
    dma = pltpu.SemaphoreType.DMA
    whole = jax.ShapeDtypeStruct((tokens, features), BF16)
    part = jax.ShapeDtypeStruct((rows, features), F32)
    hide = jax.ShapeDtypeStruct((tokens, units), BF16)
    wide = jax.ShapeDtypeStruct((tokens, channels), F32)
    narrow = jax.ShapeDtypeStruct((tokens, channels), BF16)
    sums = TensorReduce.results(tokens, features)
    results = [whole, whole, wide, wide, narrow, wide, narrow, part, whole, *sums]
    results += [part, whole, hide, hide, hide, narrow, jax.ShapeDtypeStruct((tokens, 2 * channels), BF16), narrow, whole, *sums]
    results += [down[0], down[0], gate[0], up[0]]
    gathers = TensorGather.semaphores()
    return pl.pallas_call(
        functools.partial(main_kernel, n, width, units),
        out_shape=[*results, jax.ShapeDtypeStruct((8, 8, channels), F32), jax.ShapeDtypeStruct((8, features), F32)],
        in_specs=[HBM] * 7 + [IN_VMEM] * 6,
        out_specs=[HBM] * len(results) + [IN_VMEM] * 2,
        scratch_shapes=[
            pltpu.VMEM((rows, features), BF16),
            *gathers, *gathers, *gathers, *TensorReduce.semaphores(), dma((14,)),
            *TensorReduce.semaphores(), *gathers, dma((8,)), dma((4,)),
            *down[2:4], *down[2:4], *gate[2:4], *up[2:4],
        ],
        compiler_params=pltpu.CompilerParams(vmem_limit_bytes=VMEM_BYTES, has_side_effects=True),
        cost_estimate=pl.CostEstimate(flops=60 * 10**9, bytes_accessed=120 * 10**6, transcendentals=14 * tokens * channels),
        name="main_part",
    )(cot_own, w_first, w_branch, w_out, w_gate, w_up, w_down, stream, gain_one, gain_two, masks, vecs, w_cat)


def gather_sums(gains, sends, recvs, send_sems, recv_sems):
    n, line = lax.axis_size("dp"), TensorLine()
    hops = [("tensor", line.mate), ("tensor", line.peer)]
    bit = 1
    while bit < n:
        hops.append(("dp", lax.axis_index("dp") ^ bit))
        bit *= 2
    copies = [remote(sends.at[s], recvs.at[s], send_sems.at[s], recv_sems.at[s], *hop) for s, hop in enumerate(hops)]

    def begin(s):
        sends[s] = gains[...] if s == 0 else sends[s - 1] + recvs[s - 1]
        copies[s].start()

    def step(s):
        if s > 0:
            copies[s - 1].wait_recv()
        if s < len(copies):
            begin(s)
        else:
            gains[...] = sends[s - 1] + recvs[s - 1]
            for copy in copies:
                copy.wait_send()

    return [functools.partial(step, s) for s in range(len(copies) + 1)]


def finish_kernel(n, width, plan, order, lefts_of, keep, readies, columns, out_of, *refs):
    take = Reader(refs)
    count, n_outs = len(plan), max(o for o, _ in out_of) + 1
    part_out, middle, d_middle, stream, w_gate, w_branch = take(6)
    gain, gain_grad_two = take(2)
    lefts, rights_hbm = take(max(lefts_of) + 1), take(n_outs)
    shapes = [stage_shapes(n, plan[i], width, columns[i]) for i in range(count)]
    given = [take(readies[i]) for i in range(count)]
    stream_grad_o, stream_out_o = take(2)
    outs = take(n_outs)
    (part,) = take(1)
    reduces = [take(2), take(2)]
    recv = [given[i] + take(len(shapes[i]) - readies[i]) for i in range(count)]
    (gains,) = take(1)
    rights = take(n_outs)
    wg_v, wb_v, stage_v = take(3)
    nones = [[None] * r for r in readies]
    sends = [nones[i] + take(len(shapes[i]) - readies[i]) for i in range(count)]
    send_sems = [nones[i] + take(len(shapes[i]) - readies[i]) for i in range(count)]
    recv_sems = [nones[i] + take(len(shapes[i]) - readies[i]) for i in range(count)]
    left_vs = take(max(lefts_of) + 1)
    left_s, got_s, total_s, out_s, own_v, got_v, send_v, send_w = take(8)
    value_v, base_v, gain_sends, gain_recvs = take(4)
    rs_sems = [take(3), take(3)]
    gain_ss, gain_rs, right_sem, sem, engine_sem, out_sem = take(6)

    line = TensorLine()
    engine = Engine(left_s, got_s, total_s, engine_sem, out_s, out_sem)
    tensor = [
        TensorReduce(line, source, *reduces[q], own_v, got_v, (send_v, send_w)[q], *rs_sems[q])
        for q, source in enumerate((part, part_out))
    ]
    tensor[1].start()
    loads, weights, left_loads = {}, [], {}

    def issue(kind, i):
        if kind == "left" and i in keep and i not in left_loads:
            left_loads[i] = copy_in(lefts[i], left_vs[i], right_sem.at[n_outs + 2 + i])
        if kind == "right" and i not in loads:
            loads[i] = copy_in(rights_hbm[i], rights[i], right_sem.at[i])

    def issue_for(i):
        if i >= 0:
            issue("right", out_of[i][0])
            issue("left", lefts_of[i])
        elif not weights:
            issue("right", n_outs - 2)
            issue("right", n_outs - 1)
            weights.extend([copy_in(w_gate, wg_v, right_sem.at[n_outs]), copy_in(w_branch, wb_v, right_sem.at[n_outs + 1])])

    loaded = set()

    def load_left(i):
        if left_loads.get(i) is not None:
            left_loads[i].wait()
            left_loads[i] = None

    def load(i):
        if i not in loaded:
            loads[i].wait()
            loaded.add(i)

    def columns_of(i):
        return pl.ds(out_of[i][1], columns[i])

    items = [
        Item(
            make_stages(n, plan[i]), lefts[lefts_of[i]], rights[out_of[i][0]].at[:, columns_of(i)], width, readies[i],
            (outs[out_of[i][0]].at[:, columns_of(i)], recv[i], sends[i], send_sems[i], recv_sems[i]),
            left_vs[lefts_of[i]] if lefts_of[i] in keep else None,
        )
        for i in range(count)
    ]

    rows, features = stream.shape

    def stage(index):
        at = pl.ds(pl.multiple_of(index * rows, rows), rows)

        @pl.loop(0, features // 512)
        def _(j):
            cols = pl.ds(pl.multiple_of(j * 512, 512), 512)
            total = dot_nt(rights[n_outs - 2][at, :], wg_v[cols, :]) + dot_nt(rights[n_outs - 1][at, :], wb_v[cols, :])
            stage_v[:, cols] = total.astype(BF16)

        copy_in(stage_v, tensor[0].block(index), sem.at[0]).wait()

    def part_first():
        for i in (n_outs - 2, n_outs - 1):
            load(i)
        for copy in weights:
            copy.wait()
        stage(line.cross)
        tensor[0].mates[0].start()
        stage(line.peer)

    def part_second():
        stage(line.mate)
        tensor[0].mates[1].start()
        stage(line.index)

    def grad_end():
        copies = [copy_in(stream, value_v, sem.at[0]), copy_in(d_middle, base_v, sem.at[1])]
        for copy in copies:
            copy.wait()
        gains[...] = jnp.zeros_like(gains)

        def use(at, total):
            back, terms = norm_backward(value_v[at, :].astype(F32), gain[...], total)
            base_v[at, :] = base_v[at, :] + back
            gains[...] += fold_rows(terms)

        tensor[0].end(use)
        copy_in(base_v, stream_grad_o, sem.at[0]).wait()
        first = jnp.sum(gains[...], axis=0, keepdims=True)
        second = jnp.sum(gain_grad_two[...], axis=0, keepdims=True)
        pick = lax.broadcasted_iota(jnp.int32, gains.shape, 0)
        gains[...] = jnp.where(pick == 0, first, jnp.where(pick == 1, second, 0.0))

    def out_end():
        copy_in(middle, base_v, sem.at[0]).wait()

        def use(at, total):
            base_v[at, :] = base_v[at, :] + total

        tensor[1].end(use)
        copy_in(base_v, stream_out_o, sem.at[0]).wait()

    extra = [part_first, tensor[0].middle, part_second, tensor[1].middle, grad_end, out_end]
    extra += gather_sums(gains, gain_sends, gain_recvs, gain_ss, gain_rs)
    for at, (i, t, k) in enumerate(order):
        for ahead in order[at : at + 3]:
            issue_for(ahead[0])
        if i < 0:
            if extra:
                extra.pop(0)()
            continue
        load(out_of[i][0])
        load_left(lefts_of[i])
        if t < len(shapes[i]):
            engine.round(items[i], t, k)
        else:
            engine.finish(items[i])
    for step in extra:
        step()
    engine.settle()
    for i, item in enumerate(items):
        engine.drain(item, range(readies[i], len(shapes[i])))
    for reduce in tensor:
        reduce.drain()


def task_order(plan, readies, names, n):
    tasks = []
    for last_first, ready in zip(plan, readies):
        sizes = digit_sizes(n)
        if last_first:
            sizes = sizes[1:] + sizes[:1]
        i = len(tasks)
        tasks.append([(i, t, k) for t, m in enumerate(sizes) for k in range(1, m) if t >= ready] + [(i, len(sizes), 0)])
    out, at = [], [0] * len(plan)
    for i in names:
        if i < 0:
            out.append((-1, 0, 0))
        elif at[i] < len(tasks[i]):
            out.append(tasks[i][at[i]])
            at[i] += 1
    for i in range(len(plan)):
        out += tasks[i][at[i] :]
    return out


def finish(part_out, middle, d_middle, stream, w_gate, w_branch, gain, gain_grad_two, lefts, lefts_of, rights, given, plan, out_of, names, keep):
    n = lax.axis_size("dp")
    tokens, features = part_out.shape
    width, rows = features // n, tokens // 4
    readies = [len(g) for g in given]
    pieces = [sum(o == q for o, _ in out_of) for q in range(len(rights))]
    columns = [rights[o].shape[1] // pieces[o] for o, _ in out_of]
    out_of = [(o, q * c) for (o, q), c in zip(out_of, columns)]
    widest = max(columns)
    keep = () if width % LANES else keep
    shapes = [stage_shapes(n, last_first, width, c)[ready:] for last_first, c, ready in zip(plan, columns, readies)]
    steps = 2 + (n - 1).bit_length()
    dma = pltpu.SemaphoreType.DMA
    stream_shape = jax.ShapeDtypeStruct((rows, features), F32)
    out_shape = [stream_shape, stream_shape] + [jax.ShapeDtypeStruct((width, r.shape[1]), F32) for r in rights]
    out_shape += [jax.ShapeDtypeStruct((tokens, features), BF16)]
    out_shape += TensorReduce.results(tokens, features) * 2 + [s[0] for item in shapes for s in item]
    results = pl.pallas_call(
        functools.partial(finish_kernel, n, width, plan, task_order(plan, readies, names, n), lefts_of, keep, readies, columns, out_of),
        out_shape=[*out_shape, jax.ShapeDtypeStruct((8, features), F32)],
        in_specs=[HBM] * 6 + [IN_VMEM] * 2 + [HBM] * (len(lefts) + len(rights) + sum(readies)),
        out_specs=[HBM] * len(out_shape) + [IN_VMEM],
        scratch_shapes=[
            *[pltpu.VMEM(r.shape, BF16) for r in rights],
            pltpu.VMEM(w_gate.shape, BF16), pltpu.VMEM(w_branch.shape, BF16), pltpu.VMEM((rows, features), BF16),
            *[s[1] for item in shapes for s in item],
            *[s[2] for item in shapes for s in item],
            *[s[3] for item in shapes for s in item],
            *[pltpu.VMEM((tokens, features) if i in keep else (8, features), BF16) for i in range(len(lefts))],
            pltpu.VMEM((2, tokens, width), BF16),
            pltpu.VMEM((2 * len(digit_sizes(n)), width, widest), BF16),
            pltpu.VMEM((width, widest), F32), pltpu.VMEM((width, widest), F32),
            pltpu.VMEM((rows, features), BF16), *TensorReduce.buffers(tokens, features),
            pltpu.VMEM((rows, features), BF16),
            pltpu.VMEM((rows, features), BF16),
            pltpu.VMEM((rows, features), F32),
            pltpu.VMEM((steps, 8, features), F32),
            pltpu.VMEM((steps, 8, features), F32),
            *TensorReduce.semaphores(),
            *TensorReduce.semaphores(),
            dma((steps,)), dma((steps,)), dma((len(rights) + 2 + len(lefts),)), dma((2,)), dma((2 + 2 * len(digit_sizes(n)),)), dma,
        ],
        compiler_params=pltpu.CompilerParams(vmem_limit_bytes=VMEM_BYTES, has_side_effects=True),
        cost_estimate=pl.CostEstimate(
            flops=2 * tokens * features * sum(columns), bytes_accessed=4 * features * sum(columns), transcendentals=0
        ),
        name="finish",
    )(
        part_out, middle, d_middle, stream, w_gate, w_branch, gain, gain_grad_two,
        *[column_blocks(v, n) for v in lefts], *rights, *[g for item in given for g in item],
    )
    return results[0], results[1], results[2 : 2 + len(rights)], results[-1]

DP_PLAN = [True, True, False, False, False, False, False, False]
DP_OUTS = [(0, 0), (0, 1), (1, 0), (2, 0), (2, 1), (3, 0), (4, 0), (5, 0)]
DP_ORDER = [3, 6, 2, -1, 5, -1, 3, 3, 7, 6, -1, -1, 2, 6, -1, 2, 4, -1, 7, -1, 1, 5, 7, 3, 5, 2, -1, 6, 4, 7, -1, -1, 1, 6, 4, 0, -1, 5, 7, 4, -1, 5, 0, 4]


def dot(left, right, dims, out=F32):
    return lax.dot_general(left, right, (dims, ((), ())), preferred_element_type=F32).astype(out)


def spread_heads(*weights):
    heads, width = weights[0].shape[:2]
    total = len(weights) * heads * width
    rows = []
    for h in range(heads):
        row = 0
        for q, weight in enumerate(weights):
            before = (q * heads + h) * width
            row = row + jnp.pad(weight[h], ((0, 0), (before, total - before - width)))
        rows.append(row)
    return jnp.concatenate(rows)


def head_blocks(dense, heads, width):
    return jnp.stack([dense[h * width : (h + 1) * width, h * width : (h + 1) * width] for h in range(heads)])


def on_device(
    stream_in, segments, first_gain, gelu_gate_weight, recurrent_branch_weight, conv_kernel, conv_bias, recur_weight, recur_bias,
    inlet_weight, inlet_bias, decay_param, recurrent_output_weight, second_gain, gate_projection_weight, up_projection_weight,
    down_projection_weight, cotangent,
):
    seq_len = segments.shape[1]
    heads, head_width = recur_weight.shape[:2]
    ids = jnp.pad(segments[0], (3, 8), constant_values=-1)
    same = [(ids[3 - k : 3 - k + seq_len] == segments[0]).astype(F32) for k in range(1, 4)]
    masks = jnp.pad(jnp.stack(same, axis=1), ((0, 8), (0, 5)))
    softplus = jax.nn.softplus(-decay_param)
    vecs = jnp.concatenate([conv_kernel, jnp.stack([conv_bias, recur_bias, inlet_bias, softplus])])
    w_cat = spread_heads(recur_weight, inlet_weight)

    (
        normed, cot, _, _, conv_out, _, product, middle, normed_two, _, _,
        d_middle, d_attended, hidden, d_gate, d_up, d_gated, d_ri, d_branch, part_out, _, _, *gots, sums, gain_two,
    ) = main_part(
        cotangent[0], gelu_gate_weight, recurrent_branch_weight, recurrent_output_weight, gate_projection_weight,
        up_projection_weight, down_projection_weight, stream_in[0], first_gain[None], second_gain[None], masks, vecs, w_cat,
    )
    stream_grad, stream_out, gradients, gains = finish(
        part_out, middle, d_middle, stream_in[0], gelu_gate_weight, recurrent_branch_weight, first_gain[None], gain_two,
        [cot, normed_two, d_attended, normed], [0, 0, 1, 1, 1, 2, 3, 3], [hidden, d_gate, d_up, product, d_gated, d_branch],
        [*([g] for g in gots), [], [], [], []], DP_PLAN, DP_OUTS, DP_ORDER, (1, 3),
    )
    down_gradient, gate_gradient, up_gradient, output_gradient, gated_gradient, branch_gradient = gradients

    width = heads * head_width
    dense = dot(conv_out, d_ri, ((0,), (0,)))
    grad_recur = head_blocks(dense[:, :width], heads, head_width)
    grad_inlet = head_blocks(dense[:, width:], heads, head_width)
    sums = jnp.sum(sums, axis=1)
    small = jnp.concatenate([sums.reshape(-1), grad_recur.reshape(-1), grad_inlet.reshape(-1)])
    small = lax.psum(small.astype(BF16), "dp").astype(F32)
    sums = small[: 8 * width].reshape(8, width)
    grad_recur, grad_inlet = small[8 * width :].reshape(2, heads, head_width, head_width)
    grad_decay = decay_scale * jax.nn.sigmoid(-decay_param) * sums[7]
    return (
        stream_out[None], stream_grad[None], gains[0], gated_gradient, branch_gradient, sums[:4], sums[4], grad_recur, sums[5],
        grad_inlet, sums[6], grad_decay, output_gradient.T, gains[1], gate_gradient, up_gradient, down_gradient.T,
    )


def solution(mesh):
    in_specs = (
        P("dp", "tensor", None),
        P("dp", None),
        P(),
        P(None, "tensor"),
        P(None, "tensor"),
        P(None, "tensor"),
        P("tensor"),
        P("tensor", None, None),
        P("tensor"),
        P("tensor", None, None),
        P("tensor"),
        P("tensor"),
        P("tensor", None),
        P(),
        P(None, "tensor"),
        P(None, "tensor"),
        P("tensor", None),
        P("dp", "tensor", None),
    )
    out_specs = (
        P("dp", "tensor", None),
        P("dp", "tensor", None),
        P(),
        P("dp", "tensor"),
        P("dp", "tensor"),
        P(None, "tensor"),
        P("tensor"),
        P("tensor", None, None),
        P("tensor"),
        P("tensor", None, None),
        P("tensor"),
        P("tensor"),
        P("tensor", "dp"),
        P(),
        P("dp", "tensor"),
        P("dp", "tensor"),
        P("tensor", "dp"),
    )
    return jax.shard_map(
        on_device, mesh=mesh, in_specs=in_specs, out_specs=out_specs, check_vma=False
    )
```

```python
import functools

import jax
import jax.numpy as jnp
from jax import lax
from jax.experimental import pallas as pl
from jax.experimental.pallas import tpu as pltpu
from jax.sharding import PartitionSpec as P

epsilon = 1e-06
decay_scale = 8.0
LANES = 128
GELU_C = 0.7978845608028654
GELU_K = 0.044715
F32 = jnp.float32
BF16 = jnp.bfloat16
VMEM_BYTES = 60 * 1024 * 1024


def minus_expm1(y, exp_y):
    s = 1.0 + y * (1.0 / 9.0)
    for d in range(8, 1, -1):
        s = 1.0 + (y * (1.0 / d)) * s
    return jnp.where(y > -0.5, -y * s, 1.0 - exp_y)


def gelu_parts(v):
    v2 = v * v
    t = jnp.tanh(GELU_C * v * (1.0 + GELU_K * v2))
    half = 0.5 * (1.0 + t)
    slope = half + 0.5 * v * (1.0 - t * t) * (GELU_C * (1.0 + 3.0 * GELU_K * v2))
    return v * half, slope


def lane_tiles(width):
    return [slice(j * LANES, (j + 1) * LANES) for j in range(width // LANES)]


def fold_rows(v):
    return jnp.sum(v.reshape(v.shape[0] // 8, 8, v.shape[1]), axis=0)


def gates_pre(rows, step, conv_ref, w_ref, pre_s):
    @pl.loop(0, rows // step)
    def _(i):
        r = pl.ds(pl.multiple_of(i * step, step), step)
        pre_s[r, :] = jnp.dot(conv_ref[r, :], w_ref[...], preferred_element_type=F32)


def mixer_forward_kernel(branch_ref, gated_ref, mask_ref, vec_ref, w_ref, conv_ref, states_ref, product_ref, pre_s, a_s, b_s):
    rows, width = branch_ref.shape
    seg = rows // 8
    tiles = lane_tiles(width)

    @pl.loop(0, 8)
    def _(s):
        t0 = pl.multiple_of(s * seg, seg)
        before = pl.multiple_of(jnp.maximum(t0 - 8, 0), 8)
        same = [mask_ref[pl.ds(t0, seg), k : k + 1] for k in range(3)]
        for cols in tiles:
            b = branch_ref[pl.ds(t0, seg), cols]
            ext = jnp.concatenate([branch_ref[pl.ds(before, 8), cols], b], axis=0)
            out = vec_ref[4:5, cols] + vec_ref[0:1, cols] * b
            for k in range(1, 4):
                out = out + vec_ref[k : k + 1, cols] * pltpu.roll(ext, k, 0)[8:] * same[k - 1]
            conv_ref[pl.ds(t0, seg), cols] = out.astype(BF16)

    gates_pre(rows, 256, conv_ref, w_ref, pre_s)

    @pl.loop(0, 8)
    def _(s):
        t0 = pl.multiple_of(s * seg, seg)
        c = mask_ref[pl.ds(t0, seg), 0:1]
        for j, cols in enumerate(tiles):
            cols_i = slice(width + j * LANES, width + (j + 1) * LANES)
            r = jax.nn.sigmoid(pre_s[pl.ds(t0, seg), cols] + vec_ref[5:6, cols])
            i = jax.nn.sigmoid(pre_s[pl.ds(t0, seg), cols_i] + vec_ref[6:7, cols])
            log_a = (-decay_scale * vec_ref[7:8, cols]) * r
            a = jnp.exp(log_a)
            n = jnp.sqrt(minus_expm1(2.0 * log_a, a * a))
            mult = (1.0 - c) + c * n
            a_s[j, pl.ds(t0, seg), :] = a * c
            b_s[j, pl.ds(t0, seg), :] = mult * i * conv_ref[pl.ds(t0, seg), cols].astype(F32)

    row = lax.broadcasted_iota(jnp.int32, (8, LANES), 0)

    def scan_step(i, carry):
        at = pl.ds(pl.multiple_of(i * 8, 8), 8)
        out = []
        for j, cols in enumerate(tiles):
            a, b = a_s[j, at, :], b_s[j, at, :]
            for s in (1, 2, 4):
                b = b + a * jnp.where(row >= s, pltpu.roll(b, s, 0), 0.0)
                a = a * jnp.where(row >= s, pltpu.roll(a, s, 0), 1.0)
            b = b + a * carry[j]
            states_ref[at, cols] = b
            out.append(jnp.broadcast_to(b[7:8, :], (8, LANES)))
        return tuple(out)

    lax.fori_loop(0, rows // 8, scan_step, tuple(jnp.zeros((8, LANES), F32) for _ in tiles), unroll=2)

    @pl.loop(0, 8)
    def _(s):
        at = pl.ds(pl.multiple_of(s * seg, seg), seg)
        for cols in tiles:
            act, _ = gelu_parts(gated_ref[at, cols])
            product_ref[at, cols] = (states_ref[at, cols] * act).astype(BF16)


class MixerBackward:
    def __init__(self, masks, vecs, w_cat, states, branch, conv, dgated, dri, dbranch, sums, pre_s, a_s, n_s, ac_s, e_s):
        self.masks, self.vecs, self.w_cat, self.states, self.branch, self.conv = masks, vecs, w_cat, states, branch, conv
        self.dgated, self.dri, self.dbranch, self.sums = dgated, dri, dbranch, sums
        self.pre_s, self.a_s, self.n_s, self.ac_s, self.e_s = pre_s, a_s, n_s, ac_s, e_s
        self.rows, self.width = states.shape
        self.seg = self.rows // 8
        self.tiles = lane_tiles(self.width)

    @staticmethod
    def scratch(rows, width):
        lanes = width // LANES
        return [
            pltpu.VMEM((rows, 2 * width), F32),
            pltpu.VMEM((rows, width), F32),
            pltpu.VMEM((rows + 8, width), F32),
            pltpu.VMEM((lanes, rows, LANES), F32),
            pltpu.VMEM((lanes, rows, LANES), F32),
        ]

    def gates(self):
        self.sums[...] = jnp.zeros_like(self.sums)
        gates_pre(self.rows, 256, self.conv, self.w_cat, self.pre_s)

    def factors(self, gated):
        @pl.loop(0, 8)
        def _(s):
            t0 = pl.multiple_of(s * self.seg, self.seg)
            at = pl.ds(t0, self.seg)
            c = self.masks[at, 0:1]
            for j, cols in enumerate(self.tiles):
                cols_i = slice(self.width + j * LANES, self.width + (j + 1) * LANES)
                r = jax.nn.sigmoid(self.pre_s[at, cols] + self.vecs[5:6, cols])
                self.pre_s[at, cols] = r
                self.pre_s[at, cols_i] = jax.nn.sigmoid(self.pre_s[at, cols_i] + self.vecs[6:7, cols])
                log_a = (-decay_scale * self.vecs[7:8, cols]) * r
                a = jnp.exp(log_a)
                d = self.a_s[at, cols]
                self.a_s[at, cols] = a
                self.n_s[at, cols] = jnp.sqrt(minus_expm1(2.0 * log_a, a * a))
                self.ac_s[j, at, :] = a * c
                act, slope = gelu_parts(gated[at, cols])
                self.e_s[j, at, :] = d * act
                self.dgated[at, cols] = (d * self.states[at, cols] * slope).astype(BF16)

    def scan(self):
        row = lax.broadcasted_iota(jnp.int32, (8, LANES), 0)

        def step(q, carry):
            at = pl.ds(pl.multiple_of((self.rows // 8 - 1 - q) * 8, 8), 8)
            out = []
            for j in range(len(self.tiles)):
                e, later = carry[j]
                now = self.ac_s[j, at, :]
                a = jnp.where(row == 7, later, pltpu.roll(now, 7, 0))
                b = self.e_s[j, at, :]
                for s in (1, 2, 4):
                    b = b + a * jnp.where(row < 8 - s, pltpu.roll(b, 8 - s, 0), 0.0)
                    a = a * jnp.where(row < 8 - s, pltpu.roll(a, 8 - s, 0), 1.0)
                b = b + a * e
                self.e_s[j, at, :] = b
                out.append((jnp.broadcast_to(b[0:1, :], (8, LANES)), jnp.broadcast_to(now[0:1, :], (8, LANES))))
            return tuple(out)

        none = jnp.zeros((8, LANES), F32)
        lax.fori_loop(0, self.rows // 8, step, tuple((none, none) for _ in self.tiles), unroll=2)

    def gate_gradients(self):
        seg, width = self.seg, self.width

        @pl.loop(0, 8)
        def _(s):
            t0 = pl.multiple_of(s * seg, seg)
            at = pl.ds(t0, seg)
            before = pl.multiple_of(jnp.maximum(t0 - 8, 0), 8)
            c = self.masks[at, 0:1]
            for j, cols in enumerate(self.tiles):
                cols_i = slice(width + j * LANES, width + (j + 1) * LANES)
                e = self.e_s[j, at, :]
                ext = jnp.concatenate([self.states[pl.ds(before, 8), cols], self.states[at, cols]], axis=0)
                earlier = pltpu.roll(ext, 1, 0)[8:]
                r, i, a, n = self.pre_s[at, cols], self.pre_s[at, cols_i], self.a_s[at, cols], self.n_s[at, cols]
                cv = self.conv[at, cols].astype(F32)
                ec = e * c
                d_log = a * (ec * earlier) - ec * i * cv * (a * a / n)
                rr = d_log * r
                dr = ((-decay_scale * self.vecs[7:8, cols]) * rr * (1.0 - r)).astype(BF16)
                em = e * ((1.0 - c) + c * n) * i
                di = (em * cv * (1.0 - i)).astype(BF16)
                self.dri[at, cols] = dr
                self.dri[at, cols_i] = di
                self.n_s[at, cols] = em
                self.sums[5, :, cols] += fold_rows(dr.astype(F32))
                self.sums[6, :, cols] += fold_rows(di.astype(F32))
                self.sums[7, :, cols] += fold_rows(rr)

        @pl.loop(0, self.rows // 256)
        def _(i):
            at = pl.ds(pl.multiple_of(i * 256, 256), 256)
            self.n_s[at, :] += dot_nt(self.dri[at, :], self.w_cat[...])

        self.n_s[self.rows : self.rows + 8, :] = jnp.zeros((8, width), F32)

    def convolution(self):
        @pl.loop(0, 8)
        def _(s):
            t0 = pl.multiple_of(s * self.seg, self.seg)
            at, ext = pl.ds(t0, self.seg), pl.ds(t0, self.seg + 8)
            same = [self.masks[ext, k : k + 1] for k in range(3)]
            for cols in self.tiles:
                d = self.n_s[ext, cols]
                b = self.branch[at, cols]
                self.sums[4, :, cols] += fold_rows(d[: self.seg])
                self.sums[0, :, cols] += fold_rows(d[: self.seg] * b)
                total = self.vecs[0:1, cols] * d[: self.seg]
                for k in range(1, 4):
                    moved = pltpu.roll(d * same[k - 1], self.seg + 8 - k, 0)[: self.seg]
                    total = total + self.vecs[k : k + 1, cols] * moved
                    self.sums[k, :, cols] += fold_rows(moved * b)
                self.dbranch[at, cols] = total.astype(BF16)


def dot_nt(left, right):
    return lax.dot_general(left, right, (((1,), (1,)), ((), ())), preferred_element_type=F32)


class Stage:
    def __init__(self, stride, size, later):
        self.stride, self.size, self.later = stride, size, later
        self.blocks = 1
        for s in later:
            self.blocks *= s.size
        self.digit = lax.rem(lax.axis_index("dp") // stride, size)

    def offset(self, position):
        total = 0
        for s in reversed(self.later):
            total = total + lax.rem(position, s.size) * s.stride
            position = position // s.size
        return total


def digit_sizes(n):
    if n == 8:
        return [2, 4]
    sizes = []
    while n > 1:
        m = 4 if n % 4 == 0 else 2 if n % 2 == 0 else n
        sizes.append(m)
        n //= m
    return sizes


def make_stages(n, last_first):
    digits, stride = [], 1
    for m in digit_sizes(n):
        digits.append((stride, m))
        stride *= m
    if last_first:
        digits = digits[1:] + digits[:1]
    stages = []
    for stride, m in reversed(digits):
        stages.insert(0, Stage(stride, m, list(stages)))
    return stages


class Item:
    def __init__(self, stages, left, right, width, ready, refs, resident=None):
        self.stages, self.left, self.right, self.width, self.ready = stages, left, right, width, ready
        self.resident = resident
        self.columns = right.shape[1]
        self.out, self.recv, self.send, self.send_sem, self.recv_sem = refs

    def message(self, t, back, k, slot, rows=None):
        stage = self.stages[t]
        rows = pl.ds(0, stage.blocks * self.width) if rows is None else rows
        step = jnp.where(back, -stage.stride, stage.stride)
        return pltpu.make_async_remote_copy(
            src_ref=self.send[t].at[slot, rows],
            dst_ref=self.recv[t].at[back, k - 1, rows],
            send_sem=self.send_sem[t].at[slot],
            recv_sem=self.recv_sem[t].at[back, k - 1],
            device_id={"dp": lax.axis_index("dp") + step},
            device_id_type=pl.DeviceIdType.MESH,
        )


class Engine:
    def __init__(self, left_s, got_s, total_s, sem, out_s=None, out_sem=None):
        self.left_s, self.got_s, self.total_s, self.sem = left_s, got_s, total_s, sem
        self.out_s, self.out_sem, self.finished = out_s, out_sem, None

    def fetch(self, item, block, slot):
        if len(item.left.shape) == 3:
            source = item.left.at[block]
        else:
            size = max(item.width, LANES)
            source = item.left.at[:, pl.ds(pl.multiple_of(block // (size // item.width) * size, size), size)]
        return pltpu.make_async_copy(source, self.left_s.at[slot], self.sem.at[slot])

    def columns(self, item, block, slot):
        held = self.left_s[slot]
        if held.shape[1] == item.width:
            return held
        pieces = [held[:, i * item.width : (i + 1) * item.width] for i in range(held.shape[1] // item.width)]
        value = pieces[0]
        for i, piece in enumerate(pieces[1:], 1):
            value = jnp.where(lax.rem(block, len(pieces)) == i, piece, value)
        return value

    def products(self, item, count, block_of, store, done):
        tile = item.columns // 2 if item.columns > 1024 else item.columns

        def compute(p, left):
            if tile == item.columns:
                store(p, pl.ds(0, tile), dot_tn(left(), item.right[...]))
            else:

                @pl.loop(0, item.columns // tile)
                def _(c):
                    cols = pl.ds(pl.multiple_of(c * tile, tile), tile)
                    store(p, cols, dot_tn(left(), item.right[:, cols]))

            done(p)

        if item.resident is not None:

            @pl.loop(0, count)
            def _(p):
                cols = pl.ds(pl.multiple_of(block_of(p) * item.width, item.width), item.width)
                compute(p, lambda: item.resident[:, cols])

            return
        self.fetch(item, block_of(0), 0).start()

        @pl.loop(0, count)
        def _(p):
            slot = lax.rem(p, 2)
            if count > 1:

                @pl.when(p + 1 < count)
                def _():
                    self.fetch(item, block_of(p + 1), 1 - slot).start()

            self.fetch(item, block_of(p), slot).wait()
            compute(p, lambda: self.columns(item, block_of(p), slot))

    def got_copy(self, item, i, source):
        return pltpu.make_async_copy(source, self.got_s.at[i, :, pl.ds(0, item.columns)], self.sem.at[2 + i])

    def start_gots(self, item, first, gots):
        for i, (condition, source) in enumerate(gots):

            @pl.when(condition)
            def _(i=i, source=source):
                self.got_copy(item, first + i, source).start()

    def add_gots(self, item, gots, put):
        for i, (condition, source) in enumerate(gots):

            @pl.when(condition)
            def _(i=i, source=source):
                self.got_copy(item, i, source).wait()

        @pl.loop(0, item.width // 16)
        def _(r):
            at = pl.ds(pl.multiple_of(r * 16, 16), 16)
            total = self.total_s[at, pl.ds(0, item.columns)]
            for i, (condition, _) in enumerate(gots):
                total = total + jnp.where(condition, self.got_s[i, at, pl.ds(0, item.columns)].astype(F32), 0.0)
            put(at, total)

    def arrived(self, item, t, position):
        found, last_found = [], []
        for u in range(t):
            stage = item.stages[u]
            spot = position
            scale = 1
            for s in item.stages[t:]:
                scale *= s.size
            lead = 0
            for s in item.stages[u + 1 : t]:
                lead = lead * s.size + s.digit
            rows = pl.ds((lead * scale + spot) * item.width, item.width)
            last = stage.size - 2
            if stage.size == 2:
                back = jnp.where(stage.digit == 0, 1, 0)
                (last_found if u == t - 1 else found).append((stage.digit >= 0, item.recv[u].at[back, last, rows]))
            else:
                (last_found if u == t - 1 else found).append((stage.digit >= 1, item.recv[u].at[0, last, rows]))
                (last_found if u == t - 1 else found).append((stage.digit <= stage.size - 2, item.recv[u].at[1, last, rows]))
        return found, last_found

    def own_base(self, item, t):
        base = 0
        for s in item.stages[:t]:
            base = base + s.digit * s.stride
        return base

    def wait_last(self, item, t):
        if t < item.ready:
            return
        stage = item.stages[t]
        for back in range(2):
            me = stage.digit if back == 0 else stage.size - 1 - stage.digit

            @pl.when(me >= 1)
            def _(back=back):
                item.message(t, back, stage.size - 1, 0).wait_recv()

    def round(self, item, t, k):
        stage = item.stages[t]
        base = self.own_base(item, t)
        alone = t == 0 and k == 1
        if k == 1 and t > 0:
            self.wait_last(item, t - 1)

        @pl.loop(0, 2)
        def _(back):
            me = jnp.where(back == 0, stage.digit, stage.size - 1 - stage.digit)
            there = me + stage.size - k
            value = jnp.where(back == 0, there, stage.size - 1 - there)
            slot = jnp.where(value > stage.digit, value - 1, value)

            def rows_of(p):
                return pl.ds(pl.multiple_of(p * item.width, item.width), item.width)

            def gots_of(p):
                earlier = sum(self.arrived(item, t, value * stage.blocks + p), [])
                return earlier, [(me >= 1, item.recv[t].at[back, k - 2, rows_of(p)])] if k > 1 else []

            @pl.when(me <= k - 1)
            def _():
                if not alone:
                    self.start_gots(item, 0, gots_of(0)[0])

                def store(p, cols, total):
                    if alone:
                        item.send[t][slot, rows_of(p), cols] = total.astype(BF16)
                    else:
                        self.total_s[:, cols] = total

                def done(p):
                    if not alone:
                        if k > 1:

                            @pl.when((me >= 1) & (p == 0))
                            def _():
                                item.message(t, back, k - 1, 0).wait_recv()

                        def put(at, value):
                            rows = pl.ds(pl.multiple_of(p * item.width + at.start, 16), 16)
                            item.send[t][slot, rows, :] = value.astype(BF16)

                        earlier, own = gots_of(p)
                        self.start_gots(item, len(earlier), own)
                        self.add_gots(item, earlier + own, put)

                        @pl.when(p + 1 < stage.blocks)
                        def _():
                            self.start_gots(item, 0, gots_of(p + 1)[0])

                    item.message(t, back, k, slot, rows_of(p)).start()

                self.products(item, stage.blocks, lambda p: base + value * stage.stride + stage.offset(p), store, done)

    def out_copy(self, item):
        return pltpu.make_async_copy(self.out_s.at[:, pl.ds(0, item.columns)], item.out, self.out_sem)

    def finish(self, item):
        t = len(item.stages)
        self.wait_last(item, t - 1)
        gots = sum(self.arrived(item, t, 0), [])
        self.start_gots(item, 0, gots)

        def store(p, cols, total):
            self.total_s[:, cols] = total

        def put(at, value):
            self.out_s[at, pl.ds(0, item.columns)] = value

        self.settle()
        self.products(item, 1, lambda p: self.own_base(item, t), store, lambda p: self.add_gots(item, gots, put))
        self.out_copy(item).start()
        self.finished = item

    def settle(self):
        if self.finished is not None:
            self.out_copy(self.finished).wait()
        self.finished = None

    def drain(self, item, stages):
        for t in stages:
            for slot in range(item.stages[t].size - 1):
                item.message(t, 0, 1, slot).wait_send()


def stage_shapes(n, last_first, width, columns):
    sizes = digit_sizes(n)
    if last_first:
        sizes = sizes[1:] + sizes[:1]
    left, found = n, []
    for t, m in enumerate(sizes):
        left //= m
        found.append(
            (
                jax.ShapeDtypeStruct((2, m - 1, left * width, columns), BF16),
                pltpu.VMEM((m - 1, left * width, columns), BF16),
                pltpu.SemaphoreType.DMA((m - 1,)),
                pltpu.SemaphoreType.DMA((2, m - 1)),
            )
        )
    return found


def dot_tn(left, right):
    return lax.dot_general(left, right, (((0,), (0,)), ((), ())), preferred_element_type=F32)


class Reader:
    def __init__(self, refs):
        self.refs, self.at = refs, 0

    def __call__(self, count=None):
        start = self.at
        self.at += 1 if count is None else count
        return self.refs[start] if count is None else list(self.refs[start : self.at])


def column_blocks(left, n):
    tokens, features = left.shape
    width = features // n
    return left.reshape(tokens, n, width).transpose(1, 0, 2) if width % LANES else left


class TensorLine:
    def __init__(self):
        self.index = lax.axis_index("tensor")
        self.mate, self.peer, self.cross = self.index ^ 1, self.index ^ 2, self.index ^ 3


def copy_in(source, target, sem):
    copy = pltpu.make_async_copy(source, target, sem)
    copy.start()
    return copy


def remote(source, target, send_sem, recv_sem, axis, index):
    return pltpu.make_async_remote_copy(
        src_ref=source, dst_ref=target, send_sem=send_sem, recv_sem=recv_sem,
        device_id={axis: index}, device_id_type=pl.DeviceIdType.MESH,
    )


class TensorReduce:
    def __init__(self, line, part, from_mate, from_peer, own_v, got_v, send_v, send_sem, recv_sem, sem):
        self.line, self.part, self.from_mate, self.from_peer = line, part, from_mate, from_peer
        self.own_v, self.got_v, self.send_v, self.sem = own_v, got_v, send_v, sem
        self.rows = part.shape[0] // 4
        self.mates = [
            remote(self.block(line.cross), from_mate.at[0], send_sem.at[0], recv_sem.at[0], "tensor", line.mate),
            remote(self.block(line.mate), from_mate.at[1], send_sem.at[1], recv_sem.at[1], "tensor", line.mate),
        ]
        self.over = remote(send_v, from_peer, send_sem.at[2], recv_sem.at[2], "tensor", line.peer)

    def block(self, index):
        return self.part.at[pl.ds(pl.multiple_of(index * self.rows, self.rows), self.rows)]

    def start(self):
        for copy in self.mates:
            copy.start()

    def own_rows(self, index, at):
        if self.own_v is not None:
            return self.own_v[at, :].astype(F32)
        return self.part[pl.ds(pl.multiple_of(index * self.rows + at.start, 16), 16), :].astype(F32)

    def fetch_own(self, index):
        return [] if self.own_v is None else [copy_in(self.block(index), self.own_v, self.sem.at[0])]

    def middle(self):
        copies = self.fetch_own(self.line.peer)
        self.mates[0].wait_recv()
        copies.append(copy_in(self.from_mate.at[0], self.got_v.at[0], self.sem.at[1]))
        for copy in copies:
            copy.wait()

        @pl.loop(0, self.rows // 16)
        def _(r):
            at = pl.ds(pl.multiple_of(r * 16, 16), 16)
            self.send_v[at, :] = (self.own_rows(self.line.peer, at) + self.got_v[0, at, :].astype(F32)).astype(BF16)

        self.over.start()

    def end(self, use):
        copies = self.fetch_own(self.line.index)
        self.mates[1].wait_recv()
        copies.append(copy_in(self.from_mate.at[1], self.got_v.at[0], self.sem.at[1]))
        self.over.wait_recv()
        copies.append(copy_in(self.from_peer, self.got_v.at[1], self.sem.at[2]))
        for copy in copies:
            copy.wait()

        @pl.loop(0, self.rows // 16)
        def _(r):
            at = pl.ds(pl.multiple_of(r * 16, 16), 16)
            use(at, self.own_rows(self.line.index, at) + self.got_v[0, at, :].astype(F32) + self.got_v[1, at, :].astype(F32))

    def drain(self):
        for copy in self.mates:
            copy.wait_send()
        self.over.wait_send()

    @staticmethod
    def results(tokens, features):
        return [jax.ShapeDtypeStruct((2, tokens // 4, features), BF16), jax.ShapeDtypeStruct((tokens // 4, features), BF16)]

    @staticmethod
    def semaphores():
        return [pltpu.SemaphoreType.DMA((3,)), pltpu.SemaphoreType.DMA((3,)), pltpu.SemaphoreType.DMA((3,))]

    @staticmethod
    def buffers(tokens, features):
        rows = tokens // 4
        return [pltpu.VMEM((2, rows, features), BF16), pltpu.VMEM((rows, features), BF16)]


def norm_backward(values, gain, d_normed):
    inverse = lax.rsqrt(jnp.mean(values * values, axis=-1, keepdims=True) + epsilon)
    weighted = gain * d_normed
    inner = jnp.mean(weighted * values, axis=-1, keepdims=True)
    return inverse * weighted - values * (inverse * inverse * inverse * inner), d_normed * values * inverse


HBM = pl.BlockSpec(memory_space=pl.ANY)
IN_VMEM = pl.BlockSpec(memory_space=pltpu.VMEM)


class TensorGather:
    def __init__(self, line, own_v, out, send_sem, recv_sem):
        self.line, self.own_v, self.out, self.rows = line, own_v, out, own_v.shape[0]
        self.over = remote(own_v, self.block(line.index), send_sem.at[0], recv_sem.at[0], "tensor", line.peer)
        self.aside = remote(own_v, self.block(line.index), send_sem.at[1], recv_sem.at[1], "tensor", line.mate)
        self.onward = remote(self.block(line.peer), self.block(line.peer), send_sem.at[2], recv_sem.at[2], "tensor", line.mate)

    def block(self, index):
        return self.out.at[pl.ds(pl.multiple_of(index * self.rows, self.rows), self.rows)]

    def start(self):
        self.over.start()
        self.aside.start()

    def forward(self):
        self.over.wait_recv()
        self.onward.start()

    def drain(self):
        for copy in (self.over, self.aside, self.onward):
            copy.wait_send()

    @staticmethod
    def semaphores():
        return [pltpu.SemaphoreType.DMA((3,)), pltpu.SemaphoreType.DMA((3,))]


def main_kernel(n, width, units, *refs):
    take = Reader(refs)
    cot_own, w_first, w_branch, w_out, w_gate, w_up, w_down = take(7)
    stream, gain_one, gain, masks, vecs, w_cat = take(6)
    normed, cot, gated, branch, conv, states, product, middle, normed_two, from_mate_one, from_peer_one = take(11)
    d_middle, att, hidden_o, dgate_o, dup_o, dgated_o, dri_o, dbranch_o, part_out, dense_o, from_mate, from_peer = take(12)
    down_recv, (gate_recv, up_recv) = take(2), take(2)
    sums, gain_grad = take(2)
    (att_v,) = take(1)
    one_sems, cot_sems, two_sems, one_rs = take(2), take(2), take(2), take(3)
    one_sem, rs_send, rs_recv, rs_sem, ag_send, ag_recv, sem, engine_sem = take(8)
    item_sems = [take(2) for _ in range(4)]
    rows, features = stream.shape
    tokens, channels = conv.shape
    tile = 512
    line = TensorLine()
    twos = TensorGather(line, att_v, normed_two, *two_sems)
    two_v = att_v

    def forward_phase(
        wg_v, wb_v, wo_v, own_v, cot_v, block_v, gated_v, branch_v, conv_v, states_v, product_v,
        pre_s, a_s, b_s, part_v, rs_got, rs_send_v, middle_v,
    ):
        ones = TensorGather(line, own_v, normed, *one_sems)
        cots = TensorGather(line, cot_v, cot, *cot_sems)
        reduce = TensorReduce(line, part_v, from_mate_one, from_peer_one, None, rs_got, rs_send_v, *one_rs)
        loads = [copy_in(w_first, wg_v, one_sem.at[0]), copy_in(w_branch, wb_v, one_sem.at[1]), copy_in(w_out, wo_v, one_sem.at[2])]
        cot_load = copy_in(cot_own, cot_v, one_sem.at[3])

        def chunks(body):
            @pl.loop(0, rows // 16)
            def _(r):
                body(pl.ds(pl.multiple_of(r * 16, 16), 16))

        def norm(values, gains):
            inverse = lax.rsqrt(jnp.mean(values * values, axis=-1, keepdims=True) + epsilon)
            return (values * inverse * gains).astype(BF16)

        def first_norm(at):
            own_v[at, :] = norm(stream[at, :].astype(F32), gain_one[...])

        chunks(first_norm)
        ones.start()
        keep = [copy_in(own_v, ones.block(line.index), one_sem.at[4])]
        cot_load.wait()
        cots.start()
        keep.append(copy_in(cot_v, cots.block(line.index), one_sem.at[5]))

        def project(source, index):
            at = pl.ds(pl.multiple_of(index * rows, rows), rows)
            branch_v[at, :] = jnp.dot(source, wb_v[...], preferred_element_type=F32)
            gated_v[at, :] = jnp.dot(source, wg_v[...], preferred_element_type=F32)

        loads[0].wait()
        loads[1].wait()

        @pl.loop(0, 4)
        def _(b):
            index = line.index ^ b

            @pl.when(b == 0)
            def _():
                copy_in(own_v, block_v, one_sem.at[6]).wait()

            @pl.when(b == 1)
            def _():
                ones.aside.wait_recv()

            @pl.when(b == 2)
            def _():
                ones.forward()

            @pl.when(b == 3)
            def _():
                ones.onward.wait_recv()

            @pl.when(b > 0)
            def _():
                copy_in(ones.block(index), block_v, one_sem.at[6]).wait()

            project(block_v[...], index)

        outs = [copy_in(branch_v, branch, one_sem.at[7]), copy_in(gated_v, gated, one_sem.at[8])]
        mixer_forward_kernel(branch_v, gated_v, masks, vecs, w_cat, conv_v, states_v, product_v, pre_s, a_s, b_s)
        outs += [copy_in(conv_v, conv, one_sem.at[9]), copy_in(states_v, states, one_sem.at[10]), copy_in(product_v, product, one_sem.at[11])]
        loads[2].wait()

        def out_block(index):
            at = pl.ds(pl.multiple_of(index * rows, rows), rows)
            part_v[at, :] = jnp.dot(product_v[at, :], wo_v[...], preferred_element_type=F32).astype(BF16)

        @pl.loop(0, 4)
        def _(q):
            out_block(line.cross ^ q)

            @pl.when(q == 0)
            def _():
                reduce.mates[0].start()

            @pl.when(q == 1)
            def _():
                reduce.middle()

            @pl.when(q == 2)
            def _():
                reduce.mates[1].start()

        cots.forward()

        def second_norm(at, total):
            values = stream[at, :].astype(F32) + total
            middle_v[at, :] = values
            two_v[at, :] = norm(values, gain[...])

        reduce.end(second_norm)
        twos.start()
        keep += [copy_in(two_v, twos.block(line.index), one_sem.at[12]), copy_in(middle_v, middle, one_sem.at[13])]
        cots.aside.wait_recv()
        cots.onward.wait_recv()
        for copy in keep + outs:
            copy.wait()
        for gathered in (ones, cots):
            gathered.drain()
        reduce.drain()

    block = pltpu.VMEM((rows, features), BF16)
    wide = pltpu.VMEM((tokens, channels), F32)
    narrow = pltpu.VMEM((tokens, channels), BF16)
    lanes = pltpu.VMEM((channels // LANES, tokens, LANES), F32)
    pl.run_scoped(
        forward_phase,
        pltpu.VMEM(w_first.shape, BF16), pltpu.VMEM(w_branch.shape, BF16), pltpu.VMEM(w_out.shape, BF16),
        block, block, block,
        wide, wide, narrow, wide, narrow,
        pltpu.VMEM((tokens, 2 * channels), F32), lanes, lanes,
        pltpu.VMEM((tokens, features), BF16), *TensorReduce.buffers(tokens, features),
        pltpu.VMEM((rows, features), F32),
    )

    def backward_phase(hidden, *held):
        down_one, down_two, gate_send, up_send, left_s, got_s, total_s = held
        halves = [(down_one, *item_sems[0]), (down_two, *item_sems[1])]
        (gate_ss, gate_rs), (up_ss, up_rs) = item_sems[2:]
        engine = Engine(left_s, got_s, total_s, engine_sem)
        downs = [
            Item(
                make_stages(n, True), cot, hidden.at[:, pl.ds(q * (units // 2), units // 2)], width, 0,
                (None, [down_recv[q]], [send], [send_sem], [recv_sem]),
            )
            for q, (send, send_sem, recv_sem) in enumerate(halves)
        ]
        gather = TensorGather(line, att_v, att, ag_send, ag_recv)

        def rounds(item):
            return list(range(1, item.stages[0].size))

        def row_block(ref, index):
            return ref.at[pl.ds(pl.multiple_of(index * rows, rows), rows)]

        first, between, last = rounds(downs[0])[:1], rounds(downs[0])[1:-1], rounds(downs[0])[1:][-1:]
        gate = Item(make_stages(n, False), normed_two, hidden, width, 0, (None, [gate_recv], [gate_send], [gate_ss], [gate_rs]))
        half = hidden.at[:, pl.ds(0, units // 2)]
        up = Item(make_stages(n, False), normed_two, half, width, 0, (None, [up_recv], [up_send], [up_ss], [up_rs]))

        def take_rounds(item, numbers):
            for k in numbers:
                engine.round(item, 0, k)

        def tensor_phase(wg_v, wu_v, wd_v, dgate, dup, x_v, c_v, part, got_v, send_v, dmid_v, cot_v):
            gate.right, up.right = dgate, dup.at[:, pl.ds(0, units // 2)]
            weights = [copy_in(w_gate, wg_v, sem.at[0]), copy_in(w_up, wu_v, sem.at[1]), copy_in(w_down, wd_v, sem.at[2])]
            loads = [copy_in(middle, dmid_v, sem.at[3]), copy_in(row_block(cot, line.index), cot_v, sem.at[4])]
            copy_in(row_block(normed_two, line.index), x_v, sem.at[5])
            copy_in(row_block(cot, line.index), c_v, sem.at[6])
            for load in weights:
                load.wait()

            @pl.loop(0, 4)
            def _(b):
                index = line.index ^ b
                at = pl.ds(pl.multiple_of(index * rows, rows), rows)
                pltpu.make_async_copy(row_block(normed_two, index), x_v, sem.at[5]).wait()
                pltpu.make_async_copy(row_block(cot, index), c_v, sem.at[6]).wait()

                @pl.loop(0, units // tile)
                def _(j):
                    cols = pl.ds(pl.multiple_of(j * tile, tile), tile)
                    gate_pre = jnp.dot(x_v[...], wg_v[:, cols], preferred_element_type=F32)
                    up_pre = jnp.dot(x_v[...], wu_v[:, cols], preferred_element_type=F32)
                    d_hidden = dot_nt(c_v[...], wd_v[cols, :])
                    act, slope = gelu_parts(gate_pre)
                    hidden[at, cols] = (act * up_pre).astype(BF16)
                    dgate[at, cols] = (d_hidden * up_pre * slope).astype(BF16)
                    dup[at, cols] = (d_hidden * act).astype(BF16)

                @pl.when(b == 0)
                def _():
                    twos.aside.wait_recv()

                @pl.when(b == 1)
                def _():
                    twos.forward()

                @pl.when(b == 2)
                def _():
                    twos.onward.wait_recv()

                @pl.when(b < 3)
                def _():
                    following = line.index ^ (b + 1)
                    copy_in(row_block(normed_two, following), x_v, sem.at[5])
                    copy_in(row_block(cot, following), c_v, sem.at[6])

            twos.drain()
            outs = [copy_in(hidden, hidden_o, sem.at[0]), copy_in(dgate, dgate_o, sem.at[1]), copy_in(dup, dup_o, sem.at[2])]
            for item in downs:
                take_rounds(item, first)
            take_rounds(gate, rounds(gate))

            def stage(index, value):
                @pl.loop(0, features // tile)
                def _(j):
                    at, cols = pl.ds(pl.multiple_of(index * rows, rows), rows), pl.ds(pl.multiple_of(j * tile, tile), tile)
                    part[at, cols] = value(at, cols).astype(BF16)

            def two(at, cols):
                return dot_nt(dgate[at, :], wg_v[cols, :]) + dot_nt(dup[at, :], wu_v[cols, :])

            def out(at, cols):
                return jnp.dot(hidden[at, :], wd_v[:, cols], preferred_element_type=F32)

            reduce = TensorReduce(line, part, from_mate, from_peer, None, got_v, send_v, rs_send, rs_recv, rs_sem)
            @pl.loop(0, 4)
            def _(q):
                stage(line.cross ^ q, two)

                @pl.when(q == 0)
                def _():
                    reduce.mates[0].start()

                @pl.when(q == 1)
                def _():
                    reduce.middle()

                @pl.when(q == 2)
                def _():
                    reduce.mates[1].start()

            for item in downs:
                take_rounds(item, between)
            for load in loads:
                load.wait()
            gain_grad[...] = jnp.zeros_like(gain_grad)

            def use(at, total):
                back, terms = norm_backward(dmid_v[at, :], gain[...], total)
                value = cot_v[at, :].astype(F32) + back
                dmid_v[at, :] = value
                att_v[at, :] = value.astype(BF16)
                gain_grad[...] += fold_rows(terms)

            reduce.end(use)
            gather.start()
            keep = [copy_in(att_v, gather.block(line.index), sem.at[3]), copy_in(dmid_v, d_middle, sem.at[4])]
            take_rounds(up, rounds(up))
            reduce.drain()

            @pl.loop(0, 4)
            def _(b):
                stage(b, out)
                copy_in(row_block(part, b), row_block(part_out, b), sem.at[7])

            take_rounds(downs[0], last)
            gather.forward()
            for copy in outs + keep:
                copy.wait()
            pltpu.make_async_copy(part, part_out, sem.at[7]).wait()

        weight = pltpu.VMEM((features, units), BF16)
        block = pltpu.VMEM((rows, features), BF16)
        pl.run_scoped(
            tensor_phase,
            weight, weight, pltpu.VMEM((units, features), BF16),
            pltpu.VMEM((tokens, units), BF16), pltpu.VMEM((tokens, units), BF16),
            block, block, pltpu.VMEM((tokens, features), BF16),
            *TensorReduce.buffers(tokens, features),
            pltpu.VMEM((rows, features), F32), block,
        )

        def mixer_phase(gated_v, states_v, conv_v, dgated_v, dri_v, dbranch_v, block_v, w_v, dense_v, *scratch):
            loads = [copy_in(conv, conv_v, sem.at[1]), copy_in(w_out, w_v, sem.at[0])]
            loads += [copy_in(gated, gated_v, sem.at[2]), copy_in(states, states_v, sem.at[3])]
            mixer = MixerBackward(masks, vecs, w_cat, states_v, gated_v, conv_v, dgated_v, dri_v, dbranch_v, sums, *scratch)
            loads[0].wait()
            mixer.gates()
            take_rounds(downs[1], last)
            loads[1].wait()

            def product_gradient(index, source):
                mixer.a_s[pl.ds(pl.multiple_of(index * rows, rows), rows), :] = dot_nt(source[...], w_v[...])

            def block_copy(b):
                slot = lax.rem(b, 2)
                return pltpu.make_async_copy(row_block(att, line.index ^ b), block_v.at[slot], sem.at[4 + slot])

            block_copy(0).start()

            @pl.loop(0, 4)
            def _(b):
                @pl.when(b == 0)
                def _():
                    gather.aside.wait_recv()

                @pl.when(b == 2)
                def _():
                    gather.onward.wait_recv()

                @pl.when(b < 3)
                def _():
                    block_copy(b + 1).start()

                block_copy(b).wait()
                product_gradient(line.index ^ b, block_v.at[lax.rem(b, 2)])

            loads[2].wait()
            loads[3].wait()
            mixer.factors(gated_v)
            again = copy_in(branch, gated_v, sem.at[2])
            outs = [copy_in(dgated_v, dgated_o, sem.at[1])]
            mixer.scan()
            mixer.gate_gradients()
            outs.append(copy_in(dri_v, dri_o, sem.at[3]))
            again.wait()
            mixer.convolution()
            outs.append(copy_in(dbranch_v, dbranch_o, sem.at[0]))

            @pl.loop(0, 2 * channels // 256)
            def _(j):
                cols = pl.ds(pl.multiple_of(j * 256, 256), 256)
                dense_v[:, cols] = dot_tn(conv_v[...], dri_v[:, cols])

            outs.append(copy_in(dense_v, dense_o, sem.at[4]))
            for copy in outs:
                copy.wait()

        pl.run_scoped(
            mixer_phase,
            pltpu.VMEM((tokens, channels), F32),
            pltpu.VMEM((tokens, channels), F32),
            pltpu.VMEM((tokens, channels), BF16),
            pltpu.VMEM((tokens, channels), BF16),
            pltpu.VMEM((tokens, 2 * channels), BF16),
            pltpu.VMEM((tokens, channels), BF16),
            pltpu.VMEM((2, rows, features), BF16),
            pltpu.VMEM((channels, features), BF16),
            pltpu.VMEM((channels, 2 * channels), F32),
            *MixerBackward.scratch(tokens, channels),
        )
        gather.drain()
        for item in (*downs, gate, up):
            engine.drain(item, [0])
            engine.wait_last(item, 0)

    down = stage_shapes(n, True, width, units // 2)[0][1]
    gate = stage_shapes(n, False, width, units)[0][1]
    up = stage_shapes(n, False, width, units // 2)[0][1]
    pl.run_scoped(
        backward_phase,
        pltpu.VMEM((tokens, units), BF16), down, down, gate, up,
        pltpu.VMEM((2, tokens, max(width, LANES)), BF16),
        pltpu.VMEM((2, width, units), BF16),
        pltpu.VMEM((width, units), F32),
    )


def main_part(cot_own, w_first, w_branch, w_out, w_gate, w_up, w_down, stream, gain_one, gain_two, masks, vecs, w_cat):
    n = lax.axis_size("dp")
    rows, features = stream.shape
    tokens, channels, units, width = 4 * rows, w_first.shape[1], w_gate.shape[1], features // n
    down = stage_shapes(n, True, width, units // 2)[0]
    gate = stage_shapes(n, False, width, units)[0]
    up = stage_shapes(n, False, width, units // 2)[0]
    dma = pltpu.SemaphoreType.DMA
    whole = jax.ShapeDtypeStruct((tokens, features), BF16)
    part = jax.ShapeDtypeStruct((rows, features), F32)
    hide = jax.ShapeDtypeStruct((tokens, units), BF16)
    wide = jax.ShapeDtypeStruct((tokens, channels), F32)
    narrow = jax.ShapeDtypeStruct((tokens, channels), BF16)
    sums = TensorReduce.results(tokens, features)
    results = [whole, whole, wide, wide, narrow, wide, narrow, part, whole, *sums]
    results += [part, whole, hide, hide, hide, narrow, jax.ShapeDtypeStruct((tokens, 2 * channels), BF16), narrow, whole]
    results += [jax.ShapeDtypeStruct((channels, 2 * channels), F32), *sums]
    results += [down[0], down[0], gate[0], up[0]]
    gathers = TensorGather.semaphores()
    return pl.pallas_call(
        functools.partial(main_kernel, n, width, units),
        out_shape=[*results, jax.ShapeDtypeStruct((8, 8, channels), F32), jax.ShapeDtypeStruct((8, features), F32)],
        in_specs=[HBM] * 7 + [IN_VMEM] * 6,
        out_specs=[HBM] * len(results) + [IN_VMEM] * 2,
        scratch_shapes=[
            pltpu.VMEM((rows, features), BF16),
            *gathers, *gathers, *gathers, *TensorReduce.semaphores(), dma((14,)),
            *TensorReduce.semaphores(), *gathers, dma((8,)), dma((4,)),
            *down[2:4], *down[2:4], *gate[2:4], *up[2:4],
        ],
        compiler_params=pltpu.CompilerParams(vmem_limit_bytes=VMEM_BYTES, has_side_effects=True),
        cost_estimate=pl.CostEstimate(flops=60 * 10**9, bytes_accessed=120 * 10**6, transcendentals=14 * tokens * channels),
        name="main_part",
    )(cot_own, w_first, w_branch, w_out, w_gate, w_up, w_down, stream, gain_one, gain_two, masks, vecs, w_cat)


def gather_sums(gains, sends, recvs, send_sems, recv_sems):
    n, line = lax.axis_size("dp"), TensorLine()
    hops = [("tensor", line.mate), ("tensor", line.peer)]
    bit = 1
    while bit < n:
        hops.append(("dp", lax.axis_index("dp") ^ bit))
        bit *= 2
    copies = [remote(sends.at[s], recvs.at[s], send_sems.at[s], recv_sems.at[s], *hop) for s, hop in enumerate(hops)]

    def begin(s):
        sends[s] = gains[...] if s == 0 else sends[s - 1] + recvs[s - 1]
        copies[s].start()

    def step(s):
        if s > 0:
            copies[s - 1].wait_recv()
        if s < len(copies):
            begin(s)
        else:
            gains[...] = sends[s - 1] + recvs[s - 1]
            for copy in copies:
                copy.wait_send()

    return [functools.partial(step, s) for s in range(len(copies) + 1)]


def finish_kernel(n, width, plan, order, lefts_of, keep, readies, columns, out_of, *refs):
    take = Reader(refs)
    count, n_outs = len(plan), max(o for o, _ in out_of) + 1
    part_out, middle, d_middle, stream, w_gate, w_branch = take(6)
    gain, gain_grad_two = take(2)
    lefts, rights_hbm = take(max(lefts_of) + 1), take(n_outs)
    shapes = [stage_shapes(n, plan[i], width, columns[i]) for i in range(count)]
    given = [take(readies[i]) for i in range(count)]
    stream_grad_o, stream_out_o = take(2)
    outs = take(n_outs)
    (part,) = take(1)
    reduces = [take(2), take(2)]
    recv = [given[i] + take(len(shapes[i]) - readies[i]) for i in range(count)]
    (gains,) = take(1)
    rights = take(n_outs)
    wg_v, wb_v, stage_v = take(3)
    nones = [[None] * r for r in readies]
    sends = [nones[i] + take(len(shapes[i]) - readies[i]) for i in range(count)]
    send_sems = [nones[i] + take(len(shapes[i]) - readies[i]) for i in range(count)]
    recv_sems = [nones[i] + take(len(shapes[i]) - readies[i]) for i in range(count)]
    left_vs = take(max(lefts_of) + 1)
    left_s, got_s, total_s, out_s, own_v, got_v, send_v, send_w = take(8)
    value_v, base_v, gain_sends, gain_recvs = take(4)
    rs_sems = [take(3), take(3)]
    gain_ss, gain_rs, right_sem, sem, engine_sem, out_sem = take(6)

    line = TensorLine()
    engine = Engine(left_s, got_s, total_s, engine_sem, out_s, out_sem)
    tensor = [
        TensorReduce(line, source, *reduces[q], own_v, got_v, (send_v, send_w)[q], *rs_sems[q])
        for q, source in enumerate((part, part_out))
    ]
    tensor[1].start()
    loads, weights, left_loads = {}, [], {}

    def issue(kind, i):
        if kind == "left" and i in keep and i not in left_loads:
            left_loads[i] = copy_in(lefts[i], left_vs[i], right_sem.at[n_outs + 2 + i])
        if kind == "right" and i not in loads:
            loads[i] = copy_in(rights_hbm[i], rights[i], right_sem.at[i])

    def issue_for(i):
        if i >= 0:
            issue("right", out_of[i][0])
            issue("left", lefts_of[i])
        elif not weights:
            issue("right", n_outs - 2)
            issue("right", n_outs - 1)
            weights.extend([copy_in(w_gate, wg_v, right_sem.at[n_outs]), copy_in(w_branch, wb_v, right_sem.at[n_outs + 1])])

    loaded = set()

    def load_left(i):
        if left_loads.get(i) is not None:
            left_loads[i].wait()
            left_loads[i] = None

    def load(i):
        if i not in loaded:
            loads[i].wait()
            loaded.add(i)

    def columns_of(i):
        return pl.ds(out_of[i][1], columns[i])

    items = [
        Item(
            make_stages(n, plan[i]), lefts[lefts_of[i]], rights[out_of[i][0]].at[:, columns_of(i)], width, readies[i],
            (outs[out_of[i][0]].at[:, columns_of(i)], recv[i], sends[i], send_sems[i], recv_sems[i]),
            left_vs[lefts_of[i]] if lefts_of[i] in keep else None,
        )
        for i in range(count)
    ]

    rows, features = stream.shape

    def stage(index):
        at = pl.ds(pl.multiple_of(index * rows, rows), rows)

        @pl.loop(0, features // 512)
        def _(j):
            cols = pl.ds(pl.multiple_of(j * 512, 512), 512)
            total = dot_nt(rights[n_outs - 2][at, :], wg_v[cols, :]) + dot_nt(rights[n_outs - 1][at, :], wb_v[cols, :])
            stage_v[:, cols] = total.astype(BF16)

        copy_in(stage_v, tensor[0].block(index), sem.at[0]).wait()

    def stage_pair(first, mate):
        @pl.loop(0, 2)
        def _(q):
            stage(first ^ q)

            @pl.when(q == 0)
            def _():
                tensor[0].mates[mate].start()

    def part_first():
        for i in (n_outs - 2, n_outs - 1):
            load(i)
        for copy in weights:
            copy.wait()
        stage_pair(line.cross, 0)

    def part_second():
        stage_pair(line.mate, 1)

    def grad_end():
        copies = [copy_in(stream, value_v, sem.at[0]), copy_in(d_middle, base_v, sem.at[1])]
        for copy in copies:
            copy.wait()
        gains[...] = jnp.zeros_like(gains)

        def use(at, total):
            back, terms = norm_backward(value_v[at, :].astype(F32), gain[...], total)
            base_v[at, :] = base_v[at, :] + back
            gains[...] += fold_rows(terms)

        tensor[0].end(use)
        copy_in(base_v, stream_grad_o, sem.at[0]).wait()
        first = jnp.sum(gains[...], axis=0, keepdims=True)
        second = jnp.sum(gain_grad_two[...], axis=0, keepdims=True)
        pick = lax.broadcasted_iota(jnp.int32, gains.shape, 0)
        gains[...] = jnp.where(pick == 0, first, jnp.where(pick == 1, second, 0.0))

    def out_end():
        copy_in(middle, base_v, sem.at[0]).wait()

        def use(at, total):
            base_v[at, :] = base_v[at, :] + total

        tensor[1].end(use)
        copy_in(base_v, stream_out_o, sem.at[0]).wait()

    extra = [part_first, tensor[0].middle, part_second, tensor[1].middle, grad_end, out_end]
    extra += gather_sums(gains, gain_sends, gain_recvs, gain_ss, gain_rs)
    for at, (i, t, k) in enumerate(order):
        for ahead in order[at : at + 3]:
            issue_for(ahead[0])
        if i < 0:
            if extra:
                extra.pop(0)()
            continue
        load(out_of[i][0])
        load_left(lefts_of[i])
        if t < len(shapes[i]):
            engine.round(items[i], t, k)
        else:
            engine.finish(items[i])
    for step in extra:
        step()
    engine.settle()
    for i, item in enumerate(items):
        engine.drain(item, range(readies[i], len(shapes[i])))
    for reduce in tensor:
        reduce.drain()


def task_order(plan, readies, names, n):
    tasks = []
    for last_first, ready in zip(plan, readies):
        sizes = digit_sizes(n)
        if last_first:
            sizes = sizes[1:] + sizes[:1]
        i = len(tasks)
        tasks.append([(i, t, k) for t, m in enumerate(sizes) for k in range(1, m) if t >= ready] + [(i, len(sizes), 0)])
    out, at = [], [0] * len(plan)
    for i in names:
        if i < 0:
            out.append((-1, 0, 0))
        elif at[i] < len(tasks[i]):
            out.append(tasks[i][at[i]])
            at[i] += 1
    for i in range(len(plan)):
        out += tasks[i][at[i] :]
    return out


def finish(part_out, middle, d_middle, stream, w_gate, w_branch, gain, gain_grad_two, lefts, lefts_of, rights, given, plan, out_of, names, keep):
    n = lax.axis_size("dp")
    tokens, features = part_out.shape
    width, rows = features // n, tokens // 4
    readies = [len(g) for g in given]
    pieces = [sum(o == q for o, _ in out_of) for q in range(len(rights))]
    columns = [rights[o].shape[1] // pieces[o] for o, _ in out_of]
    out_of = [(o, q * c) for (o, q), c in zip(out_of, columns)]
    widest = max(columns)
    keep = () if width % LANES else keep
    shapes = [stage_shapes(n, last_first, width, c)[ready:] for last_first, c, ready in zip(plan, columns, readies)]
    steps = 2 + (n - 1).bit_length()
    dma = pltpu.SemaphoreType.DMA
    stream_shape = jax.ShapeDtypeStruct((rows, features), F32)
    out_shape = [stream_shape, stream_shape] + [jax.ShapeDtypeStruct((width, r.shape[1]), F32) for r in rights]
    out_shape += [jax.ShapeDtypeStruct((tokens, features), BF16)]
    out_shape += TensorReduce.results(tokens, features) * 2 + [s[0] for item in shapes for s in item]
    results = pl.pallas_call(
        functools.partial(finish_kernel, n, width, plan, task_order(plan, readies, names, n), lefts_of, keep, readies, columns, out_of),
        out_shape=[*out_shape, jax.ShapeDtypeStruct((8, features), F32)],
        in_specs=[HBM] * 6 + [IN_VMEM] * 2 + [HBM] * (len(lefts) + len(rights) + sum(readies)),
        out_specs=[HBM] * len(out_shape) + [IN_VMEM],
        scratch_shapes=[
            *[pltpu.VMEM(r.shape, BF16) for r in rights],
            pltpu.VMEM(w_gate.shape, BF16), pltpu.VMEM(w_branch.shape, BF16), pltpu.VMEM((rows, features), BF16),
            *[s[1] for item in shapes for s in item],
            *[s[2] for item in shapes for s in item],
            *[s[3] for item in shapes for s in item],
            *[pltpu.VMEM((tokens, features) if i in keep else (8, features), BF16) for i in range(len(lefts))],
            pltpu.VMEM((2, tokens, width), BF16),
            pltpu.VMEM((2 * len(digit_sizes(n)), width, widest), BF16),
            pltpu.VMEM((width, widest), F32), pltpu.VMEM((width, widest), F32),
            pltpu.VMEM((rows, features), BF16), *TensorReduce.buffers(tokens, features),
            pltpu.VMEM((rows, features), BF16),
            pltpu.VMEM((rows, features), BF16),
            pltpu.VMEM((rows, features), F32),
            pltpu.VMEM((steps, 8, features), F32),
            pltpu.VMEM((steps, 8, features), F32),
            *TensorReduce.semaphores(),
            *TensorReduce.semaphores(),
            dma((steps,)), dma((steps,)), dma((len(rights) + 2 + len(lefts),)), dma((2,)), dma((2 + 2 * len(digit_sizes(n)),)), dma,
        ],
        compiler_params=pltpu.CompilerParams(vmem_limit_bytes=VMEM_BYTES, has_side_effects=True),
        cost_estimate=pl.CostEstimate(
            flops=2 * tokens * features * sum(columns), bytes_accessed=4 * features * sum(columns), transcendentals=0
        ),
        name="finish",
    )(
        part_out, middle, d_middle, stream, w_gate, w_branch, gain, gain_grad_two,
        *[column_blocks(v, n) for v in lefts], *rights, *[g for item in given for g in item],
    )
    return results[0], results[1], results[2 : 2 + len(rights)], results[-1]

DP_PLAN = [True, True, False, False, False, False, False, False]
DP_OUTS = [(0, 0), (0, 1), (1, 0), (2, 0), (2, 1), (3, 0), (4, 0), (5, 0)]
DP_ORDER = [2, 5, 3, -1, 7, 2, 4, -1, 5, -1, -1, 3, 2, -1, 7, 6, 5, -1, -1, 3, 5, -1, 4, 2, -1, 1, 7, 5, -1, 4, 6, -1, 0, 7, 1, 6, 4, -1, 3, 0, 6, 7, 4, 6]


def spread_heads(*weights):
    heads, width = weights[0].shape[:2]
    total = len(weights) * heads * width
    rows = []
    for h in range(heads):
        row = 0
        for q, weight in enumerate(weights):
            before = (q * heads + h) * width
            row = row + jnp.pad(weight[h], ((0, 0), (before, total - before - width)))
        rows.append(row)
    return jnp.concatenate(rows)


def on_device(
    stream_in, segments, first_gain, gelu_gate_weight, recurrent_branch_weight, conv_kernel, conv_bias, recur_weight, recur_bias,
    inlet_weight, inlet_bias, decay_param, recurrent_output_weight, second_gain, gate_projection_weight, up_projection_weight,
    down_projection_weight, cotangent,
):
    seq_len = segments.shape[1]
    heads, head_width = recur_weight.shape[:2]
    ids = jnp.pad(segments[0], (3, 8), constant_values=-1)
    same = [(ids[3 - k : 3 - k + seq_len] == segments[0]).astype(F32) for k in range(1, 4)]
    masks = jnp.pad(jnp.stack(same, axis=1), ((0, 8), (0, 5)))
    softplus = jax.nn.softplus(-decay_param)
    vecs = jnp.concatenate([conv_kernel, jnp.stack([conv_bias, recur_bias, inlet_bias, softplus])])
    w_cat = spread_heads(recur_weight, inlet_weight)

    (
        normed, cot, _, _, _, _, product, middle, normed_two, _, _,
        d_middle, d_attended, hidden, d_gate, d_up, d_gated, _, d_branch, part_out, dense, _, _, *gots, sums, gain_two,
    ) = main_part(
        cotangent[0], gelu_gate_weight, recurrent_branch_weight, recurrent_output_weight, gate_projection_weight,
        up_projection_weight, down_projection_weight, stream_in[0], first_gain[None], second_gain[None], masks, vecs, w_cat,
    )
    stream_grad, stream_out, gradients, gains = finish(
        part_out, middle, d_middle, stream_in[0], gelu_gate_weight, recurrent_branch_weight, first_gain[None], gain_two,
        [cot, normed_two, d_attended, normed], [0, 0, 1, 1, 1, 2, 3, 3], [hidden, d_gate, d_up, product, d_gated, d_branch],
        [*([g] for g in gots), [], [], [], []], DP_PLAN, DP_OUTS, DP_ORDER, (1, 3),
    )
    down_gradient, gate_gradient, up_gradient, output_gradient, gated_gradient, branch_gradient = gradients

    width = heads * head_width
    blocks = [dense[h * head_width : (h + 1) * head_width, :] for h in range(heads)]
    rows = [blocks[h][:, q * width + h * head_width :][:, :head_width] for q in range(2) for h in range(heads)]
    sums = jnp.sum(sums, axis=1)
    rows += [sums[:, h * head_width : (h + 1) * head_width] for h in range(heads)]
    small = lax.psum(jnp.concatenate(rows).astype(BF16), "dp").astype(F32)
    grad_recur, grad_inlet = small[: 2 * width].reshape(2, heads, head_width, head_width)
    sums = jnp.concatenate([small[2 * width + 8 * h :][:8] for h in range(heads)], axis=1)
    grad_decay = decay_scale * jax.nn.sigmoid(-decay_param) * sums[7]
    return (
        stream_out[None], stream_grad[None], gains[0], gated_gradient, branch_gradient, sums[:4], sums[4], grad_recur, sums[5],
        grad_inlet, sums[6], grad_decay, output_gradient.T, gains[1], gate_gradient, up_gradient, down_gradient.T,
    )


def solution(mesh):
    in_specs = (
        P("dp", "tensor", None),
        P("dp", None),
        P(),
        P(None, "tensor"),
        P(None, "tensor"),
        P(None, "tensor"),
        P("tensor"),
        P("tensor", None, None),
        P("tensor"),
        P("tensor", None, None),
        P("tensor"),
        P("tensor"),
        P("tensor", None),
        P(),
        P(None, "tensor"),
        P(None, "tensor"),
        P("tensor", None),
        P("dp", "tensor", None),
    )
    out_specs = (
        P("dp", "tensor", None),
        P("dp", "tensor", None),
        P(),
        P("dp", "tensor"),
        P("dp", "tensor"),
        P(None, "tensor"),
        P("tensor"),
        P("tensor", None, None),
        P("tensor"),
        P("tensor", None, None),
        P("tensor"),
        P("tensor"),
        P("tensor", "dp"),
        P(),
        P("dp", "tensor"),
        P("dp", "tensor"),
        P("tensor", "dp"),
    )
    return jax.shard_map(
        on_device, mesh=mesh, in_specs=in_specs, out_specs=out_specs, check_vma=False
    )
```

```python
import functools

import jax
import jax.numpy as jnp
from jax import lax
from jax.experimental import pallas as pl
from jax.experimental.pallas import tpu as pltpu
from jax.sharding import PartitionSpec as P

epsilon = 1e-06
decay_scale = 8.0
LANES = 128
GELU_C = 0.7978845608028654
GELU_K = 0.044715
F32 = jnp.float32
BF16 = jnp.bfloat16
VMEM_BYTES = 60 * 1024 * 1024


def minus_expm1(y, exp_y):
    s = 1.0 + y * (1.0 / 9.0)
    for d in range(8, 1, -1):
        s = 1.0 + (y * (1.0 / d)) * s
    return jnp.where(y > -0.5, -y * s, 1.0 - exp_y)


def gelu_parts(v):
    v2 = v * v
    t = jnp.tanh(GELU_C * v * (1.0 + GELU_K * v2))
    half = 0.5 * (1.0 + t)
    slope = half + 0.5 * v * (1.0 - t * t) * (GELU_C * (1.0 + 3.0 * GELU_K * v2))
    return v * half, slope


def lane_tiles(width):
    return [slice(j * LANES, (j + 1) * LANES) for j in range(width // LANES)]


def fold_rows(v):
    return jnp.sum(v.reshape(v.shape[0] // 8, 8, v.shape[1]), axis=0)


def gates_pre(rows, step, conv_ref, w_ref, pre_s):
    @pl.loop(0, rows // step)
    def _(i):
        r = pl.ds(pl.multiple_of(i * step, step), step)
        pre_s[r, :] = jnp.dot(conv_ref[r, :], w_ref[...], preferred_element_type=F32)


def mixer_forward_kernel(branch_ref, gated_ref, mask_ref, vec_ref, w_ref, conv_ref, states_ref, product_ref, pre_s, a_s, b_s):
    rows, width = branch_ref.shape
    seg = rows // 8
    tiles = lane_tiles(width)

    @pl.loop(0, 8)
    def _(s):
        t0 = pl.multiple_of(s * seg, seg)
        before = pl.multiple_of(jnp.maximum(t0 - 8, 0), 8)
        same = [mask_ref[pl.ds(t0, seg), k : k + 1] for k in range(3)]
        for cols in tiles:
            b = branch_ref[pl.ds(t0, seg), cols]
            ext = jnp.concatenate([branch_ref[pl.ds(before, 8), cols], b], axis=0)
            out = vec_ref[4:5, cols] + vec_ref[0:1, cols] * b
            for k in range(1, 4):
                out = out + vec_ref[k : k + 1, cols] * pltpu.roll(ext, k, 0)[8:] * same[k - 1]
            conv_ref[pl.ds(t0, seg), cols] = out.astype(BF16)

    gates_pre(rows, 256, conv_ref, w_ref, pre_s)

    @pl.loop(0, 8)
    def _(s):
        t0 = pl.multiple_of(s * seg, seg)
        c = mask_ref[pl.ds(t0, seg), 0:1]
        for j, cols in enumerate(tiles):
            cols_i = slice(width + j * LANES, width + (j + 1) * LANES)
            r = jax.nn.sigmoid(pre_s[pl.ds(t0, seg), cols] + vec_ref[5:6, cols])
            i = jax.nn.sigmoid(pre_s[pl.ds(t0, seg), cols_i] + vec_ref[6:7, cols])
            log_a = (-decay_scale * vec_ref[7:8, cols]) * r
            a = jnp.exp(log_a)
            n = jnp.sqrt(minus_expm1(2.0 * log_a, a * a))
            mult = (1.0 - c) + c * n
            a_s[j, pl.ds(t0, seg), :] = a * c
            b_s[j, pl.ds(t0, seg), :] = mult * i * conv_ref[pl.ds(t0, seg), cols].astype(F32)

    row = lax.broadcasted_iota(jnp.int32, (8, LANES), 0)

    def scan_step(i, carry):
        at = pl.ds(pl.multiple_of(i * 8, 8), 8)
        out = []
        for j, cols in enumerate(tiles):
            a, b = a_s[j, at, :], b_s[j, at, :]
            for s in (1, 2, 4):
                b = b + a * jnp.where(row >= s, pltpu.roll(b, s, 0), 0.0)
                a = a * jnp.where(row >= s, pltpu.roll(a, s, 0), 1.0)
            b = b + a * carry[j]
            states_ref[at, cols] = b
            out.append(jnp.broadcast_to(b[7:8, :], (8, LANES)))
        return tuple(out)

    lax.fori_loop(0, rows // 8, scan_step, tuple(jnp.zeros((8, LANES), F32) for _ in tiles), unroll=2)

    @pl.loop(0, 8)
    def _(s):
        at = pl.ds(pl.multiple_of(s * seg, seg), seg)
        for cols in tiles:
            act, _ = gelu_parts(gated_ref[at, cols])
            product_ref[at, cols] = (states_ref[at, cols] * act).astype(BF16)


class MixerBackward:
    def __init__(self, masks, vecs, w_cat, states, branch, conv, dgated, dri, dbranch, sums, pre_s, a_s, n_s, ac_s, e_s):
        self.masks, self.vecs, self.w_cat, self.states, self.branch, self.conv = masks, vecs, w_cat, states, branch, conv
        self.dgated, self.dri, self.dbranch, self.sums = dgated, dri, dbranch, sums
        self.pre_s, self.a_s, self.n_s, self.ac_s, self.e_s = pre_s, a_s, n_s, ac_s, e_s
        self.rows, self.width = states.shape
        self.seg = self.rows // 8
        self.tiles = lane_tiles(self.width)

    @staticmethod
    def scratch(rows, width):
        lanes = width // LANES
        return [
            pltpu.VMEM((rows, 2 * width), F32),
            pltpu.VMEM((rows, width), F32),
            pltpu.VMEM((rows + 8, width), F32),
            pltpu.VMEM((lanes, rows, LANES), F32),
            pltpu.VMEM((lanes, rows, LANES), F32),
        ]

    def gates(self):
        self.sums[...] = jnp.zeros_like(self.sums)
        gates_pre(self.rows, 256, self.conv, self.w_cat, self.pre_s)

    def factors(self, gated):
        @pl.loop(0, 8)
        def _(s):
            t0 = pl.multiple_of(s * self.seg, self.seg)
            at = pl.ds(t0, self.seg)
            c = self.masks[at, 0:1]
            for j, cols in enumerate(self.tiles):
                cols_i = slice(self.width + j * LANES, self.width + (j + 1) * LANES)
                r = jax.nn.sigmoid(self.pre_s[at, cols] + self.vecs[5:6, cols])
                self.pre_s[at, cols] = r
                self.pre_s[at, cols_i] = jax.nn.sigmoid(self.pre_s[at, cols_i] + self.vecs[6:7, cols])
                log_a = (-decay_scale * self.vecs[7:8, cols]) * r
                a = jnp.exp(log_a)
                d = self.a_s[at, cols]
                self.a_s[at, cols] = a
                self.n_s[at, cols] = jnp.sqrt(minus_expm1(2.0 * log_a, a * a))
                self.ac_s[j, at, :] = a * c
                act, slope = gelu_parts(gated[at, cols])
                self.e_s[j, at, :] = d * act
                self.dgated[at, cols] = (d * self.states[at, cols] * slope).astype(BF16)

    def scan(self):
        row = lax.broadcasted_iota(jnp.int32, (8, LANES), 0)

        def step(q, carry):
            at = pl.ds(pl.multiple_of((self.rows // 8 - 1 - q) * 8, 8), 8)
            out = []
            for j in range(len(self.tiles)):
                e, later = carry[j]
                now = self.ac_s[j, at, :]
                a = jnp.where(row == 7, later, pltpu.roll(now, 7, 0))
                b = self.e_s[j, at, :]
                for s in (1, 2, 4):
                    b = b + a * jnp.where(row < 8 - s, pltpu.roll(b, 8 - s, 0), 0.0)
                    a = a * jnp.where(row < 8 - s, pltpu.roll(a, 8 - s, 0), 1.0)
                b = b + a * e
                self.e_s[j, at, :] = b
                out.append((jnp.broadcast_to(b[0:1, :], (8, LANES)), jnp.broadcast_to(now[0:1, :], (8, LANES))))
            return tuple(out)

        none = jnp.zeros((8, LANES), F32)
        lax.fori_loop(0, self.rows // 8, step, tuple((none, none) for _ in self.tiles), unroll=2)

    def gate_gradients(self):
        seg, width = self.seg, self.width

        @pl.loop(0, 8)
        def _(s):
            t0 = pl.multiple_of(s * seg, seg)
            at = pl.ds(t0, seg)
            before = pl.multiple_of(jnp.maximum(t0 - 8, 0), 8)
            c = self.masks[at, 0:1]
            for j, cols in enumerate(self.tiles):
                cols_i = slice(width + j * LANES, width + (j + 1) * LANES)
                e = self.e_s[j, at, :]
                ext = jnp.concatenate([self.states[pl.ds(before, 8), cols], self.states[at, cols]], axis=0)
                earlier = pltpu.roll(ext, 1, 0)[8:]
                r, i, a, n = self.pre_s[at, cols], self.pre_s[at, cols_i], self.a_s[at, cols], self.n_s[at, cols]
                cv = self.conv[at, cols].astype(F32)
                ec = e * c
                d_log = a * (ec * earlier) - ec * i * cv * (a * a / n)
                rr = d_log * r
                dr = ((-decay_scale * self.vecs[7:8, cols]) * rr * (1.0 - r)).astype(BF16)
                em = e * ((1.0 - c) + c * n) * i
                di = (em * cv * (1.0 - i)).astype(BF16)
                self.dri[at, cols] = dr
                self.dri[at, cols_i] = di
                self.n_s[at, cols] = em
                self.sums[5, :, cols] += fold_rows(dr.astype(F32))
                self.sums[6, :, cols] += fold_rows(di.astype(F32))
                self.sums[7, :, cols] += fold_rows(rr)

        @pl.loop(0, self.rows // 256)
        def _(i):
            at = pl.ds(pl.multiple_of(i * 256, 256), 256)
            self.n_s[at, :] += dot_nt(self.dri[at, :], self.w_cat[...])

        self.n_s[self.rows : self.rows + 8, :] = jnp.zeros((8, width), F32)

    def convolution(self):
        @pl.loop(0, 8)
        def _(s):
            t0 = pl.multiple_of(s * self.seg, self.seg)
            at, ext = pl.ds(t0, self.seg), pl.ds(t0, self.seg + 8)
            same = [self.masks[ext, k : k + 1] for k in range(3)]
            for cols in self.tiles:
                d = self.n_s[ext, cols]
                b = self.branch[at, cols]
                self.sums[4, :, cols] += fold_rows(d[: self.seg])
                self.sums[0, :, cols] += fold_rows(d[: self.seg] * b)
                total = self.vecs[0:1, cols] * d[: self.seg]
                for k in range(1, 4):
                    moved = pltpu.roll(d * same[k - 1], self.seg + 8 - k, 0)[: self.seg]
                    total = total + self.vecs[k : k + 1, cols] * moved
                    self.sums[k, :, cols] += fold_rows(moved * b)
                self.dbranch[at, cols] = total.astype(BF16)


def dot_nt(left, right):
    return lax.dot_general(left, right, (((1,), (1,)), ((), ())), preferred_element_type=F32)


class Stage:
    def __init__(self, stride, size, later):
        self.stride, self.size, self.later = stride, size, later
        self.blocks = 1
        for s in later:
            self.blocks *= s.size
        self.digit = lax.rem(lax.axis_index("dp") // stride, size)

    def offset(self, position):
        total = 0
        for s in reversed(self.later):
            total = total + lax.rem(position, s.size) * s.stride
            position = position // s.size
        return total


def digit_sizes(n):
    if n == 8:
        return [2, 4]
    sizes = []
    while n > 1:
        m = 4 if n % 4 == 0 else 2 if n % 2 == 0 else n
        sizes.append(m)
        n //= m
    return sizes


def make_stages(n, last_first):
    digits, stride = [], 1
    for m in digit_sizes(n):
        digits.append((stride, m))
        stride *= m
    if last_first:
        digits = digits[1:] + digits[:1]
    stages = []
    for stride, m in reversed(digits):
        stages.insert(0, Stage(stride, m, list(stages)))
    return stages


class Item:
    def __init__(self, stages, left, right, width, ready, refs, resident=None):
        self.stages, self.left, self.right, self.width, self.ready = stages, left, right, width, ready
        self.resident = resident
        self.columns = right.shape[1]
        self.out, self.recv, self.send, self.send_sem, self.recv_sem = refs

    def message(self, t, back, k, slot, rows=None):
        stage = self.stages[t]
        rows = pl.ds(0, stage.blocks * self.width) if rows is None else rows
        step = jnp.where(back, -stage.stride, stage.stride)
        return pltpu.make_async_remote_copy(
            src_ref=self.send[t].at[slot, rows],
            dst_ref=self.recv[t].at[back, k - 1, rows],
            send_sem=self.send_sem[t].at[slot],
            recv_sem=self.recv_sem[t].at[back, k - 1],
            device_id={"dp": lax.axis_index("dp") + step},
            device_id_type=pl.DeviceIdType.MESH,
        )


class Engine:
    def __init__(self, left_s, got_s, total_s, sem, out_s=None, out_sem=None):
        self.left_s, self.got_s, self.total_s, self.sem = left_s, got_s, total_s, sem
        self.out_s, self.out_sem, self.finished = out_s, out_sem, None

    def fetch(self, item, block, slot):
        if len(item.left.shape) == 3:
            source = item.left.at[block]
        else:
            size = max(item.width, LANES)
            source = item.left.at[:, pl.ds(pl.multiple_of(block // (size // item.width) * size, size), size)]
        return pltpu.make_async_copy(source, self.left_s.at[slot], self.sem.at[slot])

    def columns(self, item, block, slot):
        held = self.left_s[slot]
        if held.shape[1] == item.width:
            return held
        pieces = [held[:, i * item.width : (i + 1) * item.width] for i in range(held.shape[1] // item.width)]
        value = pieces[0]
        for i, piece in enumerate(pieces[1:], 1):
            value = jnp.where(lax.rem(block, len(pieces)) == i, piece, value)
        return value

    def products(self, item, count, block_of, store, done):
        tile = item.columns // 2 if item.columns > 1024 else item.columns

        def compute(p, left):
            if tile == item.columns:
                store(p, pl.ds(0, tile), dot_tn(left(), item.right[...]))
            else:

                @pl.loop(0, item.columns // tile)
                def _(c):
                    cols = pl.ds(pl.multiple_of(c * tile, tile), tile)
                    store(p, cols, dot_tn(left(), item.right[:, cols]))

            done(p)

        if item.resident is not None:

            @pl.loop(0, count)
            def _(p):
                cols = pl.ds(pl.multiple_of(block_of(p) * item.width, item.width), item.width)
                compute(p, lambda: item.resident[:, cols])

            return
        self.fetch(item, block_of(0), 0).start()

        @pl.loop(0, count)
        def _(p):
            slot = lax.rem(p, 2)
            if count > 1:

                @pl.when(p + 1 < count)
                def _():
                    self.fetch(item, block_of(p + 1), 1 - slot).start()

            self.fetch(item, block_of(p), slot).wait()
            compute(p, lambda: self.columns(item, block_of(p), slot))

    def got_copy(self, item, i, source):
        return pltpu.make_async_copy(source, self.got_s.at[i, :, pl.ds(0, item.columns)], self.sem.at[2 + i])

    def start_gots(self, item, first, gots):
        for i, (condition, source) in enumerate(gots):

            @pl.when(condition)
            def _(i=i, source=source):
                self.got_copy(item, first + i, source).start()

    def add_gots(self, item, gots, put):
        for i, (condition, source) in enumerate(gots):

            @pl.when(condition)
            def _(i=i, source=source):
                self.got_copy(item, i, source).wait()

        @pl.loop(0, item.width // 16)
        def _(r):
            at = pl.ds(pl.multiple_of(r * 16, 16), 16)
            total = self.total_s[at, pl.ds(0, item.columns)]
            for i, (condition, _) in enumerate(gots):
                total = total + jnp.where(condition, self.got_s[i, at, pl.ds(0, item.columns)].astype(F32), 0.0)
            put(at, total)

    def arrived(self, item, t, position):
        found, last_found = [], []
        for u in range(t):
            stage = item.stages[u]
            spot = position
            scale = 1
            for s in item.stages[t:]:
                scale *= s.size
            lead = 0
            for s in item.stages[u + 1 : t]:
                lead = lead * s.size + s.digit
            rows = pl.ds((lead * scale + spot) * item.width, item.width)
            last = stage.size - 2
            if stage.size == 2:
                back = jnp.where(stage.digit == 0, 1, 0)
                (last_found if u == t - 1 else found).append((stage.digit >= 0, item.recv[u].at[back, last, rows]))
            else:
                (last_found if u == t - 1 else found).append((stage.digit >= 1, item.recv[u].at[0, last, rows]))
                (last_found if u == t - 1 else found).append((stage.digit <= stage.size - 2, item.recv[u].at[1, last, rows]))
        return found, last_found

    def own_base(self, item, t):
        base = 0
        for s in item.stages[:t]:
            base = base + s.digit * s.stride
        return base

    def wait_last(self, item, t):
        if t < item.ready:
            return
        stage = item.stages[t]
        for back in range(2):
            me = stage.digit if back == 0 else stage.size - 1 - stage.digit

            @pl.when(me >= 1)
            def _(back=back):
                item.message(t, back, stage.size - 1, 0).wait_recv()

    def round(self, item, t, k):
        stage = item.stages[t]
        base = self.own_base(item, t)
        alone = t == 0 and k == 1
        if k == 1 and t > 0:
            self.wait_last(item, t - 1)

        @pl.loop(0, 2)
        def _(back):
            me = jnp.where(back == 0, stage.digit, stage.size - 1 - stage.digit)
            there = me + stage.size - k
            value = jnp.where(back == 0, there, stage.size - 1 - there)
            slot = jnp.where(value > stage.digit, value - 1, value)

            def rows_of(p):
                return pl.ds(pl.multiple_of(p * item.width, item.width), item.width)

            def gots_of(p):
                earlier = sum(self.arrived(item, t, value * stage.blocks + p), [])
                return earlier, [(me >= 1, item.recv[t].at[back, k - 2, rows_of(p)])] if k > 1 else []

            @pl.when(me <= k - 1)
            def _():
                if not alone:
                    self.start_gots(item, 0, gots_of(0)[0])

                def store(p, cols, total):
                    if alone:
                        item.send[t][slot, rows_of(p), cols] = total.astype(BF16)
                    else:
                        self.total_s[:, cols] = total

                def done(p):
                    if not alone:
                        if k > 1:

                            @pl.when((me >= 1) & (p == 0))
                            def _():
                                item.message(t, back, k - 1, 0).wait_recv()

                        def put(at, value):
                            rows = pl.ds(pl.multiple_of(p * item.width + at.start, 16), 16)
                            item.send[t][slot, rows, :] = value.astype(BF16)

                        earlier, own = gots_of(p)
                        self.start_gots(item, len(earlier), own)
                        self.add_gots(item, earlier + own, put)

                        @pl.when(p + 1 < stage.blocks)
                        def _():
                            self.start_gots(item, 0, gots_of(p + 1)[0])

                    item.message(t, back, k, slot, rows_of(p)).start()

                self.products(item, stage.blocks, lambda p: base + value * stage.stride + stage.offset(p), store, done)

    def out_copy(self, item):
        return pltpu.make_async_copy(self.out_s.at[:, pl.ds(0, item.columns)], item.out, self.out_sem)

    def finish(self, item):
        t = len(item.stages)
        self.wait_last(item, t - 1)
        gots = sum(self.arrived(item, t, 0), [])
        self.start_gots(item, 0, gots)

        def store(p, cols, total):
            self.total_s[:, cols] = total

        def put(at, value):
            self.out_s[at, pl.ds(0, item.columns)] = value

        self.settle()
        self.products(item, 1, lambda p: self.own_base(item, t), store, lambda p: self.add_gots(item, gots, put))
        self.out_copy(item).start()
        self.finished = item

    def settle(self):
        if self.finished is not None:
            self.out_copy(self.finished).wait()
        self.finished = None

    def drain(self, item, stages):
        for t in stages:
            for slot in range(item.stages[t].size - 1):
                item.message(t, 0, 1, slot).wait_send()


def stage_shapes(n, last_first, width, columns):
    sizes = digit_sizes(n)
    if last_first:
        sizes = sizes[1:] + sizes[:1]
    left, found = n, []
    for t, m in enumerate(sizes):
        left //= m
        found.append(
            (
                jax.ShapeDtypeStruct((2, m - 1, left * width, columns), BF16),
                pltpu.VMEM((m - 1, left * width, columns), BF16),
                pltpu.SemaphoreType.DMA((m - 1,)),
                pltpu.SemaphoreType.DMA((2, m - 1)),
            )
        )
    return found


def dot_tn(left, right):
    return lax.dot_general(left, right, (((0,), (0,)), ((), ())), preferred_element_type=F32)


class Reader:
    def __init__(self, refs):
        self.refs, self.at = refs, 0

    def __call__(self, count=None):
        start = self.at
        self.at += 1 if count is None else count
        return self.refs[start] if count is None else list(self.refs[start : self.at])


def column_blocks(left, n):
    tokens, features = left.shape
    width = features // n
    return left.reshape(tokens, n, width).transpose(1, 0, 2) if width % LANES else left


class TensorLine:
    def __init__(self):
        self.index = lax.axis_index("tensor")
        self.mate, self.peer, self.cross = self.index ^ 1, self.index ^ 2, self.index ^ 3


def copy_in(source, target, sem):
    copy = pltpu.make_async_copy(source, target, sem)
    copy.start()
    return copy


def remote(source, target, send_sem, recv_sem, axis, index):
    return pltpu.make_async_remote_copy(
        src_ref=source, dst_ref=target, send_sem=send_sem, recv_sem=recv_sem,
        device_id={axis: index}, device_id_type=pl.DeviceIdType.MESH,
    )


class TensorReduce:
    def __init__(self, line, part, from_mate, from_peer, own_v, got_v, send_v, send_sem, recv_sem, sem):
        self.line, self.part, self.from_mate, self.from_peer = line, part, from_mate, from_peer
        self.own_v, self.got_v, self.send_v, self.sem = own_v, got_v, send_v, sem
        self.rows = part.shape[0] // 4
        self.mates = [
            remote(self.block(line.cross), from_mate.at[0], send_sem.at[0], recv_sem.at[0], "tensor", line.mate),
            remote(self.block(line.mate), from_mate.at[1], send_sem.at[1], recv_sem.at[1], "tensor", line.mate),
        ]
        self.over = remote(send_v, from_peer, send_sem.at[2], recv_sem.at[2], "tensor", line.peer)

    def block(self, index):
        return self.part.at[pl.ds(pl.multiple_of(index * self.rows, self.rows), self.rows)]

    def start(self):
        for copy in self.mates:
            copy.start()

    def own_rows(self, index, at):
        if self.own_v is not None:
            return self.own_v[at, :].astype(F32)
        return self.part[pl.ds(pl.multiple_of(index * self.rows + at.start, 16), 16), :].astype(F32)

    def fetch_own(self, index):
        return [] if self.own_v is None else [copy_in(self.block(index), self.own_v, self.sem.at[0])]

    def middle(self):
        copies = self.fetch_own(self.line.peer)
        self.mates[0].wait_recv()
        copies.append(copy_in(self.from_mate.at[0], self.got_v.at[0], self.sem.at[1]))
        for copy in copies:
            copy.wait()

        @pl.loop(0, self.rows // 16)
        def _(r):
            at = pl.ds(pl.multiple_of(r * 16, 16), 16)
            self.send_v[at, :] = (self.own_rows(self.line.peer, at) + self.got_v[0, at, :].astype(F32)).astype(BF16)

        self.over.start()

    def end(self, use):
        copies = self.fetch_own(self.line.index)
        self.mates[1].wait_recv()
        copies.append(copy_in(self.from_mate.at[1], self.got_v.at[0], self.sem.at[1]))
        self.over.wait_recv()
        copies.append(copy_in(self.from_peer, self.got_v.at[1], self.sem.at[2]))
        for copy in copies:
            copy.wait()

        @pl.loop(0, self.rows // 16)
        def _(r):
            at = pl.ds(pl.multiple_of(r * 16, 16), 16)
            use(at, self.own_rows(self.line.index, at) + self.got_v[0, at, :].astype(F32) + self.got_v[1, at, :].astype(F32))

    def drain(self):
        for copy in self.mates:
            copy.wait_send()
        self.over.wait_send()

    @staticmethod
    def results(tokens, features):
        return [jax.ShapeDtypeStruct((2, tokens // 4, features), BF16), jax.ShapeDtypeStruct((tokens // 4, features), BF16)]

    @staticmethod
    def semaphores():
        return [pltpu.SemaphoreType.DMA((3,)), pltpu.SemaphoreType.DMA((3,)), pltpu.SemaphoreType.DMA((3,))]

    @staticmethod
    def buffers(tokens, features):
        rows = tokens // 4
        return [pltpu.VMEM((2, rows, features), BF16), pltpu.VMEM((rows, features), BF16)]


def norm_backward(values, gain, d_normed):
    inverse = lax.rsqrt(jnp.mean(values * values, axis=-1, keepdims=True) + epsilon)
    weighted = gain * d_normed
    inner = jnp.mean(weighted * values, axis=-1, keepdims=True)
    return inverse * weighted - values * (inverse * inverse * inverse * inner), d_normed * values * inverse


HBM = pl.BlockSpec(memory_space=pl.ANY)
IN_VMEM = pl.BlockSpec(memory_space=pltpu.VMEM)


class TensorGather:
    def __init__(self, line, own_v, out, send_sem, recv_sem):
        self.line, self.own_v, self.out, self.rows = line, own_v, out, own_v.shape[0]
        self.over = remote(own_v, self.block(line.index), send_sem.at[0], recv_sem.at[0], "tensor", line.peer)
        self.aside = remote(own_v, self.block(line.index), send_sem.at[1], recv_sem.at[1], "tensor", line.mate)
        self.onward = remote(self.block(line.peer), self.block(line.peer), send_sem.at[2], recv_sem.at[2], "tensor", line.mate)

    def block(self, index):
        return self.out.at[pl.ds(pl.multiple_of(index * self.rows, self.rows), self.rows)]

    def start(self):
        self.over.start()
        self.aside.start()

    def forward(self):
        self.over.wait_recv()
        self.onward.start()

    def drain(self):
        for copy in (self.over, self.aside, self.onward):
            copy.wait_send()

    @staticmethod
    def semaphores():
        return [pltpu.SemaphoreType.DMA((3,)), pltpu.SemaphoreType.DMA((3,))]


def main_kernel(n, width, units, *refs):
    take = Reader(refs)
    cot_own, w_first, w_branch, w_out, w_gate, w_up, w_down = take(7)
    stream, gain_one, gain, masks, vecs, w_cat = take(6)
    normed, cot, gated, branch, conv, states, product, middle, normed_two, from_mate_one, from_peer_one = take(11)
    d_middle, att, hidden_o, dgate_o, dup_o, dgated_o, dri_o, dbranch_o, part_out, dense_o, from_mate, from_peer = take(12)
    down_recv, (gate_recv, up_recv) = take(2), take(2)
    sums, gain_grad = take(2)
    (att_v,) = take(1)
    one_sems, cot_sems, two_sems, one_rs = take(2), take(2), take(2), take(3)
    one_sem, rs_send, rs_recv, rs_sem, ag_send, ag_recv, sem, engine_sem = take(8)
    item_sems = [take(2) for _ in range(4)]
    rows, features = stream.shape
    tokens, channels = conv.shape
    tile = 512
    line = TensorLine()
    twos = TensorGather(line, att_v, normed_two, *two_sems)
    two_v = att_v

    def forward_phase(
        wg_v, wb_v, wo_v, own_v, cot_v, block_v, gated_v, branch_v, conv_v, states_v, product_v,
        pre_s, a_s, b_s, part_v, rs_got, rs_send_v, middle_v,
    ):
        ones = TensorGather(line, own_v, normed, *one_sems)
        cots = TensorGather(line, cot_v, cot, *cot_sems)
        reduce = TensorReduce(line, part_v, from_mate_one, from_peer_one, None, rs_got, rs_send_v, *one_rs)
        loads = [copy_in(w_first, wg_v, one_sem.at[0]), copy_in(w_branch, wb_v, one_sem.at[1]), copy_in(w_out, wo_v, one_sem.at[2])]
        cot_load = copy_in(cot_own, cot_v, one_sem.at[3])

        def chunks(body):
            @pl.loop(0, rows // 16)
            def _(r):
                body(pl.ds(pl.multiple_of(r * 16, 16), 16))

        def norm(values, gains):
            inverse = lax.rsqrt(jnp.mean(values * values, axis=-1, keepdims=True) + epsilon)
            return (values * inverse * gains).astype(BF16)

        def first_norm(at):
            own_v[at, :] = norm(stream[at, :].astype(F32), gain_one[...])

        chunks(first_norm)
        ones.start()
        keep = [copy_in(own_v, ones.block(line.index), one_sem.at[4])]
        cot_load.wait()
        cots.start()
        keep.append(copy_in(cot_v, cots.block(line.index), one_sem.at[5]))

        def project(source, index):
            at = pl.ds(pl.multiple_of(index * rows, rows), rows)
            branch_v[at, :] = jnp.dot(source, wb_v[...], preferred_element_type=F32)
            gated_v[at, :] = jnp.dot(source, wg_v[...], preferred_element_type=F32)

        loads[0].wait()
        loads[1].wait()

        @pl.loop(0, 4)
        def _(b):
            index = line.index ^ b

            @pl.when(b == 0)
            def _():
                copy_in(own_v, block_v, one_sem.at[6]).wait()

            @pl.when(b == 1)
            def _():
                ones.aside.wait_recv()

            @pl.when(b == 2)
            def _():
                ones.forward()

            @pl.when(b == 3)
            def _():
                ones.onward.wait_recv()

            @pl.when(b > 0)
            def _():
                copy_in(ones.block(index), block_v, one_sem.at[6]).wait()

            project(block_v[...], index)

        outs = [copy_in(branch_v, branch, one_sem.at[7]), copy_in(gated_v, gated, one_sem.at[8])]
        mixer_forward_kernel(branch_v, gated_v, masks, vecs, w_cat, conv_v, states_v, product_v, pre_s, a_s, b_s)
        outs += [copy_in(conv_v, conv, one_sem.at[9]), copy_in(states_v, states, one_sem.at[10]), copy_in(product_v, product, one_sem.at[11])]
        loads[2].wait()

        def out_block(index):
            at = pl.ds(pl.multiple_of(index * rows, rows), rows)
            part_v[at, :] = jnp.dot(product_v[at, :], wo_v[...], preferred_element_type=F32).astype(BF16)

        @pl.loop(0, 4)
        def _(q):
            out_block(line.cross ^ q)

            @pl.when(q == 0)
            def _():
                reduce.mates[0].start()

            @pl.when(q == 1)
            def _():
                reduce.middle()

            @pl.when(q == 2)
            def _():
                reduce.mates[1].start()

        cots.forward()

        def second_norm(at, total):
            values = stream[at, :].astype(F32) + total
            middle_v[at, :] = values
            two_v[at, :] = norm(values, gain[...])

        reduce.end(second_norm)
        twos.start()
        keep += [copy_in(two_v, twos.block(line.index), one_sem.at[12]), copy_in(middle_v, middle, one_sem.at[13])]
        cots.aside.wait_recv()
        cots.onward.wait_recv()
        for copy in keep + outs:
            copy.wait()
        for gathered in (ones, cots):
            gathered.drain()
        reduce.drain()

    block = pltpu.VMEM((rows, features), BF16)
    wide = pltpu.VMEM((tokens, channels), F32)
    narrow = pltpu.VMEM((tokens, channels), BF16)
    lanes = pltpu.VMEM((channels // LANES, tokens, LANES), F32)
    pl.run_scoped(
        forward_phase,
        pltpu.VMEM(w_first.shape, BF16), pltpu.VMEM(w_branch.shape, BF16), pltpu.VMEM(w_out.shape, BF16),
        block, block, block,
        wide, wide, narrow, wide, narrow,
        pltpu.VMEM((tokens, 2 * channels), F32), lanes, lanes,
        pltpu.VMEM((tokens, features), BF16), *TensorReduce.buffers(tokens, features),
        pltpu.VMEM((rows, features), F32),
    )

    def backward_phase(hidden, *held):
        down_one, down_two, gate_send, up_send, left_s, got_s, total_s = held
        halves = [(down_one, *item_sems[0]), (down_two, *item_sems[1])]
        (gate_ss, gate_rs), (up_ss, up_rs) = item_sems[2:]
        engine = Engine(left_s, got_s, total_s, engine_sem)
        downs = [
            Item(
                make_stages(n, True), cot, hidden.at[:, pl.ds(q * (units // 2), units // 2)], width, 0,
                (None, [down_recv[q]], [send], [send_sem], [recv_sem]),
            )
            for q, (send, send_sem, recv_sem) in enumerate(halves)
        ]
        gather = TensorGather(line, att_v, att, ag_send, ag_recv)

        def rounds(item):
            return list(range(1, item.stages[0].size))

        def row_block(ref, index):
            return ref.at[pl.ds(pl.multiple_of(index * rows, rows), rows)]

        first, between, last = rounds(downs[0])[:1], rounds(downs[0])[1:-1], rounds(downs[0])[1:][-1:]
        gate = Item(make_stages(n, False), normed_two, hidden, width, 0, (None, [gate_recv], [gate_send], [gate_ss], [gate_rs]))
        half = hidden.at[:, pl.ds(0, units // 2)]
        up = Item(make_stages(n, False), normed_two, half, width, 0, (None, [up_recv], [up_send], [up_ss], [up_rs]))

        def take_rounds(item, numbers):
            for k in numbers:
                engine.round(item, 0, k)

        def tensor_phase(wg_v, wu_v, wd_v, dgate, dup, x_v, c_v, part, got_v, send_v, dmid_v, cot_v):
            gate.right, up.right = dgate, dup.at[:, pl.ds(0, units // 2)]
            weights = [copy_in(w_gate, wg_v, sem.at[0]), copy_in(w_up, wu_v, sem.at[1]), copy_in(w_down, wd_v, sem.at[2])]
            loads = [copy_in(middle, dmid_v, sem.at[3]), copy_in(row_block(cot, line.index), cot_v, sem.at[4])]
            copy_in(row_block(normed_two, line.index), x_v, sem.at[5])
            copy_in(row_block(cot, line.index), c_v, sem.at[6])
            for load in weights:
                load.wait()

            @pl.loop(0, 4)
            def _(b):
                index = line.index ^ b
                at = pl.ds(pl.multiple_of(index * rows, rows), rows)
                pltpu.make_async_copy(row_block(normed_two, index), x_v, sem.at[5]).wait()
                pltpu.make_async_copy(row_block(cot, index), c_v, sem.at[6]).wait()

                @pl.loop(0, units // tile)
                def _(j):
                    cols = pl.ds(pl.multiple_of(j * tile, tile), tile)
                    gate_pre = jnp.dot(x_v[...], wg_v[:, cols], preferred_element_type=F32)
                    up_pre = jnp.dot(x_v[...], wu_v[:, cols], preferred_element_type=F32)
                    d_hidden = dot_nt(c_v[...], wd_v[cols, :])
                    act, slope = gelu_parts(gate_pre)
                    hidden[at, cols] = (act * up_pre).astype(BF16)
                    dgate[at, cols] = (d_hidden * up_pre * slope).astype(BF16)
                    dup[at, cols] = (d_hidden * act).astype(BF16)

                @pl.when(b == 0)
                def _():
                    twos.aside.wait_recv()

                @pl.when(b == 1)
                def _():
                    twos.forward()

                @pl.when(b == 2)
                def _():
                    twos.onward.wait_recv()

                @pl.when(b < 3)
                def _():
                    following = line.index ^ (b + 1)
                    copy_in(row_block(normed_two, following), x_v, sem.at[5])
                    copy_in(row_block(cot, following), c_v, sem.at[6])

            twos.drain()
            outs = [copy_in(hidden, hidden_o, sem.at[0]), copy_in(dgate, dgate_o, sem.at[1]), copy_in(dup, dup_o, sem.at[2])]
            take_rounds(downs[0], first)
            take_rounds(gate, rounds(gate))
            take_rounds(downs[1], first)

            def stage(index, value):
                @pl.loop(0, features // tile)
                def _(j):
                    at, cols = pl.ds(pl.multiple_of(index * rows, rows), rows), pl.ds(pl.multiple_of(j * tile, tile), tile)
                    part[at, cols] = value(at, cols).astype(BF16)

            def two(at, cols):
                return dot_nt(dgate[at, :], wg_v[cols, :]) + dot_nt(dup[at, :], wu_v[cols, :])

            def out(at, cols):
                return jnp.dot(hidden[at, :], wd_v[:, cols], preferred_element_type=F32)

            reduce = TensorReduce(line, part, from_mate, from_peer, None, got_v, send_v, rs_send, rs_recv, rs_sem)
            @pl.loop(0, 4)
            def _(q):
                stage(line.cross ^ q, two)

                @pl.when(q == 0)
                def _():
                    reduce.mates[0].start()

                @pl.when(q == 1)
                def _():
                    reduce.middle()

                @pl.when(q == 2)
                def _():
                    reduce.mates[1].start()

            for item in downs:
                take_rounds(item, between)
            for load in loads:
                load.wait()
            gain_grad[...] = jnp.zeros_like(gain_grad)

            def use(at, total):
                back, terms = norm_backward(dmid_v[at, :], gain[...], total)
                value = cot_v[at, :].astype(F32) + back
                dmid_v[at, :] = value
                att_v[at, :] = value.astype(BF16)
                gain_grad[...] += fold_rows(terms)

            reduce.end(use)
            gather.start()
            keep = [copy_in(att_v, gather.block(line.index), sem.at[3]), copy_in(dmid_v, d_middle, sem.at[4])]
            take_rounds(up, rounds(up))
            reduce.drain()

            @pl.loop(0, 4)
            def _(b):
                stage(b, out)
                copy_in(row_block(part, b), row_block(part_out, b), sem.at[7])

            take_rounds(downs[0], last)
            gather.forward()
            for copy in outs + keep:
                copy.wait()
            pltpu.make_async_copy(part, part_out, sem.at[7]).wait()

        weight = pltpu.VMEM((features, units), BF16)
        block = pltpu.VMEM((rows, features), BF16)
        pl.run_scoped(
            tensor_phase,
            weight, weight, pltpu.VMEM((units, features), BF16),
            pltpu.VMEM((tokens, units), BF16), pltpu.VMEM((tokens, units), BF16),
            block, block, pltpu.VMEM((tokens, features), BF16),
            *TensorReduce.buffers(tokens, features),
            pltpu.VMEM((rows, features), F32), block,
        )

        def mixer_phase(gated_v, states_v, conv_v, dgated_v, dri_v, dbranch_v, block_v, w_v, dense_v, *scratch):
            loads = [copy_in(conv, conv_v, sem.at[1]), copy_in(w_out, w_v, sem.at[0])]
            loads += [copy_in(gated, gated_v, sem.at[2]), copy_in(states, states_v, sem.at[3])]
            mixer = MixerBackward(masks, vecs, w_cat, states_v, gated_v, conv_v, dgated_v, dri_v, dbranch_v, sums, *scratch)
            loads[0].wait()
            mixer.gates()
            take_rounds(downs[1], last)
            loads[1].wait()

            def product_gradient(index, source):
                mixer.a_s[pl.ds(pl.multiple_of(index * rows, rows), rows), :] = dot_nt(source[...], w_v[...])

            def block_copy(b):
                slot = lax.rem(b, 2)
                return pltpu.make_async_copy(row_block(att, line.index ^ b), block_v.at[slot], sem.at[4 + slot])

            block_copy(0).start()

            @pl.loop(0, 4)
            def _(b):
                @pl.when(b == 0)
                def _():
                    gather.aside.wait_recv()

                @pl.when(b == 2)
                def _():
                    gather.onward.wait_recv()

                @pl.when(b < 3)
                def _():
                    block_copy(b + 1).start()

                block_copy(b).wait()
                product_gradient(line.index ^ b, block_v.at[lax.rem(b, 2)])

            loads[2].wait()
            loads[3].wait()
            mixer.factors(gated_v)
            again = copy_in(branch, gated_v, sem.at[2])
            outs = [copy_in(dgated_v, dgated_o, sem.at[1])]
            mixer.scan()
            mixer.gate_gradients()
            outs.append(copy_in(dri_v, dri_o, sem.at[3]))
            again.wait()
            mixer.convolution()
            outs.append(copy_in(dbranch_v, dbranch_o, sem.at[0]))

            @pl.loop(0, 2 * channels // 256)
            def _(j):
                cols = pl.ds(pl.multiple_of(j * 256, 256), 256)
                dense_v[:, cols] = dot_tn(conv_v[...], dri_v[:, cols])

            outs.append(copy_in(dense_v, dense_o, sem.at[4]))
            for copy in outs:
                copy.wait()

        pl.run_scoped(
            mixer_phase,
            pltpu.VMEM((tokens, channels), F32),
            pltpu.VMEM((tokens, channels), F32),
            pltpu.VMEM((tokens, channels), BF16),
            pltpu.VMEM((tokens, channels), BF16),
            pltpu.VMEM((tokens, 2 * channels), BF16),
            pltpu.VMEM((tokens, channels), BF16),
            pltpu.VMEM((2, rows, features), BF16),
            pltpu.VMEM((channels, features), BF16),
            pltpu.VMEM((channels, 2 * channels), F32),
            *MixerBackward.scratch(tokens, channels),
        )
        gather.drain()
        for item in (*downs, gate, up):
            engine.drain(item, [0])
            engine.wait_last(item, 0)

    down = stage_shapes(n, True, width, units // 2)[0][1]
    gate = stage_shapes(n, False, width, units)[0][1]
    up = stage_shapes(n, False, width, units // 2)[0][1]
    pl.run_scoped(
        backward_phase,
        pltpu.VMEM((tokens, units), BF16), down, down, gate, up,
        pltpu.VMEM((2, tokens, max(width, LANES)), BF16),
        pltpu.VMEM((2, width, units), BF16),
        pltpu.VMEM((width, units), F32),
    )


def main_part(cot_own, w_first, w_branch, w_out, w_gate, w_up, w_down, stream, gain_one, gain_two, masks, vecs, w_cat):
    n = lax.axis_size("dp")
    rows, features = stream.shape
    tokens, channels, units, width = 4 * rows, w_first.shape[1], w_gate.shape[1], features // n
    down = stage_shapes(n, True, width, units // 2)[0]
    gate = stage_shapes(n, False, width, units)[0]
    up = stage_shapes(n, False, width, units // 2)[0]
    dma = pltpu.SemaphoreType.DMA
    whole = jax.ShapeDtypeStruct((tokens, features), BF16)
    part = jax.ShapeDtypeStruct((rows, features), F32)
    hide = jax.ShapeDtypeStruct((tokens, units), BF16)
    wide = jax.ShapeDtypeStruct((tokens, channels), F32)
    narrow = jax.ShapeDtypeStruct((tokens, channels), BF16)
    sums = TensorReduce.results(tokens, features)
    results = [whole, whole, wide, wide, narrow, wide, narrow, part, whole, *sums]
    results += [part, whole, hide, hide, hide, narrow, jax.ShapeDtypeStruct((tokens, 2 * channels), BF16), narrow, whole]
    results += [jax.ShapeDtypeStruct((channels, 2 * channels), F32), *sums]
    results += [down[0], down[0], gate[0], up[0]]
    gathers = TensorGather.semaphores()
    return pl.pallas_call(
        functools.partial(main_kernel, n, width, units),
        out_shape=[*results, jax.ShapeDtypeStruct((8, 8, channels), F32), jax.ShapeDtypeStruct((8, features), F32)],
        in_specs=[HBM] * 7 + [IN_VMEM] * 6,
        out_specs=[HBM] * len(results) + [IN_VMEM] * 2,
        scratch_shapes=[
            pltpu.VMEM((rows, features), BF16),
            *gathers, *gathers, *gathers, *TensorReduce.semaphores(), dma((14,)),
            *TensorReduce.semaphores(), *gathers, dma((8,)), dma((4,)),
            *down[2:4], *down[2:4], *gate[2:4], *up[2:4],
        ],
        compiler_params=pltpu.CompilerParams(vmem_limit_bytes=VMEM_BYTES, has_side_effects=True),
        cost_estimate=pl.CostEstimate(flops=60 * 10**9, bytes_accessed=120 * 10**6, transcendentals=14 * tokens * channels),
        name="main_part",
    )(cot_own, w_first, w_branch, w_out, w_gate, w_up, w_down, stream, gain_one, gain_two, masks, vecs, w_cat)


def gather_sums(gains, sends, recvs, send_sems, recv_sems):
    n, line = lax.axis_size("dp"), TensorLine()
    hops = [("tensor", line.mate), ("tensor", line.peer)]
    bit = 1
    while bit < n:
        hops.append(("dp", lax.axis_index("dp") ^ bit))
        bit *= 2
    copies = [remote(sends.at[s], recvs.at[s], send_sems.at[s], recv_sems.at[s], *hop) for s, hop in enumerate(hops)]

    def begin(s):
        sends[s] = gains[...] if s == 0 else sends[s - 1] + recvs[s - 1]
        copies[s].start()

    def step(s):
        if s > 0:
            copies[s - 1].wait_recv()
        if s < len(copies):
            begin(s)
        else:
            gains[...] = sends[s - 1] + recvs[s - 1]
            for copy in copies:
                copy.wait_send()

    return [functools.partial(step, s) for s in range(len(copies) + 1)]


def finish_kernel(n, width, plan, order, lefts_of, keep, readies, columns, out_of, *refs):
    take = Reader(refs)
    count, n_outs = len(plan), max(o for o, _ in out_of) + 1
    part_out, middle, d_middle, stream, w_gate, w_branch = take(6)
    gain, gain_grad_two = take(2)
    lefts, rights_hbm = take(max(lefts_of) + 1), take(n_outs)
    shapes = [stage_shapes(n, plan[i], width, columns[i]) for i in range(count)]
    given = [take(readies[i]) for i in range(count)]
    stream_grad_o, stream_out_o = take(2)
    outs = take(n_outs)
    (part,) = take(1)
    reduces = [take(2), take(2)]
    recv = [given[i] + take(len(shapes[i]) - readies[i]) for i in range(count)]
    (gains,) = take(1)
    rights = take(n_outs)
    wg_v, wb_v, stage_v = take(3)
    nones = [[None] * r for r in readies]
    sends = [nones[i] + take(len(shapes[i]) - readies[i]) for i in range(count)]
    send_sems = [nones[i] + take(len(shapes[i]) - readies[i]) for i in range(count)]
    recv_sems = [nones[i] + take(len(shapes[i]) - readies[i]) for i in range(count)]
    left_vs = take(max(lefts_of) + 1)
    left_s, got_s, total_s, out_s, own_v, got_v, send_v, send_w = take(8)
    value_v, base_v, gain_sends, gain_recvs = take(4)
    rs_sems = [take(3), take(3)]
    gain_ss, gain_rs, right_sem, sem, engine_sem, out_sem = take(6)

    line = TensorLine()
    engine = Engine(left_s, got_s, total_s, engine_sem, out_s, out_sem)
    tensor = [
        TensorReduce(line, source, *reduces[q], own_v, got_v, (send_v, send_w)[q], *rs_sems[q])
        for q, source in enumerate((part, part_out))
    ]
    tensor[1].start()
    loads, weights, left_loads = {}, [], {}

    def issue(kind, i):
        if kind == "left" and i in keep and i not in left_loads:
            left_loads[i] = copy_in(lefts[i], left_vs[i], right_sem.at[n_outs + 2 + i])
        if kind == "right" and i not in loads:
            loads[i] = copy_in(rights_hbm[i], rights[i], right_sem.at[i])

    def issue_for(i):
        if i >= 0:
            issue("right", out_of[i][0])
            issue("left", lefts_of[i])
        elif not weights:
            issue("right", n_outs - 2)
            issue("right", n_outs - 1)
            weights.extend([copy_in(w_gate, wg_v, right_sem.at[n_outs]), copy_in(w_branch, wb_v, right_sem.at[n_outs + 1])])

    loaded = set()

    def load_left(i):
        if left_loads.get(i) is not None:
            left_loads[i].wait()
            left_loads[i] = None

    def load(i):
        if i not in loaded:
            loads[i].wait()
            loaded.add(i)

    def columns_of(i):
        return pl.ds(out_of[i][1], columns[i])

    items = [
        Item(
            make_stages(n, plan[i]), lefts[lefts_of[i]], rights[out_of[i][0]].at[:, columns_of(i)], width, readies[i],
            (outs[out_of[i][0]].at[:, columns_of(i)], recv[i], sends[i], send_sems[i], recv_sems[i]),
            left_vs[lefts_of[i]] if lefts_of[i] in keep else None,
        )
        for i in range(count)
    ]

    rows, features = stream.shape

    def stage(index):
        at = pl.ds(pl.multiple_of(index * rows, rows), rows)

        @pl.loop(0, features // 512)
        def _(j):
            cols = pl.ds(pl.multiple_of(j * 512, 512), 512)
            total = dot_nt(rights[n_outs - 2][at, :], wg_v[cols, :]) + dot_nt(rights[n_outs - 1][at, :], wb_v[cols, :])
            stage_v[:, cols] = total.astype(BF16)

        copy_in(stage_v, tensor[0].block(index), sem.at[0]).wait()

    def stage_pair(first, mate):
        @pl.loop(0, 2)
        def _(q):
            stage(first ^ q)

            @pl.when(q == 0)
            def _():
                tensor[0].mates[mate].start()

    def part_first():
        for i in (n_outs - 2, n_outs - 1):
            load(i)
        for copy in weights:
            copy.wait()
        stage_pair(line.cross, 0)

    def part_second():
        stage_pair(line.mate, 1)

    def grad_end():
        copies = [copy_in(stream, value_v, sem.at[0]), copy_in(d_middle, base_v, sem.at[1])]
        for copy in copies:
            copy.wait()
        gains[...] = jnp.zeros_like(gains)

        def use(at, total):
            back, terms = norm_backward(value_v[at, :].astype(F32), gain[...], total)
            base_v[at, :] = base_v[at, :] + back
            gains[...] += fold_rows(terms)

        tensor[0].end(use)
        copy_in(base_v, stream_grad_o, sem.at[0]).wait()
        first = jnp.sum(gains[...], axis=0, keepdims=True)
        second = jnp.sum(gain_grad_two[...], axis=0, keepdims=True)
        pick = lax.broadcasted_iota(jnp.int32, gains.shape, 0)
        gains[...] = jnp.where(pick == 0, first, jnp.where(pick == 1, second, 0.0))

    def out_end():
        copy_in(middle, base_v, sem.at[0]).wait()

        def use(at, total):
            base_v[at, :] = base_v[at, :] + total

        tensor[1].end(use)
        copy_in(base_v, stream_out_o, sem.at[0]).wait()

    extra = [part_first, tensor[0].middle, part_second, tensor[1].middle, grad_end, out_end]
    extra += gather_sums(gains, gain_sends, gain_recvs, gain_ss, gain_rs)
    for at, (i, t, k) in enumerate(order):
        for ahead in order[at : at + 3]:
            issue_for(ahead[0])
        if i < 0:
            if extra:
                extra.pop(0)()
            continue
        load(out_of[i][0])
        load_left(lefts_of[i])
        if t < len(shapes[i]):
            engine.round(items[i], t, k)
        else:
            engine.finish(items[i])
    for step in extra:
        step()
    engine.settle()
    for i, item in enumerate(items):
        engine.drain(item, range(readies[i], len(shapes[i])))
    for reduce in tensor:
        reduce.drain()


def task_order(plan, readies, names, n):
    tasks = []
    for last_first, ready in zip(plan, readies):
        sizes = digit_sizes(n)
        if last_first:
            sizes = sizes[1:] + sizes[:1]
        i = len(tasks)
        tasks.append([(i, t, k) for t, m in enumerate(sizes) for k in range(1, m) if t >= ready] + [(i, len(sizes), 0)])
    out, at = [], [0] * len(plan)
    for i in names:
        if i < 0:
            out.append((-1, 0, 0))
        elif at[i] < len(tasks[i]):
            out.append(tasks[i][at[i]])
            at[i] += 1
    for i in range(len(plan)):
        out += tasks[i][at[i] :]
    return out


def finish(part_out, middle, d_middle, stream, w_gate, w_branch, gain, gain_grad_two, lefts, lefts_of, rights, given, plan, out_of, names, keep):
    n = lax.axis_size("dp")
    tokens, features = part_out.shape
    width, rows = features // n, tokens // 4
    readies = [len(g) for g in given]
    pieces = [sum(o == q for o, _ in out_of) for q in range(len(rights))]
    columns = [rights[o].shape[1] // pieces[o] for o, _ in out_of]
    out_of = [(o, q * c) for (o, q), c in zip(out_of, columns)]
    widest = max(columns)
    keep = () if width % LANES else keep
    shapes = [stage_shapes(n, last_first, width, c)[ready:] for last_first, c, ready in zip(plan, columns, readies)]
    steps = 2 + (n - 1).bit_length()
    dma = pltpu.SemaphoreType.DMA
    stream_shape = jax.ShapeDtypeStruct((rows, features), F32)
    out_shape = [stream_shape, stream_shape] + [jax.ShapeDtypeStruct((width, r.shape[1]), F32) for r in rights]
    out_shape += [jax.ShapeDtypeStruct((tokens, features), BF16)]
    out_shape += TensorReduce.results(tokens, features) * 2 + [s[0] for item in shapes for s in item]
    results = pl.pallas_call(
        functools.partial(finish_kernel, n, width, plan, task_order(plan, readies, names, n), lefts_of, keep, readies, columns, out_of),
        out_shape=[*out_shape, jax.ShapeDtypeStruct((8, features), F32)],
        in_specs=[HBM] * 6 + [IN_VMEM] * 2 + [HBM] * (len(lefts) + len(rights) + sum(readies)),
        out_specs=[HBM] * len(out_shape) + [IN_VMEM],
        scratch_shapes=[
            *[pltpu.VMEM(r.shape, BF16) for r in rights],
            pltpu.VMEM(w_gate.shape, BF16), pltpu.VMEM(w_branch.shape, BF16), pltpu.VMEM((rows, features), BF16),
            *[s[1] for item in shapes for s in item],
            *[s[2] for item in shapes for s in item],
            *[s[3] for item in shapes for s in item],
            *[pltpu.VMEM((tokens, features) if i in keep else (8, features), BF16) for i in range(len(lefts))],
            pltpu.VMEM((2, tokens, width), BF16),
            pltpu.VMEM((2 * len(digit_sizes(n)), width, widest), BF16),
            pltpu.VMEM((width, widest), F32), pltpu.VMEM((width, widest), F32),
            pltpu.VMEM((rows, features), BF16), *TensorReduce.buffers(tokens, features),
            pltpu.VMEM((rows, features), BF16),
            pltpu.VMEM((rows, features), BF16),
            pltpu.VMEM((rows, features), F32),
            pltpu.VMEM((steps, 8, features), F32),
            pltpu.VMEM((steps, 8, features), F32),
            *TensorReduce.semaphores(),
            *TensorReduce.semaphores(),
            dma((steps,)), dma((steps,)), dma((len(rights) + 2 + len(lefts),)), dma((2,)), dma((2 + 2 * len(digit_sizes(n)),)), dma,
        ],
        compiler_params=pltpu.CompilerParams(vmem_limit_bytes=VMEM_BYTES, has_side_effects=True),
        cost_estimate=pl.CostEstimate(
            flops=2 * tokens * features * sum(columns), bytes_accessed=4 * features * sum(columns), transcendentals=0
        ),
        name="finish",
    )(
        part_out, middle, d_middle, stream, w_gate, w_branch, gain, gain_grad_two,
        *[column_blocks(v, n) for v in lefts], *rights, *[g for item in given for g in item],
    )
    return results[0], results[1], results[2 : 2 + len(rights)], results[-1]

DP_PLAN = [True, True, False, False, False, False, False, False]
DP_OUTS = [(0, 0), (0, 1), (1, 0), (2, 0), (2, 1), (3, 0), (4, 0), (5, 0)]
DP_ORDER = [2, 5, 3, -1, 7, 2, 4, -1, 5, -1, -1, 3, 2, -1, 7, 6, 5, -1, -1, 3, 5, -1, 4, 2, -1, 1, 7, 5, -1, 4, 6, -1, 0, 7, 1, 6, 4, -1, 3, 0, 6, 7, 4, 6]


def spread_heads(*weights):
    heads, width = weights[0].shape[:2]
    total = len(weights) * heads * width
    rows = []
    for h in range(heads):
        row = 0
        for q, weight in enumerate(weights):
            before = (q * heads + h) * width
            row = row + jnp.pad(weight[h], ((0, 0), (before, total - before - width)))
        rows.append(row)
    return jnp.concatenate(rows)


def on_device(
    stream_in, segments, first_gain, gelu_gate_weight, recurrent_branch_weight, conv_kernel, conv_bias, recur_weight, recur_bias,
    inlet_weight, inlet_bias, decay_param, recurrent_output_weight, second_gain, gate_projection_weight, up_projection_weight,
    down_projection_weight, cotangent,
):
    seq_len = segments.shape[1]
    heads, head_width = recur_weight.shape[:2]
    ids = jnp.pad(segments[0], (3, 8), constant_values=-1)
    same = [(ids[3 - k : 3 - k + seq_len] == segments[0]).astype(F32) for k in range(1, 4)]
    masks = jnp.pad(jnp.stack(same, axis=1), ((0, 8), (0, 5)))
    softplus = jax.nn.softplus(-decay_param)
    vecs = jnp.pad(conv_kernel, ((0, 4), (0, 0)))
    row = lax.broadcasted_iota(jnp.int32, vecs.shape, 0)
    for r, vec in enumerate((conv_bias, recur_bias, inlet_bias, softplus), conv_kernel.shape[0]):
        vecs = jnp.where(row == r, vec[None], vecs)
    w_cat = spread_heads(recur_weight, inlet_weight)

    (
        normed, cot, _, _, _, _, product, middle, normed_two, _, _,
        d_middle, d_attended, hidden, d_gate, d_up, d_gated, _, d_branch, part_out, dense, _, _, *gots, sums, gain_two,
    ) = main_part(
        cotangent[0], gelu_gate_weight, recurrent_branch_weight, recurrent_output_weight, gate_projection_weight,
        up_projection_weight, down_projection_weight, stream_in[0], first_gain[None], second_gain[None], masks, vecs, w_cat,
    )
    stream_grad, stream_out, gradients, gains = finish(
        part_out, middle, d_middle, stream_in[0], gelu_gate_weight, recurrent_branch_weight, first_gain[None], gain_two,
        [cot, normed_two, d_attended, normed], [0, 0, 1, 1, 1, 2, 3, 3], [hidden, d_gate, d_up, product, d_gated, d_branch],
        [*([g] for g in gots), [], [], [], []], DP_PLAN, DP_OUTS, DP_ORDER, (1, 3),
    )
    down_gradient, gate_gradient, up_gradient, output_gradient, gated_gradient, branch_gradient = gradients

    width = heads * head_width
    blocks = [dense[h * head_width : (h + 1) * head_width, :] for h in range(heads)]
    rows = [blocks[h][:, q * width + h * head_width :][:, :head_width] for q in range(2) for h in range(heads)]
    sums = jnp.sum(sums, axis=1)
    rows += [sums[:, h * head_width : (h + 1) * head_width] for h in range(heads)]
    small = lax.psum(jnp.concatenate(rows).astype(BF16), "dp").astype(F32)
    grad_recur, grad_inlet = small[: 2 * width].reshape(2, heads, head_width, head_width)
    sums = jnp.concatenate([small[2 * width + 8 * h :][:8] for h in range(heads)], axis=1)
    grad_decay = decay_scale * jax.nn.sigmoid(-decay_param) * sums[7]
    return (
        stream_out[None], stream_grad[None], gains[0], gated_gradient, branch_gradient, sums[:4], sums[4], grad_recur, sums[5],
        grad_inlet, sums[6], grad_decay, output_gradient.T, gains[1], gate_gradient, up_gradient, down_gradient.T,
    )


def solution(mesh):
    in_specs = (
        P("dp", "tensor", None),
        P("dp", None),
        P(),
        P(None, "tensor"),
        P(None, "tensor"),
        P(None, "tensor"),
        P("tensor"),
        P("tensor", None, None),
        P("tensor"),
        P("tensor", None, None),
        P("tensor"),
        P("tensor"),
        P("tensor", None),
        P(),
        P(None, "tensor"),
        P(None, "tensor"),
        P("tensor", None),
        P("dp", "tensor", None),
    )
    out_specs = (
        P("dp", "tensor", None),
        P("dp", "tensor", None),
        P(),
        P("dp", "tensor"),
        P("dp", "tensor"),
        P(None, "tensor"),
        P("tensor"),
        P("tensor", None, None),
        P("tensor"),
        P("tensor", None, None),
        P("tensor"),
        P("tensor"),
        P("tensor", "dp"),
        P(),
        P("dp", "tensor"),
        P("dp", "tensor"),
        P("tensor", "dp"),
    )
    return jax.shard_map(
        on_device, mesh=mesh, in_specs=in_specs, out_specs=out_specs, check_vma=False
    )
```
